32 devices in a mesh: row: 16 (over z, y, core), col: 2 (over x).
Axes of the slice: x: 2, y: 2, z: 4, core: 2. Of those that a mesh axis runs over, the one named last changes fastest.
Arguments:
- tokens: bfloat16 [18464, 1024], P('row', 'col'), may hold values from -6 to 6
- first_gain: float32 [1024], P(('row', 'col')), may hold values from 0.5 to 1.5
- first_shift: float32 [1024], P(('row', 'col')), may hold values from -1.75 to 1.75
- mixer_weight: float32 [1024, 3, 1024], P('row', None, 'col'), may hold values from -0.1875 to 0.1875
- mixer_bias: float32 [2, 1024], P(None, ('row', 'col')), may hold values from -1.75 to 1.75
- merge_weight: float32 [1024, 1024], P('col', 'row'), may hold values from -2 to 2
- merge_bias: float32 [1024], P(('row', 'col')), may hold values from -1.75 to 1.75
- second_gain: float32 [1024], P(('row', 'col')), may hold values from 0.5 to 1.5
- second_shift: float32 [1024], P(('row', 'col')), may hold values from -1.75 to 1.75
- expand_weight: float32 [1024, 4096], P('row', 'col'), may hold values from -0.1875 to 0.1875
- expand_bias: float32 [4096], P(('row', 'col')), may hold values from -1.75 to 1.75
- reduce_weight: float32 [4096, 1024], P('col', 'row'), may hold values from -0.09375 to 0.09375
- reduce_bias: float32 [1024], P(('row', 'col')), may hold values from -1.75 to 1.75
- cotangent: bfloat16 [18464, 1024], P('row', 'col'), may hold values from -6 to 6
Outputs:
- layer_output: bfloat16 [18464, 1024], P('row', 'col')
- tokens_gradient: float32 [18464, 1024], P('row', 'col')
- first_gain_gradient: float32 [1024], P(('row', 'col'))
- first_shift_gradient: float32 [1024], P(('row', 'col'))
- mixer_weight_gradient: float32 [1024, 3, 1024], P('row', None, 'col')
- mixer_bias_gradient: float32 [2, 1024], P(None, ('row', 'col'))
- merge_weight_gradient: float32 [1024, 1024], P('col', 'row')
- merge_bias_gradient: float32 [1024], P(('row', 'col'))
- second_gain_gradient: float32 [1024], P(('row', 'col'))
- second_shift_gradient: float32 [1024], P(('row', 'col'))
- expand_weight_gradient: float32 [1024, 4096], P('row', 'col')
- expand_bias_gradient: float32 [4096], P(('row', 'col'))
- reduce_weight_gradient: float32 [4096, 1024], P('col', 'row')
- reduce_bias_gradient: float32 [1024], P(('row', 'col'))
The draws below stay inside these ranges and needn't reach their ends.
All inputs are finite; a program needn't handle non-finite values.
Results may differ from the reference program's by a relative error of at most 0.02.
Values may be sent and summed in bfloat16 or wider, within the bound.
A program may use at most 128 MiB of HBM per device.

```python
import jax
import jax.numpy as jnp
from jax import lax

D = 1024
HEADS = 16
HEAD_DIM = 64
FF = 4096
SEQ = 577
IMG = 2
TOKENS = 18464


def block_scale(rng, shape, split, smallest, high):
    def one(axis_at, blocks):
        steps = jax.random.uniform(jax.random.fold_in(jax.random.fold_in(rng, 6), axis_at), (blocks,), jnp.float32, smallest / len(split), high / len(split))
        return jnp.repeat(jnp.exp(steps), shape[axis_at] // blocks).reshape((-1,) + (1,) * (len(shape) - axis_at - 1))

    gain = one(*split[0])
    for cut in split[1:]:
        gain = gain * one(*cut)
    return gain


def bell_draw(rng, shape, deviation, most, shards=(), held_as=jnp.bfloat16):
    gain = block_scale(rng, shape, shards, -0.22, 0.18) if shards else 1.0
    array = jax.random.normal(rng, shape, jnp.float32) * deviation * gain
    return jnp.minimum(jnp.maximum(array, -most), most).astype(held_as)


def setup_inputs(seed: int = 0) -> dict:
    splits = jax.random.split(jax.random.key(seed), 15)
    return {
        "tokens": bell_draw(splits[0], (TOKENS, D), 1.0, 6.0, ((0, 16), (1, 2))),
        "first_gain": jnp.clip(1.0 + 0.1 * jax.random.normal(splits[1], (D,), jnp.float32), 0.5, 1.5),
        "first_shift": bell_draw(splits[2], (D,), 0.3, 1.75, ((0, 32),), jnp.float32),
        "mixer_weight": bell_draw(splits[3], (D, 3, D), D ** -0.5, 0.1875, ((0, 16), (2, 2)), jnp.float32),
        "mixer_bias": bell_draw(splits[4], (2, D), 0.3, 1.75, ((1, 32),), jnp.float32),
        "merge_weight": bell_draw(splits[5], (D, D), 8 ** -0.5, 2.0, ((0, 2), (1, 16)), jnp.float32),
        "merge_bias": bell_draw(splits[6], (D,), 0.3, 1.75, ((0, 32),), jnp.float32),
        "second_gain": jnp.clip(1.0 + 0.1 * jax.random.normal(splits[7], (D,), jnp.float32), 0.5, 1.5),
        "second_shift": bell_draw(splits[8], (D,), 0.3, 1.75, ((0, 32),), jnp.float32),
        "expand_weight": bell_draw(splits[9], (D, FF), D ** -0.5, 0.1875, ((0, 16), (1, 2)), jnp.float32),
        "expand_bias": bell_draw(splits[10], (FF,), 0.3, 1.75, ((0, 32),), jnp.float32),
        "reduce_weight": bell_draw(splits[11], (FF, D), FF ** -0.5, 0.09375, ((0, 2), (1, 16)), jnp.float32),
        "reduce_bias": bell_draw(splits[12], (D,), 0.3, 1.75, ((0, 32),), jnp.float32),
        "cotangent": bell_draw(splits[13], (TOKENS, D), 1.0, 6.0, ((0, 16), (1, 2))),
    }


EPSILON = 1e-05
SLOPE = 1.702
HIGHEST = lax.Precision.HIGHEST

@jax.custom_vjp
def low(v):
    return lax.optimization_barrier(v.astype(jnp.bfloat16)).astype(jnp.float32)

@jax.custom_vjp
def low_back(v):
    return v

def low_keep(v):
    return (low(v), None)

def low_pass(kept, grad):
    return (grad,)

def back_keep(v):
    return (v, None)

def back_low(kept, grad):
    return (low(grad),)
low.defvjp(low_keep, low_pass)
low_back.defvjp(back_keep, back_low)

def normalize(values, gain_row, shift_row):
    row_mean = lax.optimization_barrier(jnp.mean(values, -1, keepdims=True))
    square = lax.optimization_barrier(jnp.mean(values * values, -1, keepdims=True))
    return (values - row_mean) * lax.rsqrt(square - row_mean * row_mean + EPSILON) * gain_row + shift_row

def image_attention(parts):
    queries, key_rows, values = parts
    scores = jnp.einsum('qhd,khd->hqk', queries, key_rows, precision=HIGHEST) * HEAD_DIM ** (-0.5)
    scores = low_back(scores)
    weights = low(jax.nn.softmax(scores, axis=-1))
    return jnp.einsum('hqk,khd->qhd', weights, values, precision=HIGHEST)

def layer(inputs, first_gain, first_shift, mixer_weight, mixer_bias, merge_weight, merge_bias, second_gain, second_shift, expand_weight, expand_bias, reduce_weight, reduce_bias):
    first_gain = low(first_gain)
    first_shift = low(first_shift)
    mixer_weight = low(mixer_weight)
    mixer_bias = low(mixer_bias)
    merge_weight = low(merge_weight)
    merge_bias = low(merge_bias)
    second_gain = low(second_gain)
    second_shift = low(second_shift)
    expand_weight = low(expand_weight)
    expand_bias = low(expand_bias)
    reduce_weight = low(reduce_weight)
    reduce_bias = low(reduce_bias)
    row_count = inputs.shape[0]
    first_low = low(normalize(inputs, first_gain, first_shift))
    projected = jnp.einsum('rd,dtc->rtc', first_low, mixer_weight, precision=HIGHEST)
    projected = projected + jnp.stack([mixer_bias[0], jnp.zeros_like(mixer_bias[0]), mixer_bias[1]])
    projected = low(low_back(projected))
    head_shape = (row_count // SEQ, SEQ, HEADS, HEAD_DIM)
    parts = (projected[:, 0].reshape(head_shape), projected[:, 1].reshape(head_shape), projected[:, 2].reshape(head_shape))
    attended = lax.map(jax.checkpoint(image_attention), parts).reshape(row_count, D)
    attended = low(low_back(attended))
    hidden = inputs + low_back(jnp.dot(attended, merge_weight, precision=HIGHEST)) + merge_bias
    second_low = low(normalize(hidden, second_gain, second_shift))
    expanded = low_back(jnp.dot(second_low, expand_weight, precision=HIGHEST) + expand_bias)
    activated = low(expanded * jax.nn.sigmoid(SLOPE * expanded))
    return hidden + low_back(jnp.dot(activated, reduce_weight, precision=HIGHEST)) + reduce_bias

def reference(tokens, first_gain, first_shift, mixer_weight, mixer_bias, merge_weight, merge_bias, second_gain, second_shift, expand_weight, expand_bias, reduce_weight, reduce_bias, cotangent):
    parameters = (first_gain, first_shift, mixer_weight, mixer_bias, merge_weight, merge_bias, second_gain, second_shift, expand_weight, expand_bias, reduce_weight, reduce_bias)
    block_rows = IMG * SEQ
    inputs = tokens.astype(jnp.float32).reshape(-1, block_rows, D)
    upstream = cotangent.astype(jnp.float32).reshape(-1, block_rows, D)

    def block_step(totals, block_item):
        block_inputs, block_upstream = block_item
        result, pullback = jax.vjp(layer, block_inputs, *parameters)
        gradients = pullback(block_upstream)
        totals = jax.tree.map(jnp.add, totals, tuple(gradients[1:]))
        return (totals, (result.astype(jnp.bfloat16), gradients[0]))
    initial = tuple((jnp.zeros_like(parameter) for parameter in parameters))
    totals, (outputs, input_grads) = lax.scan(block_step, initial, (inputs, upstream))
    return (outputs.reshape(-1, D), input_grads.reshape(-1, D), totals[0], totals[1], totals[2], totals[3], totals[4], totals[5], totals[6], totals[7], totals[8], totals[9], totals[10], totals[11])
```

```python
import jax
import jax.numpy as jnp
from jax import lax
from jax.experimental import pallas as pl
from jax.experimental.pallas import tpu as pltpu
from jax.sharding import PartitionSpec as P

HEAD_DIM = 64
SEQ = 577


EPSILON = 1e-05
SLOPE = 1.702


def quick_gelu(inputs):
    return inputs * jax.nn.sigmoid(SLOPE * inputs)


def gelu_slope(inputs):
    sigmoid_value = jax.nn.sigmoid(SLOPE * inputs)
    return sigmoid_value + SLOPE * inputs * sigmoid_value * (1.0 - sigmoid_value)


def own_columns(values, start, width):
    return lax.dynamic_slice_in_dim(values, start, width, values.ndim - 1)


def normalize(values, gain_row, shift_row):
    feature_count = values.shape[-1]
    row_mean = jnp.sum(values, -1, keepdims=True) / feature_count
    square = jnp.sum(values * values, -1, keepdims=True) / feature_count
    inverse = lax.rsqrt(square - row_mean * row_mean + EPSILON)
    scaled = (values - row_mean) * inverse
    return (scaled, inverse, scaled * gain_row + shift_row)


def column_sum(partial_value):
    return lax.psum_scatter(
        partial_value.astype(jnp.bfloat16), "col", scatter_dimension=1, tiled=True
    ).astype(jnp.float32)


def feature_totals(first_sum, second_sum):
    return lax.psum((first_sum, second_sum), "col")


def normed_gather(piece):
    return lax.all_gather(piece, "col", axis=1, tiled=True)


def shared_back(upstream, scaled, inverse, gain_row, feature_count):
    scaled_grad = upstream * gain_row
    totals = feature_totals(jnp.sum(scaled_grad, -1), jnp.sum(scaled_grad * scaled, -1))
    first_mean = totals[0][:, None] / feature_count
    second_mean = totals[1][:, None] / feature_count
    return inverse * (scaled_grad - first_mean - scaled * second_mean)


def fetch_weights(masters):
    return (
        lax.all_gather(masters[0], "row", axis=0, tiled=True),
        lax.all_gather(masters[1], "row", axis=1, tiled=True),
        lax.all_gather(masters[2], "row", axis=0, tiled=True),
        lax.all_gather(masters[3], "row", axis=1, tiled=True),
    )


def attend_forward(parts):
    queries, key_rows, values = parts
    score_scale = queries.shape[-1] ** (-0.5)
    scores = (
        jnp.einsum("qhd,khd->hqk", queries, key_rows, preferred_element_type=jnp.float32)
        * score_scale
    )
    score_top = jnp.max(scores, -1, keepdims=True)
    exponent = jnp.exp(scores - score_top)
    row_total = jnp.sum(exponent, -1, keepdims=True)
    weights = (exponent / row_total).astype(jnp.bfloat16)
    mixture = jnp.einsum("hqk,khd->qhd", weights, values, preferred_element_type=jnp.float32)
    return (mixture.astype(jnp.bfloat16), (score_top + jnp.log(row_total))[..., 0])


def attend_back(parts):
    queries, key_rows, values, log_total, upstream = parts
    score_scale = queries.shape[-1] ** (-0.5)
    scores = (
        jnp.einsum("qhd,khd->hqk", queries, key_rows, preferred_element_type=jnp.float32)
        * score_scale
    )
    probability = jnp.exp(scores - log_total[..., None])
    rounded = probability.astype(jnp.bfloat16)
    pulled = jnp.einsum("qhd,khd->hqk", upstream, values, preferred_element_type=jnp.float32)
    centre = jnp.sum(probability * pulled, -1, keepdims=True)
    score_grad = (probability * (pulled - centre)).astype(jnp.bfloat16)
    query_grad = (
        jnp.einsum("hqk,khd->qhd", score_grad, key_rows, preferred_element_type=jnp.float32)
        * score_scale
    )
    key_grad = (
        jnp.einsum("hqk,qhd->khd", score_grad, queries, preferred_element_type=jnp.float32)
        * score_scale
    )
    value_grad = jnp.einsum("hqk,qhd->khd", rounded, upstream, preferred_element_type=jnp.float32)
    return (query_grad, key_grad, value_grad)


def split_shards(
    tokens,
    first_gain,
    first_shift,
    mixer_weight,
    mixer_bias,
    merge_weight,
    merge_bias,
    second_gain,
    second_shift,
    expand_weight,
    expand_bias,
    reduce_weight,
    reduce_bias,
    cotangent,
):
    col_index = lax.axis_index("col")
    piece_width = tokens.shape[1]
    hidden_width = expand_weight.shape[1]
    start = col_index * piece_width
    hidden_start = col_index * hidden_width
    vector_pieces = jnp.stack(
        [
            first_gain,
            first_shift,
            mixer_bias[0],
            mixer_bias[1],
            merge_bias,
            second_gain,
            second_shift,
            reduce_bias,
        ]
    ).astype(jnp.bfloat16)
    vectors_low, expand_shift_low = (
        lax.all_gather(vector_pieces, ("row", "col"), axis=1, tiled=True),
        lax.all_gather(expand_bias.astype(jnp.bfloat16), ("row", "col"), axis=0, tiled=True),
    )
    vectors = vectors_low.astype(jnp.float32)
    feature_count = vectors.shape[1]
    first_gain_row, first_shift_row = (vectors[0], vectors[1])
    query_bias = own_columns(vectors[2], start, piece_width)
    value_bias = own_columns(vectors[3], start, piece_width)
    merge_shift = vectors[4]
    second_gain_row, second_shift_row = (vectors[5], vectors[6])
    reduce_shift = own_columns(vectors[7], start, piece_width)
    expand_shift = own_columns(expand_shift_low.astype(jnp.float32), hidden_start, hidden_width)
    masters = (
        mixer_weight.astype(jnp.bfloat16),
        merge_weight.astype(jnp.bfloat16),
        expand_weight.astype(jnp.bfloat16),
        reduce_weight.astype(jnp.bfloat16),
    )
    mixer_local, merger, expander, reducer = fetch_weights(masters)
    inputs_whole, upstream_whole = (
        lax.all_gather(tokens, "col", axis=1, tiled=True),
        lax.all_gather(cotangent, "col", axis=1, tiled=True),
    )
    inputs = inputs_whole.astype(jnp.float32)
    row_count = inputs.shape[0]
    first_scaled, first_inverse, first_normed = normalize(inputs, first_gain_row, first_shift_row)
    first_low = first_normed.astype(jnp.bfloat16)
    projected = jnp.einsum(
        "rd,dtc->rtc", first_low, mixer_local, preferred_element_type=jnp.float32
    )
    projected = projected + jnp.stack([query_bias, jnp.zeros_like(query_bias), value_bias])
    projected_low = projected.astype(jnp.bfloat16)
    head_shape = (row_count // SEQ, SEQ, piece_width // HEAD_DIM, HEAD_DIM)
    queries = projected_low[:, 0].reshape(head_shape)
    key_rows = projected_low[:, 1].reshape(head_shape)
    values = projected_low[:, 2].reshape(head_shape)
    attended, log_total = lax.map(attend_forward, (queries, key_rows, values))
    attended = attended.reshape(row_count, piece_width)
    merged_part = jnp.dot(attended, merger, preferred_element_type=jnp.float32)
    hidden_own = (
        own_columns(inputs, start, piece_width)
        + column_sum(merged_part)
        + own_columns(merge_shift, start, piece_width)
    )
    totals = feature_totals(jnp.sum(hidden_own, -1), jnp.sum(hidden_own * hidden_own, -1))
    row_mean = totals[0][:, None] / feature_count
    square = totals[1][:, None] / feature_count
    second_inverse = lax.rsqrt(square - row_mean * row_mean + EPSILON)
    second_scaled = (hidden_own - row_mean) * second_inverse
    second_gain_own = own_columns(second_gain_row, start, piece_width)
    second_piece = second_scaled * second_gain_own + own_columns(
        second_shift_row, start, piece_width
    )
    second_low = normed_gather(second_piece.astype(jnp.bfloat16))
    expanded = jnp.dot(second_low, expander, preferred_element_type=jnp.float32) + expand_shift
    activated = quick_gelu(expanded).astype(jnp.bfloat16)
    reduced = column_sum(jnp.dot(activated, reducer, preferred_element_type=jnp.float32))
    layer_output = (hidden_own + reduced + reduce_shift).astype(jnp.bfloat16)
    masters_again = lax.optimization_barrier((masters, layer_output))[0]
    mixer_local, merger, expander, reducer = fetch_weights(masters_again)
    upstream_own = cotangent.astype(jnp.float32)
    reducer_grad = jnp.einsum(
        "rf,rd->fd", activated, upstream_whole, preferred_element_type=jnp.float32
    )
    activated_grad = jnp.einsum(
        "rd,fd->rf", upstream_whole, reducer, preferred_element_type=jnp.float32
    )
    expanded_grad = (activated_grad * gelu_slope(expanded)).astype(jnp.bfloat16)
    expander_grad = jnp.einsum(
        "rd,rf->df", second_low, expanded_grad, preferred_element_type=jnp.float32
    )
    expand_shift_grad = jnp.sum(expanded_grad.astype(jnp.float32), 0)
    second_part = jnp.einsum(
        "rf,df->rd", expanded_grad, expander, preferred_element_type=jnp.float32
    )
    second_grad = column_sum(second_part)
    hidden_part = shared_back(
        second_grad, second_scaled, second_inverse, second_gain_own, feature_count
    )
    hidden_grad = upstream_own + hidden_part
    second_gain_grad = jnp.sum(second_grad * second_scaled, 0)
    second_shift_grad = jnp.sum(second_grad, 0)
    hidden_low = normed_gather(hidden_grad.astype(jnp.bfloat16))
    merger_grad = jnp.einsum("rc,rd->cd", attended, hidden_low, preferred_element_type=jnp.float32)
    attended_grad = jnp.einsum(
        "rd,cd->rc", hidden_low, merger, preferred_element_type=jnp.float32
    ).astype(jnp.bfloat16)
    query_grad, key_grad, value_grad = lax.map(
        attend_back, (queries, key_rows, values, log_total, attended_grad.reshape(head_shape))
    )
    projected_grad = jnp.stack(
        [
            query_grad.reshape(row_count, piece_width),
            key_grad.reshape(row_count, piece_width),
            value_grad.reshape(row_count, piece_width),
        ],
        1,
    ).astype(jnp.bfloat16)
    mixer_grad = jnp.einsum(
        "rd,rtc->dtc", first_low, projected_grad, preferred_element_type=jnp.float32
    )
    bias_sums = jnp.sum(projected_grad.astype(jnp.float32), 0)
    first_part = jnp.einsum(
        "rtc,dtc->rd", projected_grad, mixer_local, preferred_element_type=jnp.float32
    )
    first_grad = column_sum(first_part)
    first_scaled_own = own_columns(first_scaled, start, piece_width)
    input_part = shared_back(
        first_grad,
        first_scaled_own,
        first_inverse,
        own_columns(first_gain_row, start, piece_width),
        feature_count,
    )
    tokens_gradient = hidden_grad + input_part
    own_vector_grads = jnp.stack(
        [
            jnp.sum(first_grad * first_scaled_own, 0),
            jnp.sum(first_grad, 0),
            bias_sums[0],
            bias_sums[2],
            jnp.sum(hidden_grad, 0),
            second_gain_grad,
            second_shift_grad,
            jnp.sum(upstream_own, 0),
        ]
    )
    vector_whole = lax.dynamic_update_slice(
        jnp.zeros((8, feature_count), jnp.float32), own_vector_grads, (jnp.int32(0), start)
    )
    expand_whole = lax.dynamic_update_slice(
        jnp.zeros((hidden_width * lax.axis_size("col"),), jnp.float32),
        expand_shift_grad,
        (hidden_start,),
    )
    vector_total, expand_bias_total = (
        lax.psum_scatter(vector_whole, ("row", "col"), scatter_dimension=1, tiled=True),
        lax.psum_scatter(expand_whole, ("row", "col"), scatter_dimension=0, tiled=True),
    )
    mixer_total, merge_total, expand_total, reduce_total = (
        lax.psum_scatter(
            mixer_grad.astype(jnp.bfloat16), "row", scatter_dimension=0, tiled=True
        ).astype(jnp.float32),
        lax.psum_scatter(
            merger_grad.astype(jnp.bfloat16), "row", scatter_dimension=1, tiled=True
        ).astype(jnp.float32),
        lax.psum_scatter(
            expander_grad.astype(jnp.bfloat16), "row", scatter_dimension=0, tiled=True
        ).astype(jnp.float32),
        lax.psum_scatter(
            reducer_grad.astype(jnp.bfloat16), "row", scatter_dimension=1, tiled=True
        ).astype(jnp.float32),
    )
    return (
        layer_output,
        tokens_gradient,
        vector_total[0],
        vector_total[1],
        mixer_total,
        jnp.stack([vector_total[2], vector_total[3]]),
        merge_total,
        vector_total[4],
        vector_total[5],
        vector_total[6],
        expand_total,
        expand_bias_total,
        reduce_total,
        vector_total[7],
    )


GROUP = 128
BOTH = ("col", "row")


def attention_forward_kernel(projected_ref, attended_ref):
    for head in range(GROUP // HEAD_DIM):
        at = head * HEAD_DIM
        queries = projected_ref[0, :, at : at + HEAD_DIM] * jnp.bfloat16(HEAD_DIM**-0.5)
        key_rows = projected_ref[0, :, GROUP + at : GROUP + at + HEAD_DIM]
        values = projected_ref[0, :, 2 * GROUP + at : 2 * GROUP + at + HEAD_DIM]
        scores = lax.dot_general(
            key_rows, queries, (((1,), (1,)), ((), ())), preferred_element_type=jnp.float32
        )
        exponent = jnp.exp(scores - jnp.max(scores, 0, keepdims=True))
        weights = exponent * (1.0 / jnp.sum(exponent, 0, keepdims=True))
        mixture = lax.dot_general(
            values,
            weights.astype(jnp.bfloat16),
            (((0,), (0,)), ((), ())),
            preferred_element_type=jnp.float32,
        )
        attended_ref[0, :, at : at + HEAD_DIM] = mixture.T.astype(jnp.bfloat16)


def attention_back_kernel(projected_ref, upstream_ref, grad_ref):
    for head in range(GROUP // HEAD_DIM):
        at = head * HEAD_DIM
        queries = projected_ref[0, :, at : at + HEAD_DIM] * jnp.bfloat16(HEAD_DIM**-0.5)
        key_rows = projected_ref[0, :, GROUP + at : GROUP + at + HEAD_DIM]
        values = projected_ref[0, :, 2 * GROUP + at : 2 * GROUP + at + HEAD_DIM]
        upstream = upstream_ref[0, :, at : at + HEAD_DIM]
        scores = lax.dot_general(
            key_rows, queries, (((1,), (1,)), ((), ())), preferred_element_type=jnp.float32
        )
        exponent = jnp.exp(scores - jnp.max(scores, 0, keepdims=True))
        weights = exponent * (1.0 / jnp.sum(exponent, 0, keepdims=True))
        pulled = lax.dot_general(
            values, upstream, (((1,), (1,)), ((), ())), preferred_element_type=jnp.float32
        )
        centre = jnp.sum(weights * pulled, 0, keepdims=True)
        score_grad = (weights * (pulled - centre)).astype(jnp.bfloat16)
        value_grad = jnp.dot(
            weights.astype(jnp.bfloat16), upstream, preferred_element_type=jnp.float32
        )
        key_grad = jnp.dot(score_grad, queries, preferred_element_type=jnp.float32)
        query_grad = lax.dot_general(
            key_rows, score_grad, (((0,), (0,)), ((), ())), preferred_element_type=jnp.float32
        )
        query_grad = query_grad.T * HEAD_DIM**-0.5
        grad_ref[0, :, at : at + HEAD_DIM] = query_grad.astype(jnp.bfloat16)
        grad_ref[0, :, GROUP + at : GROUP + at + HEAD_DIM] = key_grad.astype(jnp.bfloat16)
        grad_ref[0, :, 2 * GROUP + at : 2 * GROUP + at + HEAD_DIM] = value_grad.astype(
            jnp.bfloat16
        )


def attention_forward(projected):
    halves, rows, width = projected.shape
    groups = width // (3 * GROUP)
    return pl.pallas_call(
        attention_forward_kernel,
        grid=(halves, groups),
        in_specs=[pl.BlockSpec((1, rows, 3 * GROUP), lambda h, g: (h, 0, g))],
        out_specs=pl.BlockSpec((1, rows, GROUP), lambda h, g: (h, 0, g)),
        out_shape=jax.ShapeDtypeStruct((halves, rows, groups * GROUP), jnp.bfloat16),
        name="attention_forward",
    )(projected)


def attention_back(projected, upstream):
    halves, rows, width = projected.shape
    groups = width // (3 * GROUP)
    return pl.pallas_call(
        attention_back_kernel,
        grid=(halves, groups),
        in_specs=[
            pl.BlockSpec((1, rows, 3 * GROUP), lambda h, g: (h, 0, g)),
            pl.BlockSpec((1, rows, GROUP), lambda h, g: (h, 0, g)),
        ],
        out_specs=pl.BlockSpec((1, rows, 3 * GROUP), lambda h, g: (h, 0, g)),
        out_shape=jax.ShapeDtypeStruct(projected.shape, jnp.bfloat16),
        name="attention_back",
    )(projected, upstream)


def to_image(piece):
    col = lax.axis_index("col")
    rows = piece.shape[0] // 2
    kept = lax.dynamic_slice_in_dim(piece, col * rows, rows, 0)
    sent = lax.dynamic_slice_in_dim(piece, (1 - col) * rows, rows, 0)
    other = lax.ppermute(sent, "col", [(0, 1), (1, 0)])
    return jnp.where(
        col == 0, jnp.concatenate([kept, other], 1), jnp.concatenate([other, kept], 1)
    )


def from_image(whole):
    col = lax.axis_index("col")
    width = whole.shape[1] // 2
    kept = lax.dynamic_slice_in_dim(whole, col * width, width, 1)
    sent = lax.dynamic_slice_in_dim(whole, (1 - col) * width, width, 1)
    other = lax.ppermute(sent, "col", [(0, 1), (1, 0)])
    return jnp.where(
        col == 0, jnp.concatenate([kept, other], 0), jnp.concatenate([other, kept], 0)
    )


def gather_blocks(block):
    whole = lax.all_gather(block, BOTH, axis=0, tiled=True)
    return whole.reshape(2, whole.shape[0] // 2, block.shape[1])


def scatter_blocks(halves):
    flat = jnp.concatenate(halves, 0)
    return lax.psum_scatter(flat, BOTH, scatter_dimension=0, tiled=True).astype(jnp.float32)


def product(left, right, left_at, right_at):
    return lax.dot_general(
        left, right, (((left_at,), (right_at,)), ((), ())), preferred_element_type=jnp.float32
    )


def norm_back(upstream, scaled, inverse, gain_row):
    scaled_grad = upstream * gain_row
    first_mean = jnp.mean(scaled_grad, -1, keepdims=True)
    second_mean = jnp.mean(scaled_grad * scaled, -1, keepdims=True)
    return inverse * (scaled_grad - first_mean - scaled * second_mean)


def group_order(block):
    rows = block.shape[0]
    return block.reshape(rows, 3, -1, GROUP).transpose(0, 2, 1, 3).reshape(rows, -1)


def part_order(block):
    rows = block.shape[0]
    return block.reshape(rows, -1, 3, GROUP).transpose(0, 2, 1, 3).reshape(rows, 3, -1)


def image_shards(
    tokens,
    first_gain,
    first_shift,
    mixer_weight,
    mixer_bias,
    merge_weight,
    merge_bias,
    second_gain,
    second_shift,
    expand_weight,
    expand_bias,
    reduce_weight,
    reduce_bias,
    cotangent,
):
    low = jnp.bfloat16
    cols = lax.axis_size("col")
    rows = lax.axis_size("row")
    piece = first_gain.shape[0]
    hidden_piece = expand_bias.shape[0]
    block_rows = mixer_weight.shape[0]
    vectors = jnp.concatenate(
        [
            jnp.stack(
                [
                    first_gain,
                    first_shift,
                    mixer_bias[0],
                    mixer_bias[1],
                    merge_bias,
                    second_gain,
                    second_shift,
                    reduce_bias,
                ]
            ).reshape(-1),
            expand_bias,
        ]
    ).astype(low)
    vector_rows = vectors.shape[0] // GROUP
    vector_block = jnp.pad(
        vectors.reshape(vector_rows, GROUP), ((0, block_rows - vector_rows), (0, 0))
    )
    mixer_width = 3 * mixer_weight.shape[2]
    first_block = jnp.concatenate([group_order(mixer_weight).astype(low), vector_block], 1)
    mixed = gather_blocks(first_block)
    mixer = mixed[:, :, :mixer_width]
    merger = gather_blocks(merge_weight.astype(low).T)
    expander = gather_blocks(expand_weight.astype(low))
    reducer = gather_blocks(reduce_weight.astype(low).T)
    spread = mixed[:, :, mixer_width:].reshape(cols, rows, block_rows, GROUP)[:, :, :vector_rows]
    spread = spread.reshape(cols, rows, -1).astype(jnp.float32).transpose(1, 0, 2)
    rows_of = spread[:, :, : 8 * piece].reshape(rows, cols, 8, piece).transpose(2, 0, 1, 3)
    rows_of = rows_of.reshape(8, -1)
    expand_shift = spread[:, :, 8 * piece :].reshape(cols, -1)
    first_gain_row, first_shift_row = rows_of[0], rows_of[1]
    query_bias, value_bias, merge_shift = rows_of[2], rows_of[3], rows_of[4]
    second_gain_row, second_shift_row, reduce_shift = rows_of[5], rows_of[6], rows_of[7]
    mixer_shift = jnp.stack(
        [
            query_bias.reshape(cols, -1, GROUP),
            jnp.zeros_like(query_bias).reshape(cols, -1, GROUP),
            value_bias.reshape(cols, -1, GROUP),
        ],
        2,
    ).reshape(cols, -1)

    image = to_image(tokens)
    upstream_low = to_image(cotangent)
    inputs = image.astype(jnp.float32)
    first_scaled, first_inverse, first_normed = normalize(inputs, first_gain_row, first_shift_row)
    first_low = first_normed.astype(low)
    projected = jnp.stack(
        [(product(first_low, mixer[h], 1, 0) + mixer_shift[h]).astype(low) for h in range(cols)]
    )
    attended = attention_forward(projected)
    merged = sum(product(attended[h], merger[h], 1, 1) for h in range(cols))
    hidden = inputs + merged + merge_shift
    second_scaled, second_inverse, second_normed = normalize(
        hidden, second_gain_row, second_shift_row
    )
    second_low = second_normed.astype(low)
    expanded = [product(second_low, expander[h], 1, 0) + expand_shift[h] for h in range(cols)]
    activated = [quick_gelu(part).astype(low) for part in expanded]
    reduced = sum(product(activated[h], reducer[h], 1, 1) for h in range(cols))
    layer_output = from_image((hidden + reduced + reduce_shift).astype(low))

    upstream = upstream_low.astype(jnp.float32)
    reducer_grad = [product(upstream_low, activated[h], 0, 0).astype(low) for h in range(cols)]
    reduce_total = scatter_blocks(reducer_grad)
    expanded_grad = [
        (product(upstream_low, reducer[h], 1, 0) * gelu_slope(expanded[h])).astype(low)
        for h in range(cols)
    ]
    expander_grad = [product(second_low, expanded_grad[h], 0, 0).astype(low) for h in range(cols)]
    expand_total = scatter_blocks(expander_grad)
    expand_shift_grad = [jnp.sum(part.astype(jnp.float32), 0) for part in expanded_grad]
    second_grad = sum(product(expanded_grad[h], expander[h], 1, 1) for h in range(cols))
    hidden_grad = upstream + norm_back(
        second_grad, second_scaled, second_inverse, second_gain_row
    )
    hidden_low = hidden_grad.astype(low)
    merger_grad = [product(hidden_low, attended[h], 0, 0).astype(low) for h in range(cols)]
    merge_total = scatter_blocks(merger_grad)
    attended_grad = jnp.stack(
        [product(hidden_low, merger[h], 1, 0).astype(low) for h in range(cols)]
    )
    projected_grad = attention_back(projected, attended_grad)
    mixer_grad = [product(first_low, projected_grad[h], 0, 0).astype(low) for h in range(cols)]
    bias_sums = jnp.sum(projected_grad.astype(jnp.float32), 1)
    bias_sums = bias_sums.reshape(cols, -1, 3, GROUP).transpose(2, 0, 1, 3).reshape(3, -1)
    first_grad = sum(product(projected_grad[h], mixer[h], 1, 1) for h in range(cols))
    input_grad = hidden_grad + norm_back(first_grad, first_scaled, first_inverse, first_gain_row)
    tokens_gradient = from_image(input_grad.astype(low)).astype(jnp.float32)
    vector_grads = jnp.stack(
        [
            jnp.sum(first_grad * first_scaled, 0),
            jnp.sum(first_grad, 0),
            bias_sums[0],
            bias_sums[2],
            jnp.sum(hidden_grad, 0),
            jnp.sum(second_grad * second_scaled, 0),
            jnp.sum(second_grad, 0),
            jnp.sum(upstream, 0),
        ]
    )
    vector_grads = vector_grads.reshape(8, rows, cols, piece).transpose(2, 1, 0, 3)
    hidden_grads = jnp.concatenate(expand_shift_grad).reshape(rows, cols, hidden_piece)
    vector_grads = jnp.concatenate(
        [vector_grads.reshape(cols, rows, -1), hidden_grads.transpose(1, 0, 2)], 2
    )
    vector_grads = vector_grads.reshape(cols, rows, vector_rows, GROUP).astype(low)
    vector_grads = jnp.pad(
        vector_grads, ((0, 0), (0, 0), (0, block_rows - vector_rows), (0, 0))
    ).reshape(cols, rows * block_rows, GROUP)
    mixed_total = scatter_blocks(
        [jnp.concatenate([mixer_grad[h], vector_grads[h]], 1) for h in range(cols)]
    )
    mixer_total = part_order(mixed_total[:, :mixer_width])
    vector_total = mixed_total[:vector_rows, mixer_width:].reshape(-1)
    small = vector_total[: 8 * piece].reshape(8, piece)
    return (
        layer_output,
        tokens_gradient,
        small[0],
        small[1],
        mixer_total,
        small[2:4],
        merge_total.T,
        small[4],
        small[5],
        small[6],
        expand_total,
        vector_total[8 * piece :],
        reduce_total.T,
        small[7],
    )


def solution(mesh):
    def body(*arguments):
        images = arguments[0].shape[0] // SEQ
        whole = images == 2 and lax.axis_size("col") == 2
        return (image_shards if whole else split_shards)(*arguments)

    return jax.shard_map(
        body,
        mesh=mesh,
        in_specs=(
            P("row", "col"),
            P(("row", "col")),
            P(("row", "col")),
            P("row", None, "col"),
            P(None, ("row", "col")),
            P("col", "row"),
            P(("row", "col")),
            P(("row", "col")),
            P(("row", "col")),
            P("row", "col"),
            P(("row", "col")),
            P("col", "row"),
            P(("row", "col")),
            P("row", "col"),
        ),
        out_specs=(
            P("row", "col"),
            P("row", "col"),
            P(("row", "col")),
            P(("row", "col")),
            P("row", None, "col"),
            P(None, ("row", "col")),
            P("col", "row"),
            P(("row", "col")),
            P(("row", "col")),
            P(("row", "col")),
            P("row", "col"),
            P(("row", "col")),
            P("col", "row"),
            P(("row", "col")),
        ),
        check_vma=False,
    )
```

```python
import functools

import jax
import jax.numpy as jnp
from jax import lax
from jax.experimental import pallas as pl
from jax.experimental.pallas import tpu as pltpu
from jax.sharding import PartitionSpec as P

HEAD_DIM = 64
SEQ = 577


EPSILON = 1e-05
SLOPE = 1.702


def quick_gelu(inputs):
    return inputs * jax.nn.sigmoid(SLOPE * inputs)


def gelu_slope(inputs):
    sigmoid_value = jax.nn.sigmoid(SLOPE * inputs)
    return sigmoid_value + SLOPE * inputs * sigmoid_value * (1.0 - sigmoid_value)


def own_columns(values, start, width):
    return lax.dynamic_slice_in_dim(values, start, width, values.ndim - 1)


def normalize(values, gain_row, shift_row):
    feature_count = values.shape[-1]
    row_mean = jnp.sum(values, -1, keepdims=True) / feature_count
    square = jnp.sum(values * values, -1, keepdims=True) / feature_count
    inverse = lax.rsqrt(square - row_mean * row_mean + EPSILON)
    scaled = (values - row_mean) * inverse
    return (scaled, inverse, scaled * gain_row + shift_row)


def column_sum(partial_value):
    return lax.psum_scatter(
        partial_value.astype(jnp.bfloat16), "col", scatter_dimension=1, tiled=True
    ).astype(jnp.float32)


def feature_totals(first_sum, second_sum):
    return lax.psum((first_sum, second_sum), "col")


def normed_gather(piece):
    return lax.all_gather(piece, "col", axis=1, tiled=True)


def shared_back(upstream, scaled, inverse, gain_row, feature_count):
    scaled_grad = upstream * gain_row
    totals = feature_totals(jnp.sum(scaled_grad, -1), jnp.sum(scaled_grad * scaled, -1))
    first_mean = totals[0][:, None] / feature_count
    second_mean = totals[1][:, None] / feature_count
    return inverse * (scaled_grad - first_mean - scaled * second_mean)


def fetch_weights(masters):
    return (
        lax.all_gather(masters[0], "row", axis=0, tiled=True),
        lax.all_gather(masters[1], "row", axis=1, tiled=True),
        lax.all_gather(masters[2], "row", axis=0, tiled=True),
        lax.all_gather(masters[3], "row", axis=1, tiled=True),
    )


def attend_forward(parts):
    queries, key_rows, values = parts
    score_scale = queries.shape[-1] ** (-0.5)
    scores = (
        jnp.einsum("qhd,khd->hqk", queries, key_rows, preferred_element_type=jnp.float32)
        * score_scale
    )
    score_top = jnp.max(scores, -1, keepdims=True)
    exponent = jnp.exp(scores - score_top)
    row_total = jnp.sum(exponent, -1, keepdims=True)
    weights = (exponent / row_total).astype(jnp.bfloat16)
    mixture = jnp.einsum("hqk,khd->qhd", weights, values, preferred_element_type=jnp.float32)
    return (mixture.astype(jnp.bfloat16), (score_top + jnp.log(row_total))[..., 0])


def attend_back(parts):
    queries, key_rows, values, log_total, upstream = parts
    score_scale = queries.shape[-1] ** (-0.5)
    scores = (
        jnp.einsum("qhd,khd->hqk", queries, key_rows, preferred_element_type=jnp.float32)
        * score_scale
    )
    probability = jnp.exp(scores - log_total[..., None])
    rounded = probability.astype(jnp.bfloat16)
    pulled = jnp.einsum("qhd,khd->hqk", upstream, values, preferred_element_type=jnp.float32)
    centre = jnp.sum(probability * pulled, -1, keepdims=True)
    score_grad = (probability * (pulled - centre)).astype(jnp.bfloat16)
    query_grad = (
        jnp.einsum("hqk,khd->qhd", score_grad, key_rows, preferred_element_type=jnp.float32)
        * score_scale
    )
    key_grad = (
        jnp.einsum("hqk,qhd->khd", score_grad, queries, preferred_element_type=jnp.float32)
        * score_scale
    )
    value_grad = jnp.einsum("hqk,qhd->khd", rounded, upstream, preferred_element_type=jnp.float32)
    return (query_grad, key_grad, value_grad)


def split_shards(
    tokens,
    first_gain,
    first_shift,
    mixer_weight,
    mixer_bias,
    merge_weight,
    merge_bias,
    second_gain,
    second_shift,
    expand_weight,
    expand_bias,
    reduce_weight,
    reduce_bias,
    cotangent,
):
    col_index = lax.axis_index("col")
    piece_width = tokens.shape[1]
    hidden_width = expand_weight.shape[1]
    start = col_index * piece_width
    hidden_start = col_index * hidden_width
    vector_pieces = jnp.stack(
        [
            first_gain,
            first_shift,
            mixer_bias[0],
            mixer_bias[1],
            merge_bias,
            second_gain,
            second_shift,
            reduce_bias,
        ]
    ).astype(jnp.bfloat16)
    vectors_low, expand_shift_low = (
        lax.all_gather(vector_pieces, ("row", "col"), axis=1, tiled=True),
        lax.all_gather(expand_bias.astype(jnp.bfloat16), ("row", "col"), axis=0, tiled=True),
    )
    vectors = vectors_low.astype(jnp.float32)
    feature_count = vectors.shape[1]
    first_gain_row, first_shift_row = (vectors[0], vectors[1])
    query_bias = own_columns(vectors[2], start, piece_width)
    value_bias = own_columns(vectors[3], start, piece_width)
    merge_shift = vectors[4]
    second_gain_row, second_shift_row = (vectors[5], vectors[6])
    reduce_shift = own_columns(vectors[7], start, piece_width)
    expand_shift = own_columns(expand_shift_low.astype(jnp.float32), hidden_start, hidden_width)
    masters = (
        mixer_weight.astype(jnp.bfloat16),
        merge_weight.astype(jnp.bfloat16),
        expand_weight.astype(jnp.bfloat16),
        reduce_weight.astype(jnp.bfloat16),
    )
    mixer_local, merger, expander, reducer = fetch_weights(masters)
    inputs_whole, upstream_whole = (
        lax.all_gather(tokens, "col", axis=1, tiled=True),
        lax.all_gather(cotangent, "col", axis=1, tiled=True),
    )
    inputs = inputs_whole.astype(jnp.float32)
    row_count = inputs.shape[0]
    first_scaled, first_inverse, first_normed = normalize(inputs, first_gain_row, first_shift_row)
    first_low = first_normed.astype(jnp.bfloat16)
    projected = jnp.einsum(
        "rd,dtc->rtc", first_low, mixer_local, preferred_element_type=jnp.float32
    )
    projected = projected + jnp.stack([query_bias, jnp.zeros_like(query_bias), value_bias])
    projected_low = projected.astype(jnp.bfloat16)
    head_shape = (row_count // SEQ, SEQ, piece_width // HEAD_DIM, HEAD_DIM)
    queries = projected_low[:, 0].reshape(head_shape)
    key_rows = projected_low[:, 1].reshape(head_shape)
    values = projected_low[:, 2].reshape(head_shape)
    attended, log_total = lax.map(attend_forward, (queries, key_rows, values))
    attended = attended.reshape(row_count, piece_width)
    merged_part = jnp.dot(attended, merger, preferred_element_type=jnp.float32)
    hidden_own = (
        own_columns(inputs, start, piece_width)
        + column_sum(merged_part)
        + own_columns(merge_shift, start, piece_width)
    )
    totals = feature_totals(jnp.sum(hidden_own, -1), jnp.sum(hidden_own * hidden_own, -1))
    row_mean = totals[0][:, None] / feature_count
    square = totals[1][:, None] / feature_count
    second_inverse = lax.rsqrt(square - row_mean * row_mean + EPSILON)
    second_scaled = (hidden_own - row_mean) * second_inverse
    second_gain_own = own_columns(second_gain_row, start, piece_width)
    second_piece = second_scaled * second_gain_own + own_columns(
        second_shift_row, start, piece_width
    )
    second_low = normed_gather(second_piece.astype(jnp.bfloat16))
    expanded = jnp.dot(second_low, expander, preferred_element_type=jnp.float32) + expand_shift
    activated = quick_gelu(expanded).astype(jnp.bfloat16)
    reduced = column_sum(jnp.dot(activated, reducer, preferred_element_type=jnp.float32))
    layer_output = (hidden_own + reduced + reduce_shift).astype(jnp.bfloat16)
    masters_again = lax.optimization_barrier((masters, layer_output))[0]
    mixer_local, merger, expander, reducer = fetch_weights(masters_again)
    upstream_own = cotangent.astype(jnp.float32)
    reducer_grad = jnp.einsum(
        "rf,rd->fd", activated, upstream_whole, preferred_element_type=jnp.float32
    )
    activated_grad = jnp.einsum(
        "rd,fd->rf", upstream_whole, reducer, preferred_element_type=jnp.float32
    )
    expanded_grad = (activated_grad * gelu_slope(expanded)).astype(jnp.bfloat16)
    expander_grad = jnp.einsum(
        "rd,rf->df", second_low, expanded_grad, preferred_element_type=jnp.float32
    )
    expand_shift_grad = jnp.sum(expanded_grad.astype(jnp.float32), 0)
    second_part = jnp.einsum(
        "rf,df->rd", expanded_grad, expander, preferred_element_type=jnp.float32
    )
    second_grad = column_sum(second_part)
    hidden_part = shared_back(
        second_grad, second_scaled, second_inverse, second_gain_own, feature_count
    )
    hidden_grad = upstream_own + hidden_part
    second_gain_grad = jnp.sum(second_grad * second_scaled, 0)
    second_shift_grad = jnp.sum(second_grad, 0)
    hidden_low = normed_gather(hidden_grad.astype(jnp.bfloat16))
    merger_grad = jnp.einsum("rc,rd->cd", attended, hidden_low, preferred_element_type=jnp.float32)
    attended_grad = jnp.einsum(
        "rd,cd->rc", hidden_low, merger, preferred_element_type=jnp.float32
    ).astype(jnp.bfloat16)
    query_grad, key_grad, value_grad = lax.map(
        attend_back, (queries, key_rows, values, log_total, attended_grad.reshape(head_shape))
    )
    projected_grad = jnp.stack(
        [
            query_grad.reshape(row_count, piece_width),
            key_grad.reshape(row_count, piece_width),
            value_grad.reshape(row_count, piece_width),
        ],
        1,
    ).astype(jnp.bfloat16)
    mixer_grad = jnp.einsum(
        "rd,rtc->dtc", first_low, projected_grad, preferred_element_type=jnp.float32
    )
    bias_sums = jnp.sum(projected_grad.astype(jnp.float32), 0)
    first_part = jnp.einsum(
        "rtc,dtc->rd", projected_grad, mixer_local, preferred_element_type=jnp.float32
    )
    first_grad = column_sum(first_part)
    first_scaled_own = own_columns(first_scaled, start, piece_width)
    input_part = shared_back(
        first_grad,
        first_scaled_own,
        first_inverse,
        own_columns(first_gain_row, start, piece_width),
        feature_count,
    )
    tokens_gradient = hidden_grad + input_part
    own_vector_grads = jnp.stack(
        [
            jnp.sum(first_grad * first_scaled_own, 0),
            jnp.sum(first_grad, 0),
            bias_sums[0],
            bias_sums[2],
            jnp.sum(hidden_grad, 0),
            second_gain_grad,
            second_shift_grad,
            jnp.sum(upstream_own, 0),
        ]
    )
    vector_whole = lax.dynamic_update_slice(
        jnp.zeros((8, feature_count), jnp.float32), own_vector_grads, (jnp.int32(0), start)
    )
    expand_whole = lax.dynamic_update_slice(
        jnp.zeros((hidden_width * lax.axis_size("col"),), jnp.float32),
        expand_shift_grad,
        (hidden_start,),
    )
    vector_total, expand_bias_total = (
        lax.psum_scatter(vector_whole, ("row", "col"), scatter_dimension=1, tiled=True),
        lax.psum_scatter(expand_whole, ("row", "col"), scatter_dimension=0, tiled=True),
    )
    mixer_total, merge_total, expand_total, reduce_total = (
        lax.psum_scatter(
            mixer_grad.astype(jnp.bfloat16), "row", scatter_dimension=0, tiled=True
        ).astype(jnp.float32),
        lax.psum_scatter(
            merger_grad.astype(jnp.bfloat16), "row", scatter_dimension=1, tiled=True
        ).astype(jnp.float32),
        lax.psum_scatter(
            expander_grad.astype(jnp.bfloat16), "row", scatter_dimension=0, tiled=True
        ).astype(jnp.float32),
        lax.psum_scatter(
            reducer_grad.astype(jnp.bfloat16), "row", scatter_dimension=1, tiled=True
        ).astype(jnp.float32),
    )
    return (
        layer_output,
        tokens_gradient,
        vector_total[0],
        vector_total[1],
        mixer_total,
        jnp.stack([vector_total[2], vector_total[3]]),
        merge_total,
        vector_total[4],
        vector_total[5],
        vector_total[6],
        expand_total,
        expand_bias_total,
        reduce_total,
        vector_total[7],
    )


GROUP = 128


def attention_forward_kernel(projected_ref, attended_ref):
    for head in range(GROUP // HEAD_DIM):
        at = head * HEAD_DIM
        queries = projected_ref[0, :, at : at + HEAD_DIM] * jnp.bfloat16(HEAD_DIM**-0.5)
        key_rows = projected_ref[0, :, GROUP + at : GROUP + at + HEAD_DIM]
        values = projected_ref[0, :, 2 * GROUP + at : 2 * GROUP + at + HEAD_DIM]
        scores = lax.dot_general(
            key_rows, queries, (((1,), (1,)), ((), ())), preferred_element_type=jnp.float32
        )
        exponent = jnp.exp(scores - jnp.max(scores, 0, keepdims=True))
        weights = exponent * (1.0 / jnp.sum(exponent, 0, keepdims=True))
        mixture = lax.dot_general(
            values,
            weights.astype(jnp.bfloat16),
            (((0,), (0,)), ((), ())),
            preferred_element_type=jnp.float32,
        )
        attended_ref[0, :, at : at + HEAD_DIM] = mixture.T.astype(jnp.bfloat16)


def attention_back_kernel(projected_ref, upstream_ref, grad_ref):
    for head in range(GROUP // HEAD_DIM):
        at = head * HEAD_DIM
        queries = projected_ref[0, :, at : at + HEAD_DIM] * jnp.bfloat16(HEAD_DIM**-0.5)
        key_rows = projected_ref[0, :, GROUP + at : GROUP + at + HEAD_DIM]
        values = projected_ref[0, :, 2 * GROUP + at : 2 * GROUP + at + HEAD_DIM]
        upstream = upstream_ref[0, :, at : at + HEAD_DIM]
        scores = lax.dot_general(
            key_rows, queries, (((1,), (1,)), ((), ())), preferred_element_type=jnp.float32
        )
        exponent = jnp.exp(scores - jnp.max(scores, 0, keepdims=True))
        weights = exponent * (1.0 / jnp.sum(exponent, 0, keepdims=True))
        pulled = lax.dot_general(
            values, upstream, (((1,), (1,)), ((), ())), preferred_element_type=jnp.float32
        )
        centre = jnp.sum(weights * pulled, 0, keepdims=True)
        score_grad = (weights * (pulled - centre)).astype(jnp.bfloat16)
        value_grad = jnp.dot(
            weights.astype(jnp.bfloat16), upstream, preferred_element_type=jnp.float32
        )
        key_grad = jnp.dot(score_grad, queries, preferred_element_type=jnp.float32)
        query_grad = lax.dot_general(
            key_rows, score_grad, (((0,), (0,)), ((), ())), preferred_element_type=jnp.float32
        )
        query_grad = query_grad.T * HEAD_DIM**-0.5
        grad_ref[0, :, at : at + HEAD_DIM] = query_grad.astype(jnp.bfloat16)
        grad_ref[0, :, GROUP + at : GROUP + at + HEAD_DIM] = key_grad.astype(jnp.bfloat16)
        grad_ref[0, :, 2 * GROUP + at : 2 * GROUP + at + HEAD_DIM] = value_grad.astype(
            jnp.bfloat16
        )


def attention_forward(projected):
    halves, rows, width = projected.shape
    groups = width // (3 * GROUP)
    return pl.pallas_call(
        attention_forward_kernel,
        grid=(halves, groups),
        in_specs=[pl.BlockSpec((1, rows, 3 * GROUP), lambda h, g: (h, 0, g))],
        out_specs=pl.BlockSpec((1, rows, GROUP), lambda h, g: (h, 0, g)),
        out_shape=jax.ShapeDtypeStruct((halves, rows, groups * GROUP), jnp.bfloat16),
        name="attention_forward",
    )(projected)


def attention_back(projected, upstream):
    halves, rows, width = projected.shape
    groups = width // (3 * GROUP)
    return pl.pallas_call(
        attention_back_kernel,
        grid=(halves, groups),
        in_specs=[
            pl.BlockSpec((1, rows, 3 * GROUP), lambda h, g: (h, 0, g)),
            pl.BlockSpec((1, rows, GROUP), lambda h, g: (h, 0, g)),
        ],
        out_specs=pl.BlockSpec((1, rows, 3 * GROUP), lambda h, g: (h, 0, g)),
        out_shape=jax.ShapeDtypeStruct(projected.shape, jnp.bfloat16),
        name="attention_back",
    )(projected, upstream)


MESH = pl.DeviceIdType.MESH
ANY = pl.BlockSpec(memory_space=pl.ANY)
IN_VMEM = pl.BlockSpec(memory_space=pltpu.VMEM)
SIDES = 2


def place():
    col = lax.axis_index("col")
    row = lax.axis_index("row")
    return col, lax.div(row, 4), lax.rem(lax.div(row, 2), 2), lax.rem(row, 2)


def device_of(x, z, y, core):
    return (z * 4 + y * 2 + core, x)


def greet(x, z, y, core, depth):
    barrier = pltpu.get_barrier_semaphore()
    others = [device_of(x, lax.rem(z + k, depth), y, core) for k in range(1, depth)]
    others += [
        device_of(x, z, 1 - y, core),
        device_of(1 - x, z, y, core),
        device_of(x, z, y, 1 - core),
    ]
    for other in others:
        pl.semaphore_signal(barrier, inc=1, device_id=other, device_id_type=MESH)
    pl.semaphore_wait(barrier, len(others))


def split_width(width):
    tiles = width // GROUP
    first = -(-tiles * 5 // 8)
    return first * GROUP


class Copies:
    def __init__(self, send_sems, recv_sems):
        self.send_sems, self.recv_sems, self.count, self.sent = send_sems, recv_sems, 0, []

    def slot(self):
        self.count += 1
        return self.count - 1

    def send(self, slot, source, target, device):
        copy = pltpu.make_async_remote_copy(
            src_ref=source,
            dst_ref=target,
            send_sem=self.send_sems.at[slot],
            recv_sem=self.recv_sems.at[slot],
            device_id=device,
            device_id_type=MESH,
        )
        copy.start()
        self.sent.append(copy)

    def arrived(self, slot, target, device):
        pltpu.make_async_remote_copy(
            src_ref=target,
            dst_ref=target,
            send_sem=self.send_sems.at[slot],
            recv_sem=self.recv_sems.at[slot],
            device_id=device,
            device_id_type=MESH,
        ).wait_recv()

    def finish(self):
        for copy in self.sent:
            copy.wait_send()


def run_waves(chains):
    stages = max(len(chain) for chain in chains)
    for wave in range(len(chains) + stages - 1):
        for stage in range(stages - 1, -1, -1):
            at = wave - stage
            if 0 <= at < len(chains) and stage < len(chains[at]):
                chains[at][stage]()


def gather_chain(copies, where, depth, block, whole, local):
    x, z, y, core = where
    width = block.shape[1]
    first = split_width(width)
    parts = (pl.ds(0, first), pl.ds(first, width - first))
    x_peer = device_of(1 - x, z, y, core)
    y_peer = device_of(x, z, 1 - y, core)
    partner = device_of(x, z, y, 1 - core)
    steps = range(1, depth)
    z_peers = [device_of(x, lax.rem(z + k, depth), y, core) for k in steps]
    z_from = [lax.rem(z + depth - k, depth) for k in steps]
    a, c = parts
    az, cz = [copies.slot() for _ in steps], [copies.slot() for _ in steps]
    ay, ax, cx, cy = [copies.slot() for _ in range(4)]
    shared = [copies.slot() for _ in range(5)]

    def share(slot, target):
        copies.send(slot, target, target, partner)

    def begin():
        mine = whole.at[x, z, y, core]
        for k in range(depth - 1):
            copies.send(az[k], block.at[:, a], mine.at[:, a], z_peers[k])
        copies.send(cx, block.at[:, c], mine.at[:, c], x_peer)

    def second():
        local.wait()
        for k in range(depth - 1):
            copies.arrived(az[k], whole.at[x, z_from[k], y, core, :, a], z_peers[k])
        column = whole.at[x, :, y, core, :, a]
        copies.send(ay, column, column, y_peer)
        copies.arrived(cx, whole.at[1 - x, z, y, core, :, c], x_peer)
        pair = whole.at[:, z, y, core, :, c]
        for k in range(depth - 1):
            copies.send(cz[k], pair, pair, z_peers[k])
        share(shared[0], column)

    def third():
        copies.arrived(ay, whole.at[x, :, 1 - y, core, :, a], y_peer)
        plane = whole.at[x, :, :, core, :, a]
        copies.send(ax, plane, plane, x_peer)
        for k in range(depth - 1):
            copies.arrived(cz[k], whole.at[:, z_from[k], y, core, :, c], z_peers[k])
        sheet = whole.at[:, :, y, core, :, c]
        copies.send(cy, sheet, sheet, y_peer)
        share(shared[1], whole.at[x, :, 1 - y, core, :, a])
        share(shared[2], sheet)

    def fourth():
        copies.arrived(ax, whole.at[1 - x, :, :, core, :, a], x_peer)
        share(shared[3], whole.at[1 - x, :, :, core, :, a])
        copies.arrived(cy, whole.at[:, :, 1 - y, core, :, c], y_peer)
        share(shared[4], whole.at[:, :, 1 - y, core, :, c])

    def last():
        other = 1 - core
        copies.arrived(shared[0], whole.at[x, :, y, other, :, a], partner)
        copies.arrived(shared[1], whole.at[x, :, 1 - y, other, :, a], partner)
        copies.arrived(shared[2], whole.at[:, :, y, other, :, c], partner)
        copies.arrived(shared[3], whole.at[1 - x, :, :, other, :, a], partner)
        copies.arrived(shared[4], whole.at[:, :, 1 - y, other, :, c], partner)

    return begin, (second, third, fourth, last)


def gather_kernel(depth, pieces_count, *refs):
    count = (len(refs) - 3 - 2 * pieces_count) // 2
    pieces, blocks = refs[:pieces_count], refs[pieces_count : pieces_count + count]
    outs = refs[pieces_count + count : -3]
    images, wholes = outs[:pieces_count], outs[pieces_count:]
    send_sems, recv_sems, own_sems = refs[-3:]
    where = place()
    x, z, y, core = where
    copies = Copies(send_sems, recv_sems)
    local = [
        pltpu.make_async_copy(block, whole.at[x, z, y, core], own_sems.at[at])
        for at, (block, whole) in enumerate(zip(blocks, wholes))
    ]
    kept = [
        pltpu.make_async_copy(piece.at[x], image.at[x], own_sems.at[count + at])
        for at, (piece, image) in enumerate(zip(pieces, images))
    ]
    for copy in local + kept:
        copy.start()
    greet(*where, depth)
    chains = [
        gather_chain(copies, where, depth, *item) for item in zip(blocks, wholes, local)
    ]
    x_peer = device_of(1 - x, z, y, core)
    slots = [copies.slot() for _ in pieces]
    for at in range(pieces_count):
        if at == 0:
            copies.send(slots[at], pieces[at].at[1 - x], images[at].at[x], x_peer)
    for begin, _ in chains:
        begin()
    for at in range(1, pieces_count):
        copies.send(slots[at], pieces[at].at[1 - x], images[at].at[x], x_peer)
    run_waves([rest for _, rest in chains])
    for at in range(pieces_count):
        copies.arrived(slots[at], images[at].at[1 - x], x_peer)
        kept[at].wait()
    copies.finish()


def gather_weights(pieces, blocks, depth):
    copies = (2 * (depth - 1) + 9) * len(blocks) + len(pieces)
    return pl.pallas_call(
        functools.partial(gather_kernel, depth, len(pieces)),
        in_specs=[IN_VMEM] * (len(pieces) + len(blocks)),
        out_specs=[ANY] * (len(pieces) + len(blocks)),
        out_shape=[jax.ShapeDtypeStruct(piece.shape, piece.dtype) for piece in pieces]
        + [
            jax.ShapeDtypeStruct((SIDES, depth, 2, 2) + block.shape, block.dtype)
            for block in blocks
        ],
        scratch_shapes=[
            pltpu.SemaphoreType.DMA((copies,)),
            pltpu.SemaphoreType.DMA((copies,)),
            pltpu.SemaphoreType.DMA((len(pieces) + len(blocks),)),
        ],
        compiler_params=pltpu.CompilerParams(collective_id=1, has_side_effects=True),
        name="gather_weights",
    )(*pieces, *blocks)


def add_blocks(count, target, term):
    @pl.loop(0, count)
    def _(at):
        total = target(at)[...].astype(jnp.float32) + term(at)[...].astype(jnp.float32)
        target(at)[...] = total.astype(jnp.bfloat16)


def scatter_chain(copies, where, depth, grad, total, buffers, load):
    x, z, y, core = where
    own, halves, ax_in, ay_in, az_in, cy_in, cz_in, c_sum, cx_in = buffers
    width = total.shape[1]
    first = split_width(width)
    a, c = pl.ds(0, first), pl.ds(first, width - first)
    x_peer = device_of(1 - x, z, y, core)
    y_peer = device_of(x, z, 1 - y, core)
    partner = device_of(x, z, y, 1 - core)
    steps = range(1, depth)
    z_to = [lax.rem(z + k, depth) for k in steps]
    z_peers = [device_of(x, at, y, core) for at in z_to]
    az, cz = [copies.slot() for _ in steps], [copies.slot() for _ in steps]
    pair = [copies.slot() for _ in range(SIDES)]
    ax, ay, cy, cx = [copies.slot() for _ in range(4)]

    def begin():
        for copy in load:
            copy.start()
        for side in range(SIDES):
            copies.send(
                pair[side], grad[side].at[:, :, 1 - core], halves.at[side], partner
            )

    def second():
        for side in range(SIDES):
            load[side].wait()
            copies.arrived(pair[side], halves.at[side], partner)

        def at_block(ref, at):
            return ref.at[lax.div(at, depth * 2), lax.rem(lax.div(at, 2), depth), lax.rem(at, 2)]

        add_blocks(
            SIDES * depth * 2, lambda at: at_block(halves, at), lambda at: at_block(own, at)
        )
        copies.send(ax, halves.at[1 - x, :, :, :, a], ax_in, x_peer)
        copies.send(cy, halves.at[:, :, 1 - y, :, c], cy_in, y_peer)

    def third():
        copies.arrived(ax, ax_in, x_peer)
        add_blocks(
            depth * 2,
            lambda at: ax_in.at[lax.div(at, 2), lax.rem(at, 2)],
            lambda at: halves.at[x, lax.div(at, 2), lax.rem(at, 2), :, a],
        )
        copies.send(ay, ax_in.at[:, 1 - y], ay_in, y_peer)
        copies.arrived(cy, cy_in, y_peer)
        add_blocks(
            SIDES * depth,
            lambda at: cy_in.at[lax.div(at, depth), lax.rem(at, depth)],
            lambda at: halves.at[lax.div(at, depth), lax.rem(at, depth), y, :, c],
        )
        for k in range(depth - 1):
            copies.send(cz[k], cy_in.at[:, z_to[k]], cz_in.at[k], z_peers[k])

    def fourth():
        copies.arrived(ay, ay_in, y_peer)
        add_blocks(depth, lambda at: ay_in.at[at], lambda at: ax_in.at[at, y])
        for k in range(depth - 1):
            copies.send(az[k], ay_in.at[z_to[k]], az_in.at[k], z_peers[k])
        for k in range(depth - 1):
            copies.arrived(cz[k], cz_in.at[k], z_peers[k])

        @pl.loop(0, SIDES)
        def _(at):
            sums = cy_in[at, z].astype(jnp.float32)
            for k in range(depth - 1):
                sums += cz_in[k, at].astype(jnp.float32)
            c_sum[at] = sums.astype(jnp.bfloat16)

        copies.send(cx, c_sum.at[1 - x], cx_in, x_peer)

    def last():
        for k in range(depth - 1):
            copies.arrived(az[k], az_in.at[k], z_peers[k])
        sums = ay_in[z].astype(jnp.float32)
        for k in range(depth - 1):
            sums += az_in[k].astype(jnp.float32)
        total[:, :first] = sums
        copies.arrived(cx, cx_in, x_peer)
        total[:, first:] = c_sum[x].astype(jnp.float32) + cx_in[...].astype(jnp.float32)

    return begin, (second, third, fourth, last)


def scatter_kernel(depth, count, wholes_count, *refs):
    grads = [refs[SIDES * at : SIDES * at + SIDES] for at in range(count)]
    refs = refs[SIDES * count :]
    wholes, refs = refs[:wholes_count], refs[wholes_count:]
    totals, pieces = refs[:count], refs[count : count + wholes_count]
    refs = refs[count + wholes_count :]
    send_sems, recv_sems, own_sems = refs[-3:]
    where = place()
    x, z, y, core = where
    copies = Copies(send_sems, recv_sems)
    greet(*where, depth)
    x_peer = device_of(1 - x, z, y, core)
    kept = []
    slots = [copies.slot() for _ in wholes]
    for at in range(wholes_count):
        width = pieces[at].shape[2]
        mine = pl.ds(pl.multiple_of(x * width, width), width)
        theirs = pl.ds(pl.multiple_of((1 - x) * width, width), width)
        copy = pltpu.make_async_copy(
            wholes[at].at[:, mine], pieces[at].at[x], own_sems.at[SIDES * count + at]
        )
        copy.start()
        kept.append(copy)
        copies.send(slots[at], wholes[at].at[:, theirs], pieces[at].at[x], x_peer)
    chains = []
    for at in range(count):
        buffers = refs[9 * at : 9 * at + 9]
        load = [
            pltpu.make_async_copy(
                grads[at][side].at[:, :, core], buffers[0].at[side], own_sems.at[SIDES * at + side]
            )
            for side in range(SIDES)
        ]
        chains.append(
            scatter_chain(copies, where, depth, grads[at], totals[at], buffers, load)
        )
    for begin, _ in chains:
        begin()
    run_waves([rest for _, rest in chains])
    for at in range(wholes_count):
        copies.arrived(slots[at], pieces[at].at[1 - x], x_peer)
        kept[at].wait()
    copies.finish()


def scatter_buffers(depth, rows, width):
    first = split_width(width)
    rest = width - first
    shapes = [
        (SIDES, depth, 2, rows, width),
        (SIDES, depth, 2, rows, width),
        (depth, 2, rows, first),
        (depth, rows, first),
        (depth - 1, rows, first),
        (SIDES, depth, rows, rest),
        (depth - 1, SIDES, rows, rest),
        (SIDES, rows, rest),
        (rows, rest),
    ]
    return [pltpu.VMEM(shape, jnp.bfloat16) for shape in shapes]


def scatter_grads(grads, wholes, depth):
    copies = (2 * (depth - 1) + 6) * len(grads) + len(wholes)
    scratch = []
    for grad in grads:
        scratch += scatter_buffers(depth, grad[0].shape[3], grad[0].shape[4])
    return pl.pallas_call(
        functools.partial(scatter_kernel, depth, len(grads), len(wholes)),
        in_specs=[ANY] * SIDES * len(grads) + [IN_VMEM] * len(wholes),
        out_specs=[IN_VMEM] * len(grads) + [ANY] * len(wholes),
        out_shape=[jax.ShapeDtypeStruct(grad[0].shape[3:], jnp.float32) for grad in grads]
        + [
            jax.ShapeDtypeStruct((SIDES, whole.shape[0], whole.shape[1] // SIDES), whole.dtype)
            for whole in wholes
        ],
        scratch_shapes=scratch
        + [
            pltpu.SemaphoreType.DMA((copies,)),
            pltpu.SemaphoreType.DMA((copies,)),
            pltpu.SemaphoreType.DMA((SIDES * len(grads) + len(wholes),)),
        ],
        compiler_params=pltpu.CompilerParams(
            collective_id=2, has_side_effects=True, vmem_limit_bytes=60 * 2**20
        ),
        name="scatter_grads",
    )(*[half for grad in grads for half in grad], *wholes)


def product(left, right, left_at, right_at):
    return lax.dot_general(
        left, right, (((left_at,), (right_at,)), ((), ())), preferred_element_type=jnp.float32
    )


def norm_back(upstream, scaled, inverse, gain_row):
    scaled_grad = upstream * gain_row
    first_mean = jnp.mean(scaled_grad, -1, keepdims=True)
    second_mean = jnp.mean(scaled_grad * scaled, -1, keepdims=True)
    return inverse * (scaled_grad - first_mean - scaled * second_mean)


def group_order(block):
    rows = block.shape[0]
    return block.reshape(rows, 3, -1, GROUP).transpose(0, 2, 1, 3).reshape(rows, -1)


def part_order(block):
    rows = block.shape[0]
    return block.reshape(rows, -1, 3, GROUP).transpose(0, 2, 1, 3).reshape(rows, 3, -1)


def image_shards(
    tokens,
    first_gain,
    first_shift,
    mixer_weight,
    mixer_bias,
    merge_weight,
    merge_bias,
    second_gain,
    second_shift,
    expand_weight,
    expand_bias,
    reduce_weight,
    reduce_bias,
    cotangent,
):
    low = jnp.bfloat16
    cols = lax.axis_size("col")
    rows = lax.axis_size("row")
    piece = first_gain.shape[0]
    hidden_piece = expand_bias.shape[0]
    block_rows = mixer_weight.shape[0]
    vectors = jnp.concatenate(
        [
            jnp.stack(
                [
                    first_gain,
                    first_shift,
                    mixer_bias[0],
                    mixer_bias[1],
                    merge_bias,
                    second_gain,
                    second_shift,
                    reduce_bias,
                ]
            ).reshape(-1),
            expand_bias,
        ]
    ).astype(low)
    vector_rows = vectors.shape[0] // GROUP
    vector_block = jnp.pad(
        vectors.reshape(vector_rows, GROUP), ((0, block_rows - vector_rows), (0, 0))
    )
    mixer_width = 3 * mixer_weight.shape[2]
    first_block = jnp.concatenate([group_order(mixer_weight).astype(low), vector_block], 1)
    depth = rows // 4
    sides = (cols, tokens.shape[0] // cols, tokens.shape[1])
    image, upstream_low, mixed, merger, expander, reducer = gather_weights(
        [tokens.reshape(sides), cotangent.reshape(sides)],
        [
            first_block,
            merge_weight.astype(low).T,
            expand_weight.astype(low),
            reduce_weight.astype(low).T,
        ],
        depth,
    )
    image = jnp.concatenate([image[h] for h in range(cols)], 1)
    upstream_low = jnp.concatenate([upstream_low[h] for h in range(cols)], 1)
    mixed, merger, expander, reducer = [
        whole.reshape(cols, rows * block_rows, whole.shape[-1])
        for whole in (mixed, merger, expander, reducer)
    ]
    mixer = mixed[:, :, :mixer_width]
    spread = mixed[:, :, mixer_width:].reshape(cols, rows, block_rows, GROUP)[:, :, :vector_rows]
    spread = spread.reshape(cols, rows, -1).astype(jnp.float32).transpose(1, 0, 2)
    rows_of = spread[:, :, : 8 * piece].reshape(rows, cols, 8, piece).transpose(2, 0, 1, 3)
    rows_of = rows_of.reshape(8, -1)
    expand_shift = spread[:, :, 8 * piece :].reshape(cols, -1)
    first_gain_row, first_shift_row = rows_of[0], rows_of[1]
    query_bias, value_bias, merge_shift = rows_of[2], rows_of[3], rows_of[4]
    second_gain_row, second_shift_row, reduce_shift = rows_of[5], rows_of[6], rows_of[7]
    mixer_shift = jnp.stack(
        [
            query_bias.reshape(cols, -1, GROUP),
            jnp.zeros_like(query_bias).reshape(cols, -1, GROUP),
            value_bias.reshape(cols, -1, GROUP),
        ],
        2,
    ).reshape(cols, -1)

    inputs = image.astype(jnp.float32)
    first_scaled, first_inverse, first_normed = normalize(inputs, first_gain_row, first_shift_row)
    first_low = first_normed.astype(low)
    projected = jnp.stack(
        [(product(first_low, mixer[h], 1, 0) + mixer_shift[h]).astype(low) for h in range(cols)]
    )
    attended = attention_forward(projected)
    merged = sum(product(attended[h], merger[h], 1, 1) for h in range(cols))
    hidden = inputs + merged + merge_shift
    second_scaled, second_inverse, second_normed = normalize(
        hidden, second_gain_row, second_shift_row
    )
    second_low = second_normed.astype(low)
    expanded = [product(second_low, expander[h], 1, 0) + expand_shift[h] for h in range(cols)]
    activated = [quick_gelu(part).astype(low) for part in expanded]
    reduced = sum(product(activated[h], reducer[h], 1, 1) for h in range(cols))
    image_output = (hidden + reduced + reduce_shift).astype(low)

    upstream = upstream_low.astype(jnp.float32)
    reducer_grad = [product(upstream_low, activated[h], 0, 0).astype(low) for h in range(cols)]
    expanded_grad = [
        (product(upstream_low, reducer[h], 1, 0) * gelu_slope(expanded[h])).astype(low)
        for h in range(cols)
    ]
    expander_grad = [product(second_low, expanded_grad[h], 0, 0).astype(low) for h in range(cols)]
    expand_shift_grad = [jnp.sum(part.astype(jnp.float32), 0) for part in expanded_grad]
    second_grad = sum(product(expanded_grad[h], expander[h], 1, 1) for h in range(cols))
    hidden_grad = upstream + norm_back(
        second_grad, second_scaled, second_inverse, second_gain_row
    )
    hidden_low = hidden_grad.astype(low)
    merger_grad = [product(hidden_low, attended[h], 0, 0).astype(low) for h in range(cols)]
    attended_grad = jnp.stack(
        [product(hidden_low, merger[h], 1, 0).astype(low) for h in range(cols)]
    )
    projected_grad = attention_back(projected, attended_grad)
    mixer_grad = [product(first_low, projected_grad[h], 0, 0).astype(low) for h in range(cols)]
    bias_sums = jnp.sum(projected_grad.astype(jnp.float32), 1)
    bias_sums = bias_sums.reshape(cols, -1, 3, GROUP).transpose(2, 0, 1, 3).reshape(3, -1)
    first_grad = sum(product(projected_grad[h], mixer[h], 1, 1) for h in range(cols))
    input_grad = hidden_grad + norm_back(first_grad, first_scaled, first_inverse, first_gain_row)
    vector_grads = jnp.stack(
        [
            jnp.sum(first_grad * first_scaled, 0),
            jnp.sum(first_grad, 0),
            bias_sums[0],
            bias_sums[2],
            jnp.sum(hidden_grad, 0),
            jnp.sum(second_grad * second_scaled, 0),
            jnp.sum(second_grad, 0),
            jnp.sum(upstream, 0),
        ]
    )
    vector_grads = vector_grads.reshape(8, rows, cols, piece).transpose(2, 1, 0, 3)
    hidden_grads = jnp.concatenate(expand_shift_grad).reshape(rows, cols, hidden_piece)
    vector_grads = jnp.concatenate(
        [vector_grads.reshape(cols, rows, -1), hidden_grads.transpose(1, 0, 2)], 2
    )
    vector_grads = vector_grads.reshape(cols, rows, vector_rows, GROUP).astype(low)
    vector_grads = jnp.pad(
        vector_grads, ((0, 0), (0, 0), (0, block_rows - vector_rows), (0, 0))
    ).reshape(cols, rows * block_rows, GROUP)
    mixed_grad = [jnp.concatenate([mixer_grad[h], vector_grads[h]], 1) for h in range(cols)]
    grads = [
        [part.reshape(depth, 2, 2, block_rows, -1) for part in halves]
        for halves in (reducer_grad, expander_grad, merger_grad, mixed_grad)
    ]
    reduce_total, expand_total, merge_total, mixed_total, layer_output, tokens_gradient = (
        scatter_grads(grads, [image_output, input_grad.astype(low)], depth)
    )
    layer_output = layer_output.reshape(tokens.shape)
    tokens_gradient = tokens_gradient.reshape(tokens.shape).astype(jnp.float32)
    mixer_total = part_order(mixed_total[:, :mixer_width])
    vector_total = mixed_total[:vector_rows, mixer_width:].reshape(-1)
    small = vector_total[: 8 * piece].reshape(8, piece)
    return (
        layer_output,
        tokens_gradient,
        small[0],
        small[1],
        mixer_total,
        small[2:4],
        merge_total.T,
        small[4],
        small[5],
        small[6],
        expand_total,
        vector_total[8 * piece :],
        reduce_total.T,
        small[7],
    )


def solution(mesh):
    def body(*arguments):
        images = arguments[0].shape[0] // SEQ
        whole = images == 2 and lax.axis_size("col") == 2
        return (image_shards if whole else split_shards)(*arguments)

    return jax.shard_map(
        body,
        mesh=mesh,
        in_specs=(
            P("row", "col"),
            P(("row", "col")),
            P(("row", "col")),
            P("row", None, "col"),
            P(None, ("row", "col")),
            P("col", "row"),
            P(("row", "col")),
            P(("row", "col")),
            P(("row", "col")),
            P("row", "col"),
            P(("row", "col")),
            P("col", "row"),
            P(("row", "col")),
            P("row", "col"),
        ),
        out_specs=(
            P("row", "col"),
            P("row", "col"),
            P(("row", "col")),
            P(("row", "col")),
            P("row", None, "col"),
            P(None, ("row", "col")),
            P("col", "row"),
            P(("row", "col")),
            P(("row", "col")),
            P(("row", "col")),
            P("row", "col"),
            P(("row", "col")),
            P("col", "row"),
            P(("row", "col")),
        ),
        check_vma=False,
    )
```

```python
import functools

import jax
import jax.numpy as jnp
from jax import lax
from jax.experimental import pallas as pl
from jax.experimental.pallas import tpu as pltpu
from jax.sharding import PartitionSpec as P

HEAD_DIM = 64
SEQ = 577


EPSILON = 1e-05
SLOPE = 1.702


def quick_gelu(inputs):
    return inputs * jax.nn.sigmoid(SLOPE * inputs)


def gelu_slope(inputs):
    sigmoid_value = jax.nn.sigmoid(SLOPE * inputs)
    return sigmoid_value + SLOPE * inputs * sigmoid_value * (1.0 - sigmoid_value)


def own_columns(values, start, width):
    return lax.dynamic_slice_in_dim(values, start, width, values.ndim - 1)


def normalize(values, gain_row, shift_row):
    feature_count = values.shape[-1]
    row_mean = jnp.sum(values, -1, keepdims=True) / feature_count
    square = jnp.sum(values * values, -1, keepdims=True) / feature_count
    inverse = lax.rsqrt(square - row_mean * row_mean + EPSILON)
    scaled = (values - row_mean) * inverse
    return (scaled, inverse, scaled * gain_row + shift_row)


def column_sum(partial_value):
    return lax.psum_scatter(
        partial_value.astype(jnp.bfloat16), "col", scatter_dimension=1, tiled=True
    ).astype(jnp.float32)


def feature_totals(first_sum, second_sum):
    return lax.psum((first_sum, second_sum), "col")


def normed_gather(piece):
    return lax.all_gather(piece, "col", axis=1, tiled=True)


def shared_back(upstream, scaled, inverse, gain_row, feature_count):
    scaled_grad = upstream * gain_row
    totals = feature_totals(jnp.sum(scaled_grad, -1), jnp.sum(scaled_grad * scaled, -1))
    first_mean = totals[0][:, None] / feature_count
    second_mean = totals[1][:, None] / feature_count
    return inverse * (scaled_grad - first_mean - scaled * second_mean)


def fetch_weights(masters):
    return (
        lax.all_gather(masters[0], "row", axis=0, tiled=True),
        lax.all_gather(masters[1], "row", axis=1, tiled=True),
        lax.all_gather(masters[2], "row", axis=0, tiled=True),
        lax.all_gather(masters[3], "row", axis=1, tiled=True),
    )


def attend_forward(parts):
    queries, key_rows, values = parts
    score_scale = queries.shape[-1] ** (-0.5)
    scores = (
        jnp.einsum("qhd,khd->hqk", queries, key_rows, preferred_element_type=jnp.float32)
        * score_scale
    )
    score_top = jnp.max(scores, -1, keepdims=True)
    exponent = jnp.exp(scores - score_top)
    row_total = jnp.sum(exponent, -1, keepdims=True)
    weights = (exponent / row_total).astype(jnp.bfloat16)
    mixture = jnp.einsum("hqk,khd->qhd", weights, values, preferred_element_type=jnp.float32)
    return (mixture.astype(jnp.bfloat16), (score_top + jnp.log(row_total))[..., 0])


def attend_back(parts):
    queries, key_rows, values, log_total, upstream = parts
    score_scale = queries.shape[-1] ** (-0.5)
    scores = (
        jnp.einsum("qhd,khd->hqk", queries, key_rows, preferred_element_type=jnp.float32)
        * score_scale
    )
    probability = jnp.exp(scores - log_total[..., None])
    rounded = probability.astype(jnp.bfloat16)
    pulled = jnp.einsum("qhd,khd->hqk", upstream, values, preferred_element_type=jnp.float32)
    centre = jnp.sum(probability * pulled, -1, keepdims=True)
    score_grad = (probability * (pulled - centre)).astype(jnp.bfloat16)
    query_grad = (
        jnp.einsum("hqk,khd->qhd", score_grad, key_rows, preferred_element_type=jnp.float32)
        * score_scale
    )
    key_grad = (
        jnp.einsum("hqk,qhd->khd", score_grad, queries, preferred_element_type=jnp.float32)
        * score_scale
    )
    value_grad = jnp.einsum("hqk,qhd->khd", rounded, upstream, preferred_element_type=jnp.float32)
    return (query_grad, key_grad, value_grad)


def split_shards(
    tokens,
    first_gain,
    first_shift,
    mixer_weight,
    mixer_bias,
    merge_weight,
    merge_bias,
    second_gain,
    second_shift,
    expand_weight,
    expand_bias,
    reduce_weight,
    reduce_bias,
    cotangent,
):
    col_index = lax.axis_index("col")
    piece_width = tokens.shape[1]
    hidden_width = expand_weight.shape[1]
    start = col_index * piece_width
    hidden_start = col_index * hidden_width
    vector_pieces = jnp.stack(
        [
            first_gain,
            first_shift,
            mixer_bias[0],
            mixer_bias[1],
            merge_bias,
            second_gain,
            second_shift,
            reduce_bias,
        ]
    ).astype(jnp.bfloat16)
    vectors_low, expand_shift_low = (
        lax.all_gather(vector_pieces, ("row", "col"), axis=1, tiled=True),
        lax.all_gather(expand_bias.astype(jnp.bfloat16), ("row", "col"), axis=0, tiled=True),
    )
    vectors = vectors_low.astype(jnp.float32)
    feature_count = vectors.shape[1]
    first_gain_row, first_shift_row = (vectors[0], vectors[1])
    query_bias = own_columns(vectors[2], start, piece_width)
    value_bias = own_columns(vectors[3], start, piece_width)
    merge_shift = vectors[4]
    second_gain_row, second_shift_row = (vectors[5], vectors[6])
    reduce_shift = own_columns(vectors[7], start, piece_width)
    expand_shift = own_columns(expand_shift_low.astype(jnp.float32), hidden_start, hidden_width)
    masters = (
        mixer_weight.astype(jnp.bfloat16),
        merge_weight.astype(jnp.bfloat16),
        expand_weight.astype(jnp.bfloat16),
        reduce_weight.astype(jnp.bfloat16),
    )
    mixer_local, merger, expander, reducer = fetch_weights(masters)
    inputs_whole, upstream_whole = (
        lax.all_gather(tokens, "col", axis=1, tiled=True),
        lax.all_gather(cotangent, "col", axis=1, tiled=True),
    )
    inputs = inputs_whole.astype(jnp.float32)
    row_count = inputs.shape[0]
    first_scaled, first_inverse, first_normed = normalize(inputs, first_gain_row, first_shift_row)
    first_low = first_normed.astype(jnp.bfloat16)
    projected = jnp.einsum(
        "rd,dtc->rtc", first_low, mixer_local, preferred_element_type=jnp.float32
    )
    projected = projected + jnp.stack([query_bias, jnp.zeros_like(query_bias), value_bias])
    projected_low = projected.astype(jnp.bfloat16)
    head_shape = (row_count // SEQ, SEQ, piece_width // HEAD_DIM, HEAD_DIM)
    queries = projected_low[:, 0].reshape(head_shape)
    key_rows = projected_low[:, 1].reshape(head_shape)
    values = projected_low[:, 2].reshape(head_shape)
    attended, log_total = lax.map(attend_forward, (queries, key_rows, values))
    attended = attended.reshape(row_count, piece_width)
    merged_part = jnp.dot(attended, merger, preferred_element_type=jnp.float32)
    hidden_own = (
        own_columns(inputs, start, piece_width)
        + column_sum(merged_part)
        + own_columns(merge_shift, start, piece_width)
    )
    totals = feature_totals(jnp.sum(hidden_own, -1), jnp.sum(hidden_own * hidden_own, -1))
    row_mean = totals[0][:, None] / feature_count
    square = totals[1][:, None] / feature_count
    second_inverse = lax.rsqrt(square - row_mean * row_mean + EPSILON)
    second_scaled = (hidden_own - row_mean) * second_inverse
    second_gain_own = own_columns(second_gain_row, start, piece_width)
    second_piece = second_scaled * second_gain_own + own_columns(
        second_shift_row, start, piece_width
    )
    second_low = normed_gather(second_piece.astype(jnp.bfloat16))
    expanded = jnp.dot(second_low, expander, preferred_element_type=jnp.float32) + expand_shift
    activated = quick_gelu(expanded).astype(jnp.bfloat16)
    reduced = column_sum(jnp.dot(activated, reducer, preferred_element_type=jnp.float32))
    layer_output = (hidden_own + reduced + reduce_shift).astype(jnp.bfloat16)
    masters_again = lax.optimization_barrier((masters, layer_output))[0]
    mixer_local, merger, expander, reducer = fetch_weights(masters_again)
    upstream_own = cotangent.astype(jnp.float32)
    reducer_grad = jnp.einsum(
        "rf,rd->fd", activated, upstream_whole, preferred_element_type=jnp.float32
    )
    activated_grad = jnp.einsum(
        "rd,fd->rf", upstream_whole, reducer, preferred_element_type=jnp.float32
    )
    expanded_grad = (activated_grad * gelu_slope(expanded)).astype(jnp.bfloat16)
    expander_grad = jnp.einsum(
        "rd,rf->df", second_low, expanded_grad, preferred_element_type=jnp.float32
    )
    expand_shift_grad = jnp.sum(expanded_grad.astype(jnp.float32), 0)
    second_part = jnp.einsum(
        "rf,df->rd", expanded_grad, expander, preferred_element_type=jnp.float32
    )
    second_grad = column_sum(second_part)
    hidden_part = shared_back(
        second_grad, second_scaled, second_inverse, second_gain_own, feature_count
    )
    hidden_grad = upstream_own + hidden_part
    second_gain_grad = jnp.sum(second_grad * second_scaled, 0)
    second_shift_grad = jnp.sum(second_grad, 0)
    hidden_low = normed_gather(hidden_grad.astype(jnp.bfloat16))
    merger_grad = jnp.einsum("rc,rd->cd", attended, hidden_low, preferred_element_type=jnp.float32)
    attended_grad = jnp.einsum(
        "rd,cd->rc", hidden_low, merger, preferred_element_type=jnp.float32
    ).astype(jnp.bfloat16)
    query_grad, key_grad, value_grad = lax.map(
        attend_back, (queries, key_rows, values, log_total, attended_grad.reshape(head_shape))
    )
    projected_grad = jnp.stack(
        [
            query_grad.reshape(row_count, piece_width),
            key_grad.reshape(row_count, piece_width),
            value_grad.reshape(row_count, piece_width),
        ],
        1,
    ).astype(jnp.bfloat16)
    mixer_grad = jnp.einsum(
        "rd,rtc->dtc", first_low, projected_grad, preferred_element_type=jnp.float32
    )
    bias_sums = jnp.sum(projected_grad.astype(jnp.float32), 0)
    first_part = jnp.einsum(
        "rtc,dtc->rd", projected_grad, mixer_local, preferred_element_type=jnp.float32
    )
    first_grad = column_sum(first_part)
    first_scaled_own = own_columns(first_scaled, start, piece_width)
    input_part = shared_back(
        first_grad,
        first_scaled_own,
        first_inverse,
        own_columns(first_gain_row, start, piece_width),
        feature_count,
    )
    tokens_gradient = hidden_grad + input_part
    own_vector_grads = jnp.stack(
        [
            jnp.sum(first_grad * first_scaled_own, 0),
            jnp.sum(first_grad, 0),
            bias_sums[0],
            bias_sums[2],
            jnp.sum(hidden_grad, 0),
            second_gain_grad,
            second_shift_grad,
            jnp.sum(upstream_own, 0),
        ]
    )
    vector_whole = lax.dynamic_update_slice(
        jnp.zeros((8, feature_count), jnp.float32), own_vector_grads, (jnp.int32(0), start)
    )
    expand_whole = lax.dynamic_update_slice(
        jnp.zeros((hidden_width * lax.axis_size("col"),), jnp.float32),
        expand_shift_grad,
        (hidden_start,),
    )
    vector_total, expand_bias_total = (
        lax.psum_scatter(vector_whole, ("row", "col"), scatter_dimension=1, tiled=True),
        lax.psum_scatter(expand_whole, ("row", "col"), scatter_dimension=0, tiled=True),
    )
    mixer_total, merge_total, expand_total, reduce_total = (
        lax.psum_scatter(
            mixer_grad.astype(jnp.bfloat16), "row", scatter_dimension=0, tiled=True
        ).astype(jnp.float32),
        lax.psum_scatter(
            merger_grad.astype(jnp.bfloat16), "row", scatter_dimension=1, tiled=True
        ).astype(jnp.float32),
        lax.psum_scatter(
            expander_grad.astype(jnp.bfloat16), "row", scatter_dimension=0, tiled=True
        ).astype(jnp.float32),
        lax.psum_scatter(
            reducer_grad.astype(jnp.bfloat16), "row", scatter_dimension=1, tiled=True
        ).astype(jnp.float32),
    )
    return (
        layer_output,
        tokens_gradient,
        vector_total[0],
        vector_total[1],
        mixer_total,
        jnp.stack([vector_total[2], vector_total[3]]),
        merge_total,
        vector_total[4],
        vector_total[5],
        vector_total[6],
        expand_total,
        expand_bias_total,
        reduce_total,
        vector_total[7],
    )


GROUP = 128


def attention_forward_kernel(projected_ref, attended_ref):
    for head in range(GROUP // HEAD_DIM):
        at = head * HEAD_DIM
        queries = projected_ref[0, :, at : at + HEAD_DIM] * jnp.bfloat16(HEAD_DIM**-0.5)
        key_rows = projected_ref[0, :, GROUP + at : GROUP + at + HEAD_DIM]
        values = projected_ref[0, :, 2 * GROUP + at : 2 * GROUP + at + HEAD_DIM]
        scores = lax.dot_general(
            key_rows, queries, (((1,), (1,)), ((), ())), preferred_element_type=jnp.float32
        )
        exponent = jnp.exp(scores - jnp.max(scores, 0, keepdims=True))
        weights = exponent * (1.0 / jnp.sum(exponent, 0, keepdims=True))
        mixture = lax.dot_general(
            values,
            weights.astype(jnp.bfloat16),
            (((0,), (0,)), ((), ())),
            preferred_element_type=jnp.float32,
        )
        attended_ref[0, :, at : at + HEAD_DIM] = mixture.T.astype(jnp.bfloat16)


def attention_back_kernel(projected_ref, upstream_ref, grad_ref):
    for head in range(GROUP // HEAD_DIM):
        at = head * HEAD_DIM
        queries = projected_ref[0, :, at : at + HEAD_DIM] * jnp.bfloat16(HEAD_DIM**-0.5)
        key_rows = projected_ref[0, :, GROUP + at : GROUP + at + HEAD_DIM]
        values = projected_ref[0, :, 2 * GROUP + at : 2 * GROUP + at + HEAD_DIM]
        upstream = upstream_ref[0, :, at : at + HEAD_DIM]
        scores = lax.dot_general(
            key_rows, queries, (((1,), (1,)), ((), ())), preferred_element_type=jnp.float32
        )
        exponent = jnp.exp(scores - jnp.max(scores, 0, keepdims=True))
        weights = exponent * (1.0 / jnp.sum(exponent, 0, keepdims=True))
        pulled = lax.dot_general(
            values, upstream, (((1,), (1,)), ((), ())), preferred_element_type=jnp.float32
        )
        centre = jnp.sum(weights * pulled, 0, keepdims=True)
        score_grad = (weights * (pulled - centre)).astype(jnp.bfloat16)
        value_grad = jnp.dot(
            weights.astype(jnp.bfloat16), upstream, preferred_element_type=jnp.float32
        )
        key_grad = jnp.dot(score_grad, queries, preferred_element_type=jnp.float32)
        query_grad = lax.dot_general(
            key_rows, score_grad, (((0,), (0,)), ((), ())), preferred_element_type=jnp.float32
        )
        query_grad = query_grad.T * HEAD_DIM**-0.5
        grad_ref[0, :, at : at + HEAD_DIM] = query_grad.astype(jnp.bfloat16)
        grad_ref[0, :, GROUP + at : GROUP + at + HEAD_DIM] = key_grad.astype(jnp.bfloat16)
        grad_ref[0, :, 2 * GROUP + at : 2 * GROUP + at + HEAD_DIM] = value_grad.astype(
            jnp.bfloat16
        )


def attention_forward(projected):
    halves, rows, width = projected.shape
    groups = width // (3 * GROUP)
    return pl.pallas_call(
        attention_forward_kernel,
        grid=(halves, groups),
        in_specs=[pl.BlockSpec((1, rows, 3 * GROUP), lambda h, g: (h, 0, g))],
        out_specs=pl.BlockSpec((1, rows, GROUP), lambda h, g: (h, 0, g)),
        out_shape=jax.ShapeDtypeStruct((halves, rows, groups * GROUP), jnp.bfloat16),
        name="attention_forward",
    )(projected)


def attention_back(projected, upstream):
    halves, rows, width = projected.shape
    groups = width // (3 * GROUP)
    return pl.pallas_call(
        attention_back_kernel,
        grid=(halves, groups),
        in_specs=[
            pl.BlockSpec((1, rows, 3 * GROUP), lambda h, g: (h, 0, g)),
            pl.BlockSpec((1, rows, GROUP), lambda h, g: (h, 0, g)),
        ],
        out_specs=pl.BlockSpec((1, rows, 3 * GROUP), lambda h, g: (h, 0, g)),
        out_shape=jax.ShapeDtypeStruct(projected.shape, jnp.bfloat16),
        name="attention_back",
    )(projected, upstream)


MESH = pl.DeviceIdType.MESH
ANY = pl.BlockSpec(memory_space=pl.ANY)
IN_VMEM = pl.BlockSpec(memory_space=pltpu.VMEM)
SIDES = 2
BUFFERS = 6
CHUNK = 4
AHEAD = 12
SPACING = 2


def place():
    col = lax.axis_index("col")
    row = lax.axis_index("row")
    return col, lax.div(row, 4), lax.rem(lax.div(row, 2), 2), lax.rem(row, 2)


def device_of(x, z, y, core):
    return (z * 4 + y * 2 + core, x)


def greet(x, z, y, core, depth):
    barrier = pltpu.get_barrier_semaphore()
    others = [device_of(x, lax.rem(z + k, depth), y, core) for k in range(1, depth)]
    others += [
        device_of(x, z, 1 - y, core),
        device_of(1 - x, z, y, core),
        device_of(x, z, y, 1 - core),
    ]
    for other in others:
        pl.semaphore_signal(barrier, inc=1, device_id=other, device_id_type=MESH)
    pl.semaphore_wait(barrier, len(others))


def split_width(width):
    return width // GROUP // 2 * GROUP


def chunks_of(width):
    tiles = width // GROUP
    count = max(tiles // CHUNK, 1)
    edges = [CHUNK * GROUP * at for at in range(count)] + [width]
    return [(edges[at], edges[at + 1] - edges[at]) for at in range(count)]


class Copies:
    def __init__(self, send_sems, recv_sems):
        self.send_sems, self.recv_sems, self.count, self.sent = send_sems, recv_sems, 0, []

    def slot(self):
        self.count += 1
        return self.count - 1

    def send(self, slot, source, target, device):
        copy = pltpu.make_async_remote_copy(
            src_ref=source,
            dst_ref=target,
            send_sem=self.send_sems.at[slot],
            recv_sem=self.recv_sems.at[slot],
            device_id=device,
            device_id_type=MESH,
        )
        copy.start()
        self.sent.append(copy)

    def arrived(self, slot, target, device):
        pltpu.make_async_remote_copy(
            src_ref=target,
            dst_ref=target,
            send_sem=self.send_sems.at[slot],
            recv_sem=self.recv_sems.at[slot],
            device_id=device,
            device_id_type=MESH,
        ).wait_recv()

    def finish(self):
        for copy in self.sent:
            copy.wait_send()


def run_waves(chains):
    stages = len(chains[0])
    count = len(chains)
    for at in range(min(AHEAD, count)):
        chains[at][0]()
    for wave in range(1, count + SPACING * (stages - 1)):
        if wave + AHEAD - 1 < count:
            chains[wave + AHEAD - 1][0]()
        for stage in range(stages - 1, 0, -1):
            at = wave - 1 - SPACING * (stage - 1)
            if 0 <= at < count:
                chains[at][stage]()


def gather_chain(copies, where, depth, block, whole, local, start, width):
    x, z, y, core = where
    first = split_width(width)
    every = pl.ds(start, width)
    a, b = pl.ds(start, first), pl.ds(start + first, width - first)
    x_peer = device_of(1 - x, z, y, core)
    y_peer = device_of(x, z, 1 - y, core)
    partner = device_of(x, z, y, 1 - core)
    steps = range(1, depth)
    z_peers = [device_of(x, lax.rem(z + k, depth), y, core) for k in steps]
    z_from = [lax.rem(z + depth - k, depth) for k in steps]
    along = [copies.slot() for _ in steps]
    ay, ax, bx, by = [copies.slot() for _ in range(4)]
    shared = [copies.slot() for _ in range(5)]

    def share(slot, target):
        copies.send(slot, target, target, partner)

    def begin():
        mine = whole.at[x, z, y, core]
        for k in range(depth - 1):
            copies.send(along[k], block.at[:, every], mine.at[:, every], z_peers[k])

    def second():
        if local is not None:
            local.wait()
        for k in range(depth - 1):
            copies.arrived(along[k], whole.at[x, z_from[k], y, core, :, every], z_peers[k])
        for slot, part, peer in ((ay, a, y_peer), (bx, b, x_peer)):
            column = whole.at[x, :, y, core, :, part]
            copies.send(slot, column, column, peer)
        share(shared[0], whole.at[x, :, y, core, :, every])

    def third():
        copies.arrived(ay, whole.at[x, :, 1 - y, core, :, a], y_peer)
        plane = whole.at[x, :, :, core, :, a]
        copies.send(ax, plane, plane, x_peer)
        copies.arrived(bx, whole.at[1 - x, :, y, core, :, b], x_peer)
        sheet = whole.at[:, :, y, core, :, b]
        copies.send(by, sheet, sheet, y_peer)
        share(shared[1], whole.at[x, :, 1 - y, core, :, a])
        share(shared[2], whole.at[1 - x, :, y, core, :, b])

    def fourth():
        copies.arrived(ax, whole.at[1 - x, :, :, core, :, a], x_peer)
        share(shared[3], whole.at[1 - x, :, :, core, :, a])
        copies.arrived(by, whole.at[:, :, 1 - y, core, :, b], y_peer)
        share(shared[4], whole.at[:, :, 1 - y, core, :, b])

    def last():
        other = 1 - core
        copies.arrived(shared[0], whole.at[x, :, y, other, :, every], partner)
        copies.arrived(shared[1], whole.at[x, :, 1 - y, other, :, a], partner)
        copies.arrived(shared[2], whole.at[1 - x, :, y, other, :, b], partner)
        copies.arrived(shared[3], whole.at[1 - x, :, :, other, :, a], partner)
        copies.arrived(shared[4], whole.at[:, :, 1 - y, other, :, b], partner)

    return begin, second, third, fourth, last


def gather_kernel(depth, pieces_count, *refs):
    count = (len(refs) - 3 - 2 * pieces_count) // 2
    pieces, blocks = refs[:pieces_count], refs[pieces_count : pieces_count + count]
    outs = refs[pieces_count + count : -3]
    images, wholes = outs[:pieces_count], outs[pieces_count:]
    send_sems, recv_sems, own_sems = refs[-3:]
    where = place()
    x, z, y, core = where
    copies = Copies(send_sems, recv_sems)
    local = [
        pltpu.make_async_copy(block, whole.at[x, z, y, core], own_sems.at[at])
        for at, (block, whole) in enumerate(zip(blocks, wholes))
    ]
    kept = [
        pltpu.make_async_copy(piece.at[x], image.at[x], own_sems.at[count + at])
        for at, (piece, image) in enumerate(zip(pieces, images))
    ]
    for copy in local + kept:
        copy.start()
    greet(*where, depth)
    chains = []
    for block, whole, copy in zip(blocks, wholes, local):
        for start, width in chunks_of(block.shape[1]):
            once = copy if start == 0 else None
            chains.append(gather_chain(copies, where, depth, block, whole, once, start, width))
    slots = []
    x_peer = device_of(1 - x, z, y, core)
    for at in range(pieces_count):
        slots.append(copies.slot())
        copies.send(slots[at], pieces[at].at[1 - x], images[at].at[x], x_peer)
    run_waves(chains)
    for at in range(pieces_count):
        copies.arrived(slots[at], images[at].at[1 - x], x_peer)
        kept[at].wait()
    copies.finish()


def gather_weights(pieces, blocks, depth):
    chunks = sum(len(chunks_of(block.shape[1])) for block in blocks)
    copies = (depth + 8) * chunks + len(pieces)
    return pl.pallas_call(
        functools.partial(gather_kernel, depth, len(pieces)),
        in_specs=[IN_VMEM] * (len(pieces) + len(blocks)),
        out_specs=[ANY] * (len(pieces) + len(blocks)),
        out_shape=[jax.ShapeDtypeStruct(piece.shape, piece.dtype) for piece in pieces]
        + [
            jax.ShapeDtypeStruct((SIDES, depth, 2, 2) + block.shape, block.dtype)
            for block in blocks
        ],
        scratch_shapes=[
            pltpu.SemaphoreType.DMA((copies,)),
            pltpu.SemaphoreType.DMA((copies,)),
            pltpu.SemaphoreType.DMA((len(pieces) + len(blocks),)),
        ],
        compiler_params=pltpu.CompilerParams(collective_id=1, has_side_effects=True),
        name="gather_weights",
    )(*pieces, *blocks)


def add_blocks(count, target, term):
    @pl.loop(0, count)
    def _(at):
        total = target(at)[...].astype(jnp.float32) + term(at)[...].astype(jnp.float32)
        target(at)[...] = total.astype(jnp.bfloat16)


def scatter_chain(copies, where, depth, grad, total, buffers, load_sems, start, width):
    x, z, y, core = where
    own, halves, ax_in, by_in, along, along_in = buffers
    first = split_width(width)
    every = pl.ds(start, width)
    a, b = pl.ds(start, first), pl.ds(start + first, width - first)
    x_peer = device_of(1 - x, z, y, core)
    y_peer = device_of(x, z, 1 - y, core)
    partner = device_of(x, z, y, 1 - core)
    steps = range(1, depth)
    z_to = [lax.rem(z + k, depth) for k in steps]
    z_peers = [device_of(x, at, y, core) for at in z_to]
    pair = [copies.slot() for _ in range(SIDES)]
    ax, ay, bx, by = [copies.slot() for _ in range(4)]
    hops = [copies.slot() for _ in steps]
    load = [
        pltpu.make_async_copy(
            grad[side].at[:, :, core, :, every],
            own.at[side, :, :, :, every],
            load_sems[side],
        )
        for side in range(SIDES)
    ]

    def begin():
        for side in range(SIDES):
            load[side].start()
            copies.send(
                pair[side],
                grad[side].at[:, :, 1 - core, :, every],
                halves.at[side, :, :, :, every],
                partner,
            )

    def second():
        for side in range(SIDES):
            load[side].wait()
            copies.arrived(pair[side], halves.at[side, :, :, :, every], partner)

        def at_block(ref, at):
            return ref.at[
                lax.div(at, depth * 2), lax.rem(lax.div(at, 2), depth), lax.rem(at, 2), :, every
            ]

        add_blocks(
            SIDES * depth * 2, lambda at: at_block(halves, at), lambda at: at_block(own, at)
        )
        copies.send(ax, halves.at[1 - x, :, :, :, a], ax_in.at[:, :, :, a], x_peer)
        copies.send(by, halves.at[:, :, 1 - y, :, b], by_in.at[:, :, :, b], y_peer)

    def third():
        copies.arrived(ax, ax_in.at[:, :, :, a], x_peer)
        add_blocks(
            depth * 2,
            lambda at: ax_in.at[lax.div(at, 2), lax.rem(at, 2), :, a],
            lambda at: halves.at[x, lax.div(at, 2), lax.rem(at, 2), :, a],
        )
        copies.send(ay, ax_in.at[:, 1 - y, :, a], along.at[:, :, a], y_peer)
        copies.arrived(by, by_in.at[:, :, :, b], y_peer)
        add_blocks(
            SIDES * depth,
            lambda at: by_in.at[lax.div(at, depth), lax.rem(at, depth), :, b],
            lambda at: halves.at[lax.div(at, depth), lax.rem(at, depth), y, :, b],
        )
        copies.send(bx, by_in.at[1 - x, :, :, b], along.at[:, :, b], x_peer)

    def fourth():
        copies.arrived(ay, along.at[:, :, a], y_peer)
        add_blocks(depth, lambda at: along.at[at, :, a], lambda at: ax_in.at[at, y, :, a])
        copies.arrived(bx, along.at[:, :, b], x_peer)
        add_blocks(depth, lambda at: along.at[at, :, b], lambda at: by_in.at[x, at, :, b])
        for k in range(depth - 1):
            copies.send(
                hops[k], along.at[z_to[k], :, every], along_in.at[k, :, every], z_peers[k]
            )

    def last():
        for k in range(depth - 1):
            copies.arrived(hops[k], along_in.at[k, :, every], z_peers[k])
        sums = along[z, :, every].astype(jnp.float32)
        for k in range(depth - 1):
            sums += along_in[k, :, every].astype(jnp.float32)
        total[:, every] = sums

    return begin, second, third, fourth, last


def scatter_kernel(depth, count, wholes_count, *refs):
    grads = [refs[SIDES * at : SIDES * at + SIDES] for at in range(count)]
    refs = refs[SIDES * count :]
    wholes, refs = refs[:wholes_count], refs[wholes_count:]
    totals, pieces = refs[:count], refs[count : count + wholes_count]
    refs = refs[count + wholes_count :]
    send_sems, recv_sems, own_sems = refs[-3:]
    where = place()
    x, z, y, core = where
    copies = Copies(send_sems, recv_sems)
    greet(*where, depth)
    x_peer = device_of(1 - x, z, y, core)
    kept = []
    slots = [copies.slot() for _ in wholes]
    for at in range(wholes_count):
        width = pieces[at].shape[2]
        mine = pl.ds(pl.multiple_of(x * width, width), width)
        theirs = pl.ds(pl.multiple_of((1 - x) * width, width), width)
        copy = pltpu.make_async_copy(
            wholes[at].at[:, mine], pieces[at].at[x], own_sems.at[at]
        )
        copy.start()
        kept.append(copy)
        copies.send(slots[at], wholes[at].at[:, theirs], pieces[at].at[x], x_peer)
    chains = []
    loads = iter(range(own_sems.shape[0] - wholes_count))
    for at in range(count):
        buffers = refs[BUFFERS * at : BUFFERS * at + BUFFERS]
        for start, width in chunks_of(totals[at].shape[1]):
            load_sems = [own_sems.at[wholes_count + next(loads)] for _ in range(SIDES)]
            chains.append(
                scatter_chain(
                    copies, where, depth, grads[at], totals[at], buffers, load_sems, start, width
                )
            )
    run_waves(chains)
    for at in range(wholes_count):
        copies.arrived(slots[at], pieces[at].at[1 - x], x_peer)
        kept[at].wait()
    copies.finish()


def scatter_buffers(depth, rows, width):
    shapes = [
        (SIDES, depth, 2, rows, width),
        (SIDES, depth, 2, rows, width),
        (depth, 2, rows, width),
        (SIDES, depth, rows, width),
        (depth, rows, width),
        (depth - 1, rows, width),
    ]
    return [pltpu.VMEM(shape, jnp.bfloat16) for shape in shapes]


def scatter_grads(grads, wholes, depth):
    chunks = sum(len(chunks_of(grad[0].shape[4])) for grad in grads)
    copies = (depth + 5) * chunks + len(wholes)
    scratch = []
    for grad in grads:
        scratch += scatter_buffers(depth, grad[0].shape[3], grad[0].shape[4])
    return pl.pallas_call(
        functools.partial(scatter_kernel, depth, len(grads), len(wholes)),
        in_specs=[ANY] * SIDES * len(grads) + [IN_VMEM] * len(wholes),
        out_specs=[IN_VMEM] * len(grads) + [ANY] * len(wholes),
        out_shape=[jax.ShapeDtypeStruct(grad[0].shape[3:], jnp.float32) for grad in grads]
        + [
            jax.ShapeDtypeStruct((SIDES, whole.shape[0], whole.shape[1] // SIDES), whole.dtype)
            for whole in wholes
        ],
        scratch_shapes=scratch
        + [
            pltpu.SemaphoreType.DMA((copies,)),
            pltpu.SemaphoreType.DMA((copies,)),
            pltpu.SemaphoreType.DMA((SIDES * chunks + len(wholes),)),
        ],
        compiler_params=pltpu.CompilerParams(
            collective_id=2, has_side_effects=True, vmem_limit_bytes=60 * 2**20
        ),
        name="scatter_grads",
    )(*[half for grad in grads for half in grad], *wholes)


def to_image(piece):
    col = lax.axis_index("col")
    rows = piece.shape[0] // 2
    kept = lax.dynamic_slice_in_dim(piece, col * rows, rows, 0)
    sent = lax.dynamic_slice_in_dim(piece, (1 - col) * rows, rows, 0)
    other = lax.ppermute(sent, "col", [(0, 1), (1, 0)])
    return jnp.where(
        col == 0, jnp.concatenate([kept, other], 1), jnp.concatenate([other, kept], 1)
    )


def from_image(whole):
    col = lax.axis_index("col")
    width = whole.shape[1] // 2
    kept = lax.dynamic_slice_in_dim(whole, col * width, width, 1)
    sent = lax.dynamic_slice_in_dim(whole, (1 - col) * width, width, 1)
    other = lax.ppermute(sent, "col", [(0, 1), (1, 0)])
    return jnp.where(
        col == 0, jnp.concatenate([kept, other], 0), jnp.concatenate([other, kept], 0)
    )


def product(left, right, left_at, right_at):
    return lax.dot_general(
        left, right, (((left_at,), (right_at,)), ((), ())), preferred_element_type=jnp.float32
    )


def norm_back(upstream, scaled, inverse, gain_row):
    scaled_grad = upstream * gain_row
    first_mean = jnp.mean(scaled_grad, -1, keepdims=True)
    second_mean = jnp.mean(scaled_grad * scaled, -1, keepdims=True)
    return inverse * (scaled_grad - first_mean - scaled * second_mean)


def group_order(block):
    rows = block.shape[0]
    return block.reshape(rows, 3, -1, GROUP).transpose(0, 2, 1, 3).reshape(rows, -1)


def part_order(block):
    rows = block.shape[0]
    return block.reshape(rows, -1, 3, GROUP).transpose(0, 2, 1, 3).reshape(rows, 3, -1)


def image_shards(
    tokens,
    first_gain,
    first_shift,
    mixer_weight,
    mixer_bias,
    merge_weight,
    merge_bias,
    second_gain,
    second_shift,
    expand_weight,
    expand_bias,
    reduce_weight,
    reduce_bias,
    cotangent,
):
    low = jnp.bfloat16
    cols = lax.axis_size("col")
    rows = lax.axis_size("row")
    piece = first_gain.shape[0]
    hidden_piece = expand_bias.shape[0]
    block_rows = mixer_weight.shape[0]
    vectors = jnp.concatenate(
        [
            jnp.stack(
                [
                    first_gain,
                    first_shift,
                    mixer_bias[0],
                    mixer_bias[1],
                    merge_bias,
                    second_gain,
                    second_shift,
                    reduce_bias,
                ]
            ).reshape(-1),
            expand_bias,
        ]
    ).astype(low)
    vector_rows = vectors.shape[0] // GROUP
    vector_block = jnp.pad(
        vectors.reshape(vector_rows, GROUP), ((0, block_rows - vector_rows), (0, 0))
    )
    mixer_width = 3 * mixer_weight.shape[2]
    first_block = jnp.concatenate([group_order(mixer_weight).astype(low), vector_block], 1)
    depth = rows // 4
    sides = (cols, tokens.shape[0] // cols, tokens.shape[1])
    image, mixed, merger, expander, reducer = gather_weights(
        [tokens.reshape(sides)],
        [
            first_block,
            merge_weight.astype(low).T,
            expand_weight.astype(low),
            reduce_weight.astype(low).T,
        ],
        depth,
    )
    image = jnp.concatenate([image[h] for h in range(cols)], 1)
    upstream_low = to_image(cotangent)
    mixed, merger, expander, reducer = [
        whole.reshape(cols, rows * block_rows, whole.shape[-1])
        for whole in (mixed, merger, expander, reducer)
    ]
    mixer = mixed[:, :, :mixer_width]
    spread = mixed[:, :, mixer_width:].reshape(cols, rows, block_rows, GROUP)[:, :, :vector_rows]
    spread = spread.reshape(cols, rows, -1).astype(jnp.float32).transpose(1, 0, 2)
    rows_of = spread[:, :, : 8 * piece].reshape(rows, cols, 8, piece).transpose(2, 0, 1, 3)
    rows_of = rows_of.reshape(8, -1)
    expand_shift = spread[:, :, 8 * piece :].reshape(cols, -1)
    first_gain_row, first_shift_row = rows_of[0], rows_of[1]
    query_bias, value_bias, merge_shift = rows_of[2], rows_of[3], rows_of[4]
    second_gain_row, second_shift_row, reduce_shift = rows_of[5], rows_of[6], rows_of[7]
    mixer_shift = jnp.stack(
        [
            query_bias.reshape(cols, -1, GROUP),
            jnp.zeros_like(query_bias).reshape(cols, -1, GROUP),
            value_bias.reshape(cols, -1, GROUP),
        ],
        2,
    ).reshape(cols, -1)

    inputs = image.astype(jnp.float32)
    first_scaled, first_inverse, first_normed = normalize(inputs, first_gain_row, first_shift_row)
    first_low = first_normed.astype(low)
    projected = jnp.stack(
        [(product(first_low, mixer[h], 1, 0) + mixer_shift[h]).astype(low) for h in range(cols)]
    )
    attended = attention_forward(projected)
    merged = sum(product(attended[h], merger[h], 1, 1) for h in range(cols))
    hidden = inputs + merged + merge_shift
    second_scaled, second_inverse, second_normed = normalize(
        hidden, second_gain_row, second_shift_row
    )
    second_low = second_normed.astype(low)
    expanded = [product(second_low, expander[h], 1, 0) + expand_shift[h] for h in range(cols)]
    activated = [quick_gelu(part).astype(low) for part in expanded]
    reduced = sum(product(activated[h], reducer[h], 1, 1) for h in range(cols))
    layer_output = from_image((hidden + reduced + reduce_shift).astype(low))

    upstream = upstream_low.astype(jnp.float32)
    reducer_grad = [product(upstream_low, activated[h], 0, 0).astype(low) for h in range(cols)]
    reducer_parts = [part.reshape(rows, block_rows, -1) for part in reducer_grad]
    reduce_total = lax.psum_scatter(
        jnp.stack(reducer_parts, 1).reshape(rows * cols * block_rows, -1),
        ("row", "col"),
        scatter_dimension=0,
        tiled=True,
    ).astype(jnp.float32)
    expanded_grad = [
        (product(upstream_low, reducer[h], 1, 0) * gelu_slope(expanded[h])).astype(low)
        for h in range(cols)
    ]
    expander_grad = [product(second_low, expanded_grad[h], 0, 0).astype(low) for h in range(cols)]
    expand_shift_grad = [jnp.sum(part.astype(jnp.float32), 0) for part in expanded_grad]
    second_grad = sum(product(expanded_grad[h], expander[h], 1, 1) for h in range(cols))
    hidden_grad = upstream + norm_back(
        second_grad, second_scaled, second_inverse, second_gain_row
    )
    hidden_low = hidden_grad.astype(low)
    merger_grad = [product(hidden_low, attended[h], 0, 0).astype(low) for h in range(cols)]
    attended_grad = jnp.stack(
        [product(hidden_low, merger[h], 1, 0).astype(low) for h in range(cols)]
    )
    projected_grad = attention_back(projected, attended_grad)
    mixer_grad = [product(first_low, projected_grad[h], 0, 0).astype(low) for h in range(cols)]
    bias_sums = jnp.sum(projected_grad.astype(jnp.float32), 1)
    bias_sums = bias_sums.reshape(cols, -1, 3, GROUP).transpose(2, 0, 1, 3).reshape(3, -1)
    first_grad = sum(product(projected_grad[h], mixer[h], 1, 1) for h in range(cols))
    input_grad = hidden_grad + norm_back(first_grad, first_scaled, first_inverse, first_gain_row)
    vector_grads = jnp.stack(
        [
            jnp.sum(first_grad * first_scaled, 0),
            jnp.sum(first_grad, 0),
            bias_sums[0],
            bias_sums[2],
            jnp.sum(hidden_grad, 0),
            jnp.sum(second_grad * second_scaled, 0),
            jnp.sum(second_grad, 0),
            jnp.sum(upstream, 0),
        ]
    )
    vector_grads = vector_grads.reshape(8, rows, cols, piece).transpose(2, 1, 0, 3)
    hidden_grads = jnp.concatenate(expand_shift_grad).reshape(rows, cols, hidden_piece)
    vector_grads = jnp.concatenate(
        [vector_grads.reshape(cols, rows, -1), hidden_grads.transpose(1, 0, 2)], 2
    )
    vector_grads = vector_grads.reshape(cols, rows, vector_rows, GROUP).astype(low)
    vector_grads = jnp.pad(
        vector_grads, ((0, 0), (0, 0), (0, block_rows - vector_rows), (0, 0))
    ).reshape(cols, rows * block_rows, GROUP)
    mixed_grad = [jnp.concatenate([mixer_grad[h], vector_grads[h]], 1) for h in range(cols)]
    grads = [
        [part.reshape(depth, 2, 2, block_rows, -1) for part in halves]
        for halves in (expander_grad, merger_grad, mixed_grad)
    ]
    expand_total, merge_total, mixed_total, tokens_gradient = (
        scatter_grads(grads, [input_grad.astype(low)], depth)
    )
    tokens_gradient = tokens_gradient.reshape(tokens.shape).astype(jnp.float32)
    mixer_total = part_order(mixed_total[:, :mixer_width])
    vector_total = mixed_total[:vector_rows, mixer_width:].reshape(-1)
    small = vector_total[: 8 * piece].reshape(8, piece)
    return (
        layer_output,
        tokens_gradient,
        small[0],
        small[1],
        mixer_total,
        small[2:4],
        merge_total.T,
        small[4],
        small[5],
        small[6],
        expand_total,
        vector_total[8 * piece :],
        reduce_total.T,
        small[7],
    )


def solution(mesh):
    def body(*arguments):
        images = arguments[0].shape[0] // SEQ
        whole = images == 2 and lax.axis_size("col") == 2
        return (image_shards if whole else split_shards)(*arguments)

    return jax.shard_map(
        body,
        mesh=mesh,
        in_specs=(
            P("row", "col"),
            P(("row", "col")),
            P(("row", "col")),
            P("row", None, "col"),
            P(None, ("row", "col")),
            P("col", "row"),
            P(("row", "col")),
            P(("row", "col")),
            P(("row", "col")),
            P("row", "col"),
            P(("row", "col")),
            P("col", "row"),
            P(("row", "col")),
            P("row", "col"),
        ),
        out_specs=(
            P("row", "col"),
            P("row", "col"),
            P(("row", "col")),
            P(("row", "col")),
            P("row", None, "col"),
            P(None, ("row", "col")),
            P("col", "row"),
            P(("row", "col")),
            P(("row", "col")),
            P(("row", "col")),
            P("row", "col"),
            P(("row", "col")),
            P("col", "row"),
            P(("row", "col")),
        ),
        check_vma=False,
    )
```

```python
import functools

import jax
import jax.numpy as jnp
from jax import lax
from jax.experimental import pallas as pl
from jax.experimental.pallas import tpu as pltpu
from jax.sharding import PartitionSpec as P

HEAD_DIM = 64
SEQ = 577


EPSILON = 1e-05
SLOPE = 1.702


def quick_gelu(inputs):
    return inputs * jax.nn.sigmoid(SLOPE * inputs)


def gelu_slope(inputs):
    sigmoid_value = jax.nn.sigmoid(SLOPE * inputs)
    return sigmoid_value + SLOPE * inputs * sigmoid_value * (1.0 - sigmoid_value)


def own_columns(values, start, width):
    return lax.dynamic_slice_in_dim(values, start, width, values.ndim - 1)


def normalize(values, gain_row, shift_row):
    feature_count = values.shape[-1]
    row_mean = jnp.sum(values, -1, keepdims=True) / feature_count
    square = jnp.sum(values * values, -1, keepdims=True) / feature_count
    inverse = lax.rsqrt(square - row_mean * row_mean + EPSILON)
    scaled = (values - row_mean) * inverse
    return (scaled, inverse, scaled * gain_row + shift_row)


def column_sum(partial_value):
    return lax.psum_scatter(
        partial_value.astype(jnp.bfloat16), "col", scatter_dimension=1, tiled=True
    ).astype(jnp.float32)


def feature_totals(first_sum, second_sum):
    return lax.psum((first_sum, second_sum), "col")


def normed_gather(piece):
    return lax.all_gather(piece, "col", axis=1, tiled=True)


def shared_back(upstream, scaled, inverse, gain_row, feature_count):
    scaled_grad = upstream * gain_row
    totals = feature_totals(jnp.sum(scaled_grad, -1), jnp.sum(scaled_grad * scaled, -1))
    first_mean = totals[0][:, None] / feature_count
    second_mean = totals[1][:, None] / feature_count
    return inverse * (scaled_grad - first_mean - scaled * second_mean)


def fetch_weights(masters):
    return (
        lax.all_gather(masters[0], "row", axis=0, tiled=True),
        lax.all_gather(masters[1], "row", axis=1, tiled=True),
        lax.all_gather(masters[2], "row", axis=0, tiled=True),
        lax.all_gather(masters[3], "row", axis=1, tiled=True),
    )


def attend_forward(parts):
    queries, key_rows, values = parts
    score_scale = queries.shape[-1] ** (-0.5)
    scores = (
        jnp.einsum("qhd,khd->hqk", queries, key_rows, preferred_element_type=jnp.float32)
        * score_scale
    )
    score_top = jnp.max(scores, -1, keepdims=True)
    exponent = jnp.exp(scores - score_top)
    row_total = jnp.sum(exponent, -1, keepdims=True)
    weights = (exponent / row_total).astype(jnp.bfloat16)
    mixture = jnp.einsum("hqk,khd->qhd", weights, values, preferred_element_type=jnp.float32)
    return (mixture.astype(jnp.bfloat16), (score_top + jnp.log(row_total))[..., 0])


def attend_back(parts):
    queries, key_rows, values, log_total, upstream = parts
    score_scale = queries.shape[-1] ** (-0.5)
    scores = (
        jnp.einsum("qhd,khd->hqk", queries, key_rows, preferred_element_type=jnp.float32)
        * score_scale
    )
    probability = jnp.exp(scores - log_total[..., None])
    rounded = probability.astype(jnp.bfloat16)
    pulled = jnp.einsum("qhd,khd->hqk", upstream, values, preferred_element_type=jnp.float32)
    centre = jnp.sum(probability * pulled, -1, keepdims=True)
    score_grad = (probability * (pulled - centre)).astype(jnp.bfloat16)
    query_grad = (
        jnp.einsum("hqk,khd->qhd", score_grad, key_rows, preferred_element_type=jnp.float32)
        * score_scale
    )
    key_grad = (
        jnp.einsum("hqk,qhd->khd", score_grad, queries, preferred_element_type=jnp.float32)
        * score_scale
    )
    value_grad = jnp.einsum("hqk,qhd->khd", rounded, upstream, preferred_element_type=jnp.float32)
    return (query_grad, key_grad, value_grad)


def split_shards(
    tokens,
    first_gain,
    first_shift,
    mixer_weight,
    mixer_bias,
    merge_weight,
    merge_bias,
    second_gain,
    second_shift,
    expand_weight,
    expand_bias,
    reduce_weight,
    reduce_bias,
    cotangent,
):
    col_index = lax.axis_index("col")
    piece_width = tokens.shape[1]
    hidden_width = expand_weight.shape[1]
    start = col_index * piece_width
    hidden_start = col_index * hidden_width
    vector_pieces = jnp.stack(
        [
            first_gain,
            first_shift,
            mixer_bias[0],
            mixer_bias[1],
            merge_bias,
            second_gain,
            second_shift,
            reduce_bias,
        ]
    ).astype(jnp.bfloat16)
    vectors_low, expand_shift_low = (
        lax.all_gather(vector_pieces, ("row", "col"), axis=1, tiled=True),
        lax.all_gather(expand_bias.astype(jnp.bfloat16), ("row", "col"), axis=0, tiled=True),
    )
    vectors = vectors_low.astype(jnp.float32)
    feature_count = vectors.shape[1]
    first_gain_row, first_shift_row = (vectors[0], vectors[1])
    query_bias = own_columns(vectors[2], start, piece_width)
    value_bias = own_columns(vectors[3], start, piece_width)
    merge_shift = vectors[4]
    second_gain_row, second_shift_row = (vectors[5], vectors[6])
    reduce_shift = own_columns(vectors[7], start, piece_width)
    expand_shift = own_columns(expand_shift_low.astype(jnp.float32), hidden_start, hidden_width)
    masters = (
        mixer_weight.astype(jnp.bfloat16),
        merge_weight.astype(jnp.bfloat16),
        expand_weight.astype(jnp.bfloat16),
        reduce_weight.astype(jnp.bfloat16),
    )
    mixer_local, merger, expander, reducer = fetch_weights(masters)
    inputs_whole, upstream_whole = (
        lax.all_gather(tokens, "col", axis=1, tiled=True),
        lax.all_gather(cotangent, "col", axis=1, tiled=True),
    )
    inputs = inputs_whole.astype(jnp.float32)
    row_count = inputs.shape[0]
    first_scaled, first_inverse, first_normed = normalize(inputs, first_gain_row, first_shift_row)
    first_low = first_normed.astype(jnp.bfloat16)
    projected = jnp.einsum(
        "rd,dtc->rtc", first_low, mixer_local, preferred_element_type=jnp.float32
    )
    projected = projected + jnp.stack([query_bias, jnp.zeros_like(query_bias), value_bias])
    projected_low = projected.astype(jnp.bfloat16)
    head_shape = (row_count // SEQ, SEQ, piece_width // HEAD_DIM, HEAD_DIM)
    queries = projected_low[:, 0].reshape(head_shape)
    key_rows = projected_low[:, 1].reshape(head_shape)
    values = projected_low[:, 2].reshape(head_shape)
    attended, log_total = lax.map(attend_forward, (queries, key_rows, values))
    attended = attended.reshape(row_count, piece_width)
    merged_part = jnp.dot(attended, merger, preferred_element_type=jnp.float32)
    hidden_own = (
        own_columns(inputs, start, piece_width)
        + column_sum(merged_part)
        + own_columns(merge_shift, start, piece_width)
    )
    totals = feature_totals(jnp.sum(hidden_own, -1), jnp.sum(hidden_own * hidden_own, -1))
    row_mean = totals[0][:, None] / feature_count
    square = totals[1][:, None] / feature_count
    second_inverse = lax.rsqrt(square - row_mean * row_mean + EPSILON)
    second_scaled = (hidden_own - row_mean) * second_inverse
    second_gain_own = own_columns(second_gain_row, start, piece_width)
    second_piece = second_scaled * second_gain_own + own_columns(
        second_shift_row, start, piece_width
    )
    second_low = normed_gather(second_piece.astype(jnp.bfloat16))
    expanded = jnp.dot(second_low, expander, preferred_element_type=jnp.float32) + expand_shift
    activated = quick_gelu(expanded).astype(jnp.bfloat16)
    reduced = column_sum(jnp.dot(activated, reducer, preferred_element_type=jnp.float32))
    layer_output = (hidden_own + reduced + reduce_shift).astype(jnp.bfloat16)
    masters_again = lax.optimization_barrier((masters, layer_output))[0]
    mixer_local, merger, expander, reducer = fetch_weights(masters_again)
    upstream_own = cotangent.astype(jnp.float32)
    reducer_grad = jnp.einsum(
        "rf,rd->fd", activated, upstream_whole, preferred_element_type=jnp.float32
    )
    activated_grad = jnp.einsum(
        "rd,fd->rf", upstream_whole, reducer, preferred_element_type=jnp.float32
    )
    expanded_grad = (activated_grad * gelu_slope(expanded)).astype(jnp.bfloat16)
    expander_grad = jnp.einsum(
        "rd,rf->df", second_low, expanded_grad, preferred_element_type=jnp.float32
    )
    expand_shift_grad = jnp.sum(expanded_grad.astype(jnp.float32), 0)
    second_part = jnp.einsum(
        "rf,df->rd", expanded_grad, expander, preferred_element_type=jnp.float32
    )
    second_grad = column_sum(second_part)
    hidden_part = shared_back(
        second_grad, second_scaled, second_inverse, second_gain_own, feature_count
    )
    hidden_grad = upstream_own + hidden_part
    second_gain_grad = jnp.sum(second_grad * second_scaled, 0)
    second_shift_grad = jnp.sum(second_grad, 0)
    hidden_low = normed_gather(hidden_grad.astype(jnp.bfloat16))
    merger_grad = jnp.einsum("rc,rd->cd", attended, hidden_low, preferred_element_type=jnp.float32)
    attended_grad = jnp.einsum(
        "rd,cd->rc", hidden_low, merger, preferred_element_type=jnp.float32
    ).astype(jnp.bfloat16)
    query_grad, key_grad, value_grad = lax.map(
        attend_back, (queries, key_rows, values, log_total, attended_grad.reshape(head_shape))
    )
    projected_grad = jnp.stack(
        [
            query_grad.reshape(row_count, piece_width),
            key_grad.reshape(row_count, piece_width),
            value_grad.reshape(row_count, piece_width),
        ],
        1,
    ).astype(jnp.bfloat16)
    mixer_grad = jnp.einsum(
        "rd,rtc->dtc", first_low, projected_grad, preferred_element_type=jnp.float32
    )
    bias_sums = jnp.sum(projected_grad.astype(jnp.float32), 0)
    first_part = jnp.einsum(
        "rtc,dtc->rd", projected_grad, mixer_local, preferred_element_type=jnp.float32
    )
    first_grad = column_sum(first_part)
    first_scaled_own = own_columns(first_scaled, start, piece_width)
    input_part = shared_back(
        first_grad,
        first_scaled_own,
        first_inverse,
        own_columns(first_gain_row, start, piece_width),
        feature_count,
    )
    tokens_gradient = hidden_grad + input_part
    own_vector_grads = jnp.stack(
        [
            jnp.sum(first_grad * first_scaled_own, 0),
            jnp.sum(first_grad, 0),
            bias_sums[0],
            bias_sums[2],
            jnp.sum(hidden_grad, 0),
            second_gain_grad,
            second_shift_grad,
            jnp.sum(upstream_own, 0),
        ]
    )
    vector_whole = lax.dynamic_update_slice(
        jnp.zeros((8, feature_count), jnp.float32), own_vector_grads, (jnp.int32(0), start)
    )
    expand_whole = lax.dynamic_update_slice(
        jnp.zeros((hidden_width * lax.axis_size("col"),), jnp.float32),
        expand_shift_grad,
        (hidden_start,),
    )
    vector_total, expand_bias_total = (
        lax.psum_scatter(vector_whole, ("row", "col"), scatter_dimension=1, tiled=True),
        lax.psum_scatter(expand_whole, ("row", "col"), scatter_dimension=0, tiled=True),
    )
    mixer_total, merge_total, expand_total, reduce_total = (
        lax.psum_scatter(
            mixer_grad.astype(jnp.bfloat16), "row", scatter_dimension=0, tiled=True
        ).astype(jnp.float32),
        lax.psum_scatter(
            merger_grad.astype(jnp.bfloat16), "row", scatter_dimension=1, tiled=True
        ).astype(jnp.float32),
        lax.psum_scatter(
            expander_grad.astype(jnp.bfloat16), "row", scatter_dimension=0, tiled=True
        ).astype(jnp.float32),
        lax.psum_scatter(
            reducer_grad.astype(jnp.bfloat16), "row", scatter_dimension=1, tiled=True
        ).astype(jnp.float32),
    )
    return (
        layer_output,
        tokens_gradient,
        vector_total[0],
        vector_total[1],
        mixer_total,
        jnp.stack([vector_total[2], vector_total[3]]),
        merge_total,
        vector_total[4],
        vector_total[5],
        vector_total[6],
        expand_total,
        expand_bias_total,
        reduce_total,
        vector_total[7],
    )


GROUP = 128


def attention_forward_kernel(projected_ref, attended_ref):
    for head in range(GROUP // HEAD_DIM):
        at = head * HEAD_DIM
        queries = projected_ref[0, :, at : at + HEAD_DIM] * jnp.bfloat16(HEAD_DIM**-0.5)
        key_rows = projected_ref[0, :, GROUP + at : GROUP + at + HEAD_DIM]
        values = projected_ref[0, :, 2 * GROUP + at : 2 * GROUP + at + HEAD_DIM]
        scores = lax.dot_general(
            key_rows, queries, (((1,), (1,)), ((), ())), preferred_element_type=jnp.float32
        )
        exponent = jnp.exp(scores - jnp.max(scores, 0, keepdims=True))
        weights = exponent * (1.0 / jnp.sum(exponent, 0, keepdims=True))
        mixture = lax.dot_general(
            values,
            weights.astype(jnp.bfloat16),
            (((0,), (0,)), ((), ())),
            preferred_element_type=jnp.float32,
        )
        attended_ref[0, :, at : at + HEAD_DIM] = mixture.T.astype(jnp.bfloat16)


def attention_back_kernel(projected_ref, upstream_ref, grad_ref):
    for head in range(GROUP // HEAD_DIM):
        at = head * HEAD_DIM
        queries = projected_ref[0, :, at : at + HEAD_DIM] * jnp.bfloat16(HEAD_DIM**-0.5)
        key_rows = projected_ref[0, :, GROUP + at : GROUP + at + HEAD_DIM]
        values = projected_ref[0, :, 2 * GROUP + at : 2 * GROUP + at + HEAD_DIM]
        upstream = upstream_ref[0, :, at : at + HEAD_DIM]
        scores = lax.dot_general(
            key_rows, queries, (((1,), (1,)), ((), ())), preferred_element_type=jnp.float32
        )
        exponent = jnp.exp(scores - jnp.max(scores, 0, keepdims=True))
        weights = exponent * (1.0 / jnp.sum(exponent, 0, keepdims=True))
        pulled = lax.dot_general(
            values, upstream, (((1,), (1,)), ((), ())), preferred_element_type=jnp.float32
        )
        centre = jnp.sum(weights * pulled, 0, keepdims=True)
        score_grad = (weights * (pulled - centre)).astype(jnp.bfloat16)
        value_grad = jnp.dot(
            weights.astype(jnp.bfloat16), upstream, preferred_element_type=jnp.float32
        )
        key_grad = jnp.dot(score_grad, queries, preferred_element_type=jnp.float32)
        query_grad = lax.dot_general(
            key_rows, score_grad, (((0,), (0,)), ((), ())), preferred_element_type=jnp.float32
        )
        query_grad = query_grad.T * HEAD_DIM**-0.5
        grad_ref[0, :, at : at + HEAD_DIM] = query_grad.astype(jnp.bfloat16)
        grad_ref[0, :, GROUP + at : GROUP + at + HEAD_DIM] = key_grad.astype(jnp.bfloat16)
        grad_ref[0, :, 2 * GROUP + at : 2 * GROUP + at + HEAD_DIM] = value_grad.astype(
            jnp.bfloat16
        )


def attention_forward(projected):
    halves, rows, width = projected.shape
    groups = width // (3 * GROUP)
    return pl.pallas_call(
        attention_forward_kernel,
        grid=(halves, groups),
        in_specs=[pl.BlockSpec((1, rows, 3 * GROUP), lambda h, g: (h, 0, g))],
        out_specs=pl.BlockSpec((1, rows, GROUP), lambda h, g: (h, 0, g)),
        out_shape=jax.ShapeDtypeStruct((halves, rows, groups * GROUP), jnp.bfloat16),
        name="attention_forward",
    )(projected)


def attention_back(projected, upstream):
    halves, rows, width = projected.shape
    groups = width // (3 * GROUP)
    return pl.pallas_call(
        attention_back_kernel,
        grid=(halves, groups),
        in_specs=[
            pl.BlockSpec((1, rows, 3 * GROUP), lambda h, g: (h, 0, g)),
            pl.BlockSpec((1, rows, GROUP), lambda h, g: (h, 0, g)),
        ],
        out_specs=pl.BlockSpec((1, rows, 3 * GROUP), lambda h, g: (h, 0, g)),
        out_shape=jax.ShapeDtypeStruct(projected.shape, jnp.bfloat16),
        name="attention_back",
    )(projected, upstream)


MESH = pl.DeviceIdType.MESH
ANY = pl.BlockSpec(memory_space=pl.ANY)
IN_VMEM = pl.BlockSpec(memory_space=pltpu.VMEM)
SIDES = 2
BUFFERS = 6
CHUNK = 4
AHEAD = 12
SPACING = 2


def place():
    col = lax.axis_index("col")
    row = lax.axis_index("row")
    return col, lax.div(row, 4), lax.rem(lax.div(row, 2), 2), lax.rem(row, 2)


def device_of(x, z, y, core):
    return (z * 4 + y * 2 + core, x)


def greet(x, z, y, core, depth):
    barrier = pltpu.get_barrier_semaphore()
    others = [device_of(x, lax.rem(z + k, depth), y, core) for k in range(1, depth)]
    others += [
        device_of(x, z, 1 - y, core),
        device_of(1 - x, z, y, core),
        device_of(x, z, y, 1 - core),
    ]
    for other in others:
        pl.semaphore_signal(barrier, inc=1, device_id=other, device_id_type=MESH)
    pl.semaphore_wait(barrier, len(others))


def split_width(width):
    return width // GROUP // 2 * GROUP


def chunks_of(width):
    tiles = width // GROUP
    count = max(tiles // CHUNK, 1)
    edges = [CHUNK * GROUP * at for at in range(count)] + [width]
    return [(edges[at], edges[at + 1] - edges[at]) for at in range(count)]


class Copies:
    def __init__(self, send_sems, recv_sems):
        self.send_sems, self.recv_sems, self.count, self.sent = send_sems, recv_sems, 0, []

    def slot(self):
        self.count += 1
        return self.count - 1

    def send(self, slot, source, target, device):
        copy = pltpu.make_async_remote_copy(
            src_ref=source,
            dst_ref=target,
            send_sem=self.send_sems.at[slot],
            recv_sem=self.recv_sems.at[slot],
            device_id=device,
            device_id_type=MESH,
        )
        copy.start()
        self.sent.append(copy)

    def arrived(self, slot, target, device):
        pltpu.make_async_remote_copy(
            src_ref=target,
            dst_ref=target,
            send_sem=self.send_sems.at[slot],
            recv_sem=self.recv_sems.at[slot],
            device_id=device,
            device_id_type=MESH,
        ).wait_recv()

    def finish(self):
        for copy in self.sent:
            copy.wait_send()


def run_waves(chains):
    stages = len(chains[0])
    count = len(chains)
    for at in range(min(AHEAD, count)):
        chains[at][0]()
    for wave in range(1, count + SPACING * (stages - 1)):
        if wave + AHEAD - 1 < count:
            chains[wave + AHEAD - 1][0]()
        for stage in range(stages - 1, 0, -1):
            at = wave - 1 - SPACING * (stage - 1)
            if 0 <= at < count:
                chains[at][stage]()


def gather_chain(copies, where, depth, block, whole, local, start, width):
    x, z, y, core = where
    first = split_width(width)
    every = pl.ds(start, width)
    a, b = pl.ds(start, first), pl.ds(start + first, width - first)
    x_peer = device_of(1 - x, z, y, core)
    y_peer = device_of(x, z, 1 - y, core)
    partner = device_of(x, z, y, 1 - core)
    steps = range(1, depth)
    z_peers = [device_of(x, lax.rem(z + k, depth), y, core) for k in steps]
    z_from = [lax.rem(z + depth - k, depth) for k in steps]
    along = [copies.slot() for _ in steps]
    ay, ax, bx, by = [copies.slot() for _ in range(4)]
    shared = [copies.slot() for _ in range(5)]

    def share(slot, target):
        copies.send(slot, target, target, partner)

    def begin():
        mine = whole.at[x, z, y, core]
        for k in range(depth - 1):
            copies.send(along[k], block.at[:, every], mine.at[:, every], z_peers[k])

    def second():
        if local is not None:
            local.wait()
        for k in range(depth - 1):
            copies.arrived(along[k], whole.at[x, z_from[k], y, core, :, every], z_peers[k])
        for slot, part, peer in ((ay, a, y_peer), (bx, b, x_peer)):
            column = whole.at[x, :, y, core, :, part]
            copies.send(slot, column, column, peer)
        share(shared[0], whole.at[x, :, y, core, :, every])

    def third():
        copies.arrived(ay, whole.at[x, :, 1 - y, core, :, a], y_peer)
        plane = whole.at[x, :, :, core, :, a]
        copies.send(ax, plane, plane, x_peer)
        copies.arrived(bx, whole.at[1 - x, :, y, core, :, b], x_peer)
        sheet = whole.at[:, :, y, core, :, b]
        copies.send(by, sheet, sheet, y_peer)
        share(shared[1], whole.at[x, :, 1 - y, core, :, a])
        share(shared[2], whole.at[1 - x, :, y, core, :, b])

    def fourth():
        copies.arrived(ax, whole.at[1 - x, :, :, core, :, a], x_peer)
        share(shared[3], whole.at[1 - x, :, :, core, :, a])
        copies.arrived(by, whole.at[:, :, 1 - y, core, :, b], y_peer)
        share(shared[4], whole.at[:, :, 1 - y, core, :, b])

    def last():
        other = 1 - core
        copies.arrived(shared[0], whole.at[x, :, y, other, :, every], partner)
        copies.arrived(shared[1], whole.at[x, :, 1 - y, other, :, a], partner)
        copies.arrived(shared[2], whole.at[1 - x, :, y, other, :, b], partner)
        copies.arrived(shared[3], whole.at[1 - x, :, :, other, :, a], partner)
        copies.arrived(shared[4], whole.at[:, :, 1 - y, other, :, b], partner)

    return begin, second, third, fourth, last


def gather_kernel(depth, pieces_count, *refs):
    count = (len(refs) - 3 - 2 * pieces_count) // 2
    pieces, blocks = refs[:pieces_count], refs[pieces_count : pieces_count + count]
    outs = refs[pieces_count + count : -3]
    images, wholes = outs[:pieces_count], outs[pieces_count:]
    send_sems, recv_sems, own_sems = refs[-3:]
    where = place()
    x, z, y, core = where
    copies = Copies(send_sems, recv_sems)
    local = [
        pltpu.make_async_copy(block, whole.at[x, z, y, core], own_sems.at[at])
        for at, (block, whole) in enumerate(zip(blocks, wholes))
    ]
    kept = [
        pltpu.make_async_copy(piece.at[x], image.at[x], own_sems.at[count + at])
        for at, (piece, image) in enumerate(zip(pieces, images))
    ]
    for copy in local + kept:
        copy.start()
    greet(*where, depth)
    chains = []
    for block, whole, copy in zip(blocks, wholes, local):
        for start, width in chunks_of(block.shape[1]):
            once = copy if start == 0 else None
            chains.append(gather_chain(copies, where, depth, block, whole, once, start, width))
    slots = []
    x_peer = device_of(1 - x, z, y, core)
    for at in range(pieces_count):
        slots.append(copies.slot())
        copies.send(slots[at], pieces[at].at[1 - x], images[at].at[x], x_peer)
    run_waves(chains)
    for at in range(pieces_count):
        copies.arrived(slots[at], images[at].at[1 - x], x_peer)
        kept[at].wait()
    copies.finish()


def gather_weights(pieces, blocks, depth):
    chunks = sum(len(chunks_of(block.shape[1])) for block in blocks)
    copies = (depth + 8) * chunks + len(pieces)
    return pl.pallas_call(
        functools.partial(gather_kernel, depth, len(pieces)),
        in_specs=[IN_VMEM] * (len(pieces) + len(blocks)),
        out_specs=[ANY] * (len(pieces) + len(blocks)),
        out_shape=[jax.ShapeDtypeStruct(piece.shape, piece.dtype) for piece in pieces]
        + [
            jax.ShapeDtypeStruct((SIDES, depth, 2, 2) + block.shape, block.dtype)
            for block in blocks
        ],
        scratch_shapes=[
            pltpu.SemaphoreType.DMA((copies,)),
            pltpu.SemaphoreType.DMA((copies,)),
            pltpu.SemaphoreType.DMA((len(pieces) + len(blocks),)),
        ],
        compiler_params=pltpu.CompilerParams(collective_id=1, has_side_effects=True),
        name="gather_weights",
    )(*pieces, *blocks)


def add_blocks(count, target, term):
    @pl.loop(0, count)
    def _(at):
        total = target(at)[...].astype(jnp.float32) + term(at)[...].astype(jnp.float32)
        target(at)[...] = total.astype(jnp.bfloat16)


def scatter_chain(copies, where, depth, grad, total, buffers, load_sems, start, width):
    x, z, y, core = where
    own, halves, ax_in, by_in, along, along_in = buffers
    first = split_width(width)
    every = pl.ds(start, width)
    a, b = pl.ds(start, first), pl.ds(start + first, width - first)
    x_peer = device_of(1 - x, z, y, core)
    y_peer = device_of(x, z, 1 - y, core)
    partner = device_of(x, z, y, 1 - core)
    steps = range(1, depth)
    z_to = [lax.rem(z + k, depth) for k in steps]
    z_peers = [device_of(x, at, y, core) for at in z_to]
    pair = [copies.slot() for _ in range(SIDES)]
    ax, ay, bx, by = [copies.slot() for _ in range(4)]
    hops = [copies.slot() for _ in steps]
    load = [
        pltpu.make_async_copy(
            grad[side].at[:, :, core, :, every],
            own.at[side, :, :, :, every],
            load_sems[side],
        )
        for side in range(SIDES)
    ]

    def begin():
        for side in range(SIDES):
            load[side].start()
            copies.send(
                pair[side],
                grad[side].at[:, :, 1 - core, :, every],
                halves.at[side, :, :, :, every],
                partner,
            )

    def second():
        for side in range(SIDES):
            load[side].wait()
            copies.arrived(pair[side], halves.at[side, :, :, :, every], partner)

        def at_block(ref, at):
            return ref.at[
                lax.div(at, depth * 2), lax.rem(lax.div(at, 2), depth), lax.rem(at, 2), :, every
            ]

        add_blocks(
            SIDES * depth * 2, lambda at: at_block(halves, at), lambda at: at_block(own, at)
        )
        copies.send(ax, halves.at[1 - x, :, :, :, a], ax_in.at[:, :, :, a], x_peer)
        copies.send(by, halves.at[:, :, 1 - y, :, b], by_in.at[:, :, :, b], y_peer)

    def third():
        copies.arrived(ax, ax_in.at[:, :, :, a], x_peer)
        add_blocks(
            depth * 2,
            lambda at: ax_in.at[lax.div(at, 2), lax.rem(at, 2), :, a],
            lambda at: halves.at[x, lax.div(at, 2), lax.rem(at, 2), :, a],
        )
        copies.send(ay, ax_in.at[:, 1 - y, :, a], along.at[:, :, a], y_peer)
        copies.arrived(by, by_in.at[:, :, :, b], y_peer)
        add_blocks(
            SIDES * depth,
            lambda at: by_in.at[lax.div(at, depth), lax.rem(at, depth), :, b],
            lambda at: halves.at[lax.div(at, depth), lax.rem(at, depth), y, :, b],
        )
        copies.send(bx, by_in.at[1 - x, :, :, b], along.at[:, :, b], x_peer)

    def fourth():
        copies.arrived(ay, along.at[:, :, a], y_peer)
        add_blocks(depth, lambda at: along.at[at, :, a], lambda at: ax_in.at[at, y, :, a])
        copies.arrived(bx, along.at[:, :, b], x_peer)
        add_blocks(depth, lambda at: along.at[at, :, b], lambda at: by_in.at[x, at, :, b])
        for k in range(depth - 1):
            copies.send(
                hops[k], along.at[z_to[k], :, every], along_in.at[k, :, every], z_peers[k]
            )

    def last():
        for k in range(depth - 1):
            copies.arrived(hops[k], along_in.at[k, :, every], z_peers[k])
        sums = along[z, :, every].astype(jnp.float32)
        for k in range(depth - 1):
            sums += along_in[k, :, every].astype(jnp.float32)
        total[:, every] = sums

    return begin, second, third, fourth, last


def scatter_kernel(depth, count, wholes_count, *refs):
    grads = [refs[SIDES * at : SIDES * at + SIDES] for at in range(count)]
    refs = refs[SIDES * count :]
    wholes, refs = refs[:wholes_count], refs[wholes_count:]
    totals, pieces = refs[:count], refs[count : count + wholes_count]
    refs = refs[count + wholes_count :]
    send_sems, recv_sems, own_sems = refs[-3:]
    where = place()
    x, z, y, core = where
    copies = Copies(send_sems, recv_sems)
    greet(*where, depth)
    x_peer = device_of(1 - x, z, y, core)
    kept = []
    slots = [copies.slot() for _ in wholes]
    for at in range(wholes_count):
        width = pieces[at].shape[2]
        mine = pl.ds(pl.multiple_of(x * width, width), width)
        theirs = pl.ds(pl.multiple_of((1 - x) * width, width), width)
        copy = pltpu.make_async_copy(
            wholes[at].at[:, mine], pieces[at].at[x], own_sems.at[at]
        )
        copy.start()
        kept.append(copy)
        copies.send(slots[at], wholes[at].at[:, theirs], pieces[at].at[x], x_peer)
    chains = []
    loads = iter(range(own_sems.shape[0] - wholes_count))
    for at in range(count):
        buffers = refs[BUFFERS * at : BUFFERS * at + BUFFERS]
        for start, width in chunks_of(totals[at].shape[1]):
            load_sems = [own_sems.at[wholes_count + next(loads)] for _ in range(SIDES)]
            chains.append(
                scatter_chain(
                    copies, where, depth, grads[at], totals[at], buffers, load_sems, start, width
                )
            )
    run_waves(chains)
    for at in range(wholes_count):
        copies.arrived(slots[at], pieces[at].at[1 - x], x_peer)
        kept[at].wait()
    copies.finish()


def scatter_buffers(depth, rows, width):
    shapes = [
        (SIDES, depth, 2, rows, width),
        (SIDES, depth, 2, rows, width),
        (depth, 2, rows, width),
        (SIDES, depth, rows, width),
        (depth, rows, width),
        (depth - 1, rows, width),
    ]
    return [pltpu.VMEM(shape, jnp.bfloat16) for shape in shapes]


def scatter_grads(grads, wholes, depth):
    chunks = sum(len(chunks_of(grad[0].shape[4])) for grad in grads)
    copies = (depth + 5) * chunks + len(wholes)
    scratch = []
    for grad in grads:
        scratch += scatter_buffers(depth, grad[0].shape[3], grad[0].shape[4])
    return pl.pallas_call(
        functools.partial(scatter_kernel, depth, len(grads), len(wholes)),
        in_specs=[ANY] * SIDES * len(grads) + [IN_VMEM] * len(wholes),
        out_specs=[IN_VMEM] * len(grads) + [ANY] * len(wholes),
        out_shape=[jax.ShapeDtypeStruct(grad[0].shape[3:], jnp.float32) for grad in grads]
        + [
            jax.ShapeDtypeStruct((SIDES, whole.shape[0], whole.shape[1] // SIDES), whole.dtype)
            for whole in wholes
        ],
        scratch_shapes=scratch
        + [
            pltpu.SemaphoreType.DMA((copies,)),
            pltpu.SemaphoreType.DMA((copies,)),
            pltpu.SemaphoreType.DMA((SIDES * chunks + len(wholes),)),
        ],
        compiler_params=pltpu.CompilerParams(
            collective_id=2, has_side_effects=True, vmem_limit_bytes=60 * 2**20
        ),
        name="scatter_grads",
    )(*[half for grad in grads for half in grad], *wholes)


def to_image(piece):
    col = lax.axis_index("col")
    rows = piece.shape[0] // 2
    kept = lax.dynamic_slice_in_dim(piece, col * rows, rows, 0)
    sent = lax.dynamic_slice_in_dim(piece, (1 - col) * rows, rows, 0)
    other = lax.ppermute(sent, "col", [(0, 1), (1, 0)])
    return jnp.where(
        col == 0, jnp.concatenate([kept, other], 1), jnp.concatenate([other, kept], 1)
    )


def from_image(whole):
    col = lax.axis_index("col")
    width = whole.shape[1] // 2
    kept = lax.dynamic_slice_in_dim(whole, col * width, width, 1)
    sent = lax.dynamic_slice_in_dim(whole, (1 - col) * width, width, 1)
    other = lax.ppermute(sent, "col", [(0, 1), (1, 0)])
    return jnp.where(
        col == 0, jnp.concatenate([kept, other], 0), jnp.concatenate([other, kept], 0)
    )


def product(left, right, left_at, right_at):
    return lax.dot_general(
        left, right, (((left_at,), (right_at,)), ((), ())), preferred_element_type=jnp.float32
    )


def norm_back(upstream, scaled, inverse, gain_row):
    scaled_grad = upstream * gain_row
    first_mean = jnp.mean(scaled_grad, -1, keepdims=True)
    second_mean = jnp.mean(scaled_grad * scaled, -1, keepdims=True)
    return inverse * (scaled_grad - first_mean - scaled * second_mean)


def group_order(block):
    rows = block.shape[0]
    return block.reshape(rows, 3, -1, GROUP).transpose(0, 2, 1, 3).reshape(rows, -1)


def part_order(block):
    rows = block.shape[0]
    return block.reshape(rows, -1, 3, GROUP).transpose(0, 2, 1, 3).reshape(rows, 3, -1)


def image_shards(
    tokens,
    first_gain,
    first_shift,
    mixer_weight,
    mixer_bias,
    merge_weight,
    merge_bias,
    second_gain,
    second_shift,
    expand_weight,
    expand_bias,
    reduce_weight,
    reduce_bias,
    cotangent,
):
    low = jnp.bfloat16
    cols = lax.axis_size("col")
    rows = lax.axis_size("row")
    piece = first_gain.shape[0]
    hidden_piece = expand_bias.shape[0]
    block_rows = mixer_weight.shape[0]
    vectors = jnp.concatenate(
        [
            jnp.stack(
                [
                    first_gain,
                    first_shift,
                    mixer_bias[0],
                    mixer_bias[1],
                    merge_bias,
                    second_gain,
                    second_shift,
                    reduce_bias,
                ]
            ).reshape(-1),
            expand_bias,
        ]
    ).astype(low)
    vector_rows = vectors.shape[0] // GROUP
    vector_block = jnp.pad(
        vectors.reshape(vector_rows, GROUP), ((0, block_rows - vector_rows), (0, 0))
    )
    mixer_width = 3 * mixer_weight.shape[2]
    first_block = jnp.concatenate([group_order(mixer_weight).astype(low), vector_block], 1)
    depth = rows // 4
    sides = (cols, tokens.shape[0] // cols, tokens.shape[1])
    image, mixed, merger, expander, reducer = gather_weights(
        [tokens.reshape(sides)],
        [
            first_block,
            merge_weight.astype(low).T,
            expand_weight.astype(low),
            reduce_weight.astype(low).T,
        ],
        depth,
    )
    image = jnp.concatenate([image[h] for h in range(cols)], 1)
    upstream_low = to_image(cotangent)
    mixed, merger, expander, reducer = [
        whole.reshape(cols, rows * block_rows, whole.shape[-1])
        for whole in (mixed, merger, expander, reducer)
    ]
    mixer = mixed[:, :, :mixer_width]
    spread = mixed[:, :, mixer_width:].reshape(cols, rows, block_rows, GROUP)[:, :, :vector_rows]
    spread = spread.reshape(cols, rows, -1).astype(jnp.float32).transpose(1, 0, 2)
    rows_of = spread[:, :, : 8 * piece].reshape(rows, cols, 8, piece).transpose(2, 0, 1, 3)
    rows_of = rows_of.reshape(8, -1)
    expand_shift = spread[:, :, 8 * piece :].reshape(cols, -1)
    first_gain_row, first_shift_row = rows_of[0], rows_of[1]
    query_bias, value_bias, merge_shift = rows_of[2], rows_of[3], rows_of[4]
    second_gain_row, second_shift_row, reduce_shift = rows_of[5], rows_of[6], rows_of[7]
    mixer_shift = jnp.stack(
        [
            query_bias.reshape(cols, -1, GROUP),
            jnp.zeros_like(query_bias).reshape(cols, -1, GROUP),
            value_bias.reshape(cols, -1, GROUP),
        ],
        2,
    ).reshape(cols, -1)

    inputs = image.astype(jnp.float32)
    first_scaled, first_inverse, first_normed = normalize(inputs, first_gain_row, first_shift_row)
    first_low = first_normed.astype(low)
    projected = jnp.stack(
        [(product(first_low, mixer[h], 1, 0) + mixer_shift[h]).astype(low) for h in range(cols)]
    )
    attended = attention_forward(projected)
    merged = sum(product(attended[h], merger[h], 1, 1) for h in range(cols))
    hidden = inputs + merged + merge_shift
    second_scaled, second_inverse, second_normed = normalize(
        hidden, second_gain_row, second_shift_row
    )
    second_low = second_normed.astype(low)
    expanded = [product(second_low, expander[h], 1, 0) + expand_shift[h] for h in range(cols)]
    activated = [quick_gelu(part).astype(low) for part in expanded]
    reduced = sum(product(activated[h], reducer[h], 1, 1) for h in range(cols))
    layer_output = from_image((hidden + reduced + reduce_shift).astype(low))

    upstream = upstream_low.astype(jnp.float32)
    reducer_grad = [product(upstream_low, activated[h], 0, 0).astype(low) for h in range(cols)]
    expanded_grad = [
        (product(upstream_low, reducer[h], 1, 0) * gelu_slope(expanded[h])).astype(low)
        for h in range(cols)
    ]
    expander_grad = [product(second_low, expanded_grad[h], 0, 0).astype(low) for h in range(cols)]
    expand_shift_grad = [jnp.sum(part.astype(jnp.float32), 0) for part in expanded_grad]
    second_grad = sum(product(expanded_grad[h], expander[h], 1, 1) for h in range(cols))
    hidden_grad = upstream + norm_back(
        second_grad, second_scaled, second_inverse, second_gain_row
    )
    hidden_low = hidden_grad.astype(low)
    merger_grad = [product(hidden_low, attended[h], 0, 0).astype(low) for h in range(cols)]
    attended_grad = jnp.stack(
        [product(hidden_low, merger[h], 1, 0).astype(low) for h in range(cols)]
    )
    projected_grad = attention_back(projected, attended_grad)
    mixer_grad = [product(first_low, projected_grad[h], 0, 0).astype(low) for h in range(cols)]
    bias_sums = jnp.sum(projected_grad.astype(jnp.float32), 1)
    bias_sums = bias_sums.reshape(cols, -1, 3, GROUP).transpose(2, 0, 1, 3).reshape(3, -1)
    first_grad = sum(product(projected_grad[h], mixer[h], 1, 1) for h in range(cols))
    input_grad = hidden_grad + norm_back(first_grad, first_scaled, first_inverse, first_gain_row)
    vector_grads = jnp.stack(
        [
            jnp.sum(first_grad * first_scaled, 0),
            jnp.sum(first_grad, 0),
            bias_sums[0],
            bias_sums[2],
            jnp.sum(hidden_grad, 0),
            jnp.sum(second_grad * second_scaled, 0),
            jnp.sum(second_grad, 0),
            jnp.sum(upstream, 0),
        ]
    )
    vector_grads = vector_grads.reshape(8, rows, cols, piece).transpose(2, 1, 0, 3)
    hidden_grads = jnp.concatenate(expand_shift_grad).reshape(rows, cols, hidden_piece)
    vector_grads = jnp.concatenate(
        [vector_grads.reshape(cols, rows, -1), hidden_grads.transpose(1, 0, 2)], 2
    )
    vector_grads = vector_grads.reshape(cols, rows, vector_rows, GROUP).astype(low)
    vector_grads = jnp.pad(
        vector_grads, ((0, 0), (0, 0), (0, block_rows - vector_rows), (0, 0))
    ).reshape(cols, rows * block_rows, GROUP)
    mixed_grad = [jnp.concatenate([mixer_grad[h], vector_grads[h]], 1) for h in range(cols)]
    grads = [
        [part.reshape(depth, 2, 2, block_rows, -1) for part in halves]
        for halves in (reducer_grad, expander_grad, merger_grad, mixed_grad)
    ]
    reduce_total, expand_total, merge_total, mixed_total, tokens_gradient = (
        scatter_grads(grads, [input_grad.astype(low)], depth)
    )
    tokens_gradient = tokens_gradient.reshape(tokens.shape).astype(jnp.float32)
    mixer_total = part_order(mixed_total[:, :mixer_width])
    vector_total = mixed_total[:vector_rows, mixer_width:].reshape(-1)
    small = vector_total[: 8 * piece].reshape(8, piece)
    return (
        layer_output,
        tokens_gradient,
        small[0],
        small[1],
        mixer_total,
        small[2:4],
        merge_total.T,
        small[4],
        small[5],
        small[6],
        expand_total,
        vector_total[8 * piece :],
        reduce_total.T,
        small[7],
    )


def solution(mesh):
    def body(*arguments):
        images = arguments[0].shape[0] // SEQ
        whole = images == 2 and lax.axis_size("col") == 2
        return (image_shards if whole else split_shards)(*arguments)

    return jax.shard_map(
        body,
        mesh=mesh,
        in_specs=(
            P("row", "col"),
            P(("row", "col")),
            P(("row", "col")),
            P("row", None, "col"),
            P(None, ("row", "col")),
            P("col", "row"),
            P(("row", "col")),
            P(("row", "col")),
            P(("row", "col")),
            P("row", "col"),
            P(("row", "col")),
            P("col", "row"),
            P(("row", "col")),
            P("row", "col"),
        ),
        out_specs=(
            P("row", "col"),
            P("row", "col"),
            P(("row", "col")),
            P(("row", "col")),
            P("row", None, "col"),
            P(None, ("row", "col")),
            P("col", "row"),
            P(("row", "col")),
            P(("row", "col")),
            P(("row", "col")),
            P("row", "col"),
            P(("row", "col")),
            P("col", "row"),
            P(("row", "col")),
        ),
        check_vma=False,
    )
```

```python
import functools

import jax
import jax.numpy as jnp
from jax import lax
from jax.experimental import pallas as pl
from jax.experimental.pallas import tpu as pltpu
from jax.sharding import PartitionSpec as P

HEAD_DIM = 64
SEQ = 577


EPSILON = 1e-05
SLOPE = 1.702


def quick_gelu(inputs):
    return inputs * jax.nn.sigmoid(SLOPE * inputs)


def gelu_slope(inputs):
    sigmoid_value = jax.nn.sigmoid(SLOPE * inputs)
    return sigmoid_value + SLOPE * inputs * sigmoid_value * (1.0 - sigmoid_value)


def own_columns(values, start, width):
    return lax.dynamic_slice_in_dim(values, start, width, values.ndim - 1)


def normalize(values, gain_row, shift_row):
    feature_count = values.shape[-1]
    row_mean = jnp.sum(values, -1, keepdims=True) / feature_count
    square = jnp.sum(values * values, -1, keepdims=True) / feature_count
    inverse = lax.rsqrt(square - row_mean * row_mean + EPSILON)
    scaled = (values - row_mean) * inverse
    return (scaled, inverse, scaled * gain_row + shift_row)


def column_sum(partial_value):
    return lax.psum_scatter(
        partial_value.astype(jnp.bfloat16), "col", scatter_dimension=1, tiled=True
    ).astype(jnp.float32)


def feature_totals(first_sum, second_sum):
    return lax.psum((first_sum, second_sum), "col")


def normed_gather(piece):
    return lax.all_gather(piece, "col", axis=1, tiled=True)


def shared_back(upstream, scaled, inverse, gain_row, feature_count):
    scaled_grad = upstream * gain_row
    totals = feature_totals(jnp.sum(scaled_grad, -1), jnp.sum(scaled_grad * scaled, -1))
    first_mean = totals[0][:, None] / feature_count
    second_mean = totals[1][:, None] / feature_count
    return inverse * (scaled_grad - first_mean - scaled * second_mean)


def fetch_weights(masters):
    return (
        lax.all_gather(masters[0], "row", axis=0, tiled=True),
        lax.all_gather(masters[1], "row", axis=1, tiled=True),
        lax.all_gather(masters[2], "row", axis=0, tiled=True),
        lax.all_gather(masters[3], "row", axis=1, tiled=True),
    )


def attend_forward(parts):
    queries, key_rows, values = parts
    score_scale = queries.shape[-1] ** (-0.5)
    scores = (
        jnp.einsum("qhd,khd->hqk", queries, key_rows, preferred_element_type=jnp.float32)
        * score_scale
    )
    score_top = jnp.max(scores, -1, keepdims=True)
    exponent = jnp.exp(scores - score_top)
    row_total = jnp.sum(exponent, -1, keepdims=True)
    weights = (exponent / row_total).astype(jnp.bfloat16)
    mixture = jnp.einsum("hqk,khd->qhd", weights, values, preferred_element_type=jnp.float32)
    return (mixture.astype(jnp.bfloat16), (score_top + jnp.log(row_total))[..., 0])


def attend_back(parts):
    queries, key_rows, values, log_total, upstream = parts
    score_scale = queries.shape[-1] ** (-0.5)
    scores = (
        jnp.einsum("qhd,khd->hqk", queries, key_rows, preferred_element_type=jnp.float32)
        * score_scale
    )
    probability = jnp.exp(scores - log_total[..., None])
    rounded = probability.astype(jnp.bfloat16)
    pulled = jnp.einsum("qhd,khd->hqk", upstream, values, preferred_element_type=jnp.float32)
    centre = jnp.sum(probability * pulled, -1, keepdims=True)
    score_grad = (probability * (pulled - centre)).astype(jnp.bfloat16)
    query_grad = (
        jnp.einsum("hqk,khd->qhd", score_grad, key_rows, preferred_element_type=jnp.float32)
        * score_scale
    )
    key_grad = (
        jnp.einsum("hqk,qhd->khd", score_grad, queries, preferred_element_type=jnp.float32)
        * score_scale
    )
    value_grad = jnp.einsum("hqk,qhd->khd", rounded, upstream, preferred_element_type=jnp.float32)
    return (query_grad, key_grad, value_grad)


def split_shards(
    tokens,
    first_gain,
    first_shift,
    mixer_weight,
    mixer_bias,
    merge_weight,
    merge_bias,
    second_gain,
    second_shift,
    expand_weight,
    expand_bias,
    reduce_weight,
    reduce_bias,
    cotangent,
):
    col_index = lax.axis_index("col")
    piece_width = tokens.shape[1]
    hidden_width = expand_weight.shape[1]
    start = col_index * piece_width
    hidden_start = col_index * hidden_width
    vector_pieces = jnp.stack(
        [
            first_gain,
            first_shift,
            mixer_bias[0],
            mixer_bias[1],
            merge_bias,
            second_gain,
            second_shift,
            reduce_bias,
        ]
    ).astype(jnp.bfloat16)
    vectors_low, expand_shift_low = (
        lax.all_gather(vector_pieces, ("row", "col"), axis=1, tiled=True),
        lax.all_gather(expand_bias.astype(jnp.bfloat16), ("row", "col"), axis=0, tiled=True),
    )
    vectors = vectors_low.astype(jnp.float32)
    feature_count = vectors.shape[1]
    first_gain_row, first_shift_row = (vectors[0], vectors[1])
    query_bias = own_columns(vectors[2], start, piece_width)
    value_bias = own_columns(vectors[3], start, piece_width)
    merge_shift = vectors[4]
    second_gain_row, second_shift_row = (vectors[5], vectors[6])
    reduce_shift = own_columns(vectors[7], start, piece_width)
    expand_shift = own_columns(expand_shift_low.astype(jnp.float32), hidden_start, hidden_width)
    masters = (
        mixer_weight.astype(jnp.bfloat16),
        merge_weight.astype(jnp.bfloat16),
        expand_weight.astype(jnp.bfloat16),
        reduce_weight.astype(jnp.bfloat16),
    )
    mixer_local, merger, expander, reducer = fetch_weights(masters)
    inputs_whole, upstream_whole = (
        lax.all_gather(tokens, "col", axis=1, tiled=True),
        lax.all_gather(cotangent, "col", axis=1, tiled=True),
    )
    inputs = inputs_whole.astype(jnp.float32)
    row_count = inputs.shape[0]
    first_scaled, first_inverse, first_normed = normalize(inputs, first_gain_row, first_shift_row)
    first_low = first_normed.astype(jnp.bfloat16)
    projected = jnp.einsum(
        "rd,dtc->rtc", first_low, mixer_local, preferred_element_type=jnp.float32
    )
    projected = projected + jnp.stack([query_bias, jnp.zeros_like(query_bias), value_bias])
    projected_low = projected.astype(jnp.bfloat16)
    head_shape = (row_count // SEQ, SEQ, piece_width // HEAD_DIM, HEAD_DIM)
    queries = projected_low[:, 0].reshape(head_shape)
    key_rows = projected_low[:, 1].reshape(head_shape)
    values = projected_low[:, 2].reshape(head_shape)
    attended, log_total = lax.map(attend_forward, (queries, key_rows, values))
    attended = attended.reshape(row_count, piece_width)
    merged_part = jnp.dot(attended, merger, preferred_element_type=jnp.float32)
    hidden_own = (
        own_columns(inputs, start, piece_width)
        + column_sum(merged_part)
        + own_columns(merge_shift, start, piece_width)
    )
    totals = feature_totals(jnp.sum(hidden_own, -1), jnp.sum(hidden_own * hidden_own, -1))
    row_mean = totals[0][:, None] / feature_count
    square = totals[1][:, None] / feature_count
    second_inverse = lax.rsqrt(square - row_mean * row_mean + EPSILON)
    second_scaled = (hidden_own - row_mean) * second_inverse
    second_gain_own = own_columns(second_gain_row, start, piece_width)
    second_piece = second_scaled * second_gain_own + own_columns(
        second_shift_row, start, piece_width
    )
    second_low = normed_gather(second_piece.astype(jnp.bfloat16))
    expanded = jnp.dot(second_low, expander, preferred_element_type=jnp.float32) + expand_shift
    activated = quick_gelu(expanded).astype(jnp.bfloat16)
    reduced = column_sum(jnp.dot(activated, reducer, preferred_element_type=jnp.float32))
    layer_output = (hidden_own + reduced + reduce_shift).astype(jnp.bfloat16)
    masters_again = lax.optimization_barrier((masters, layer_output))[0]
    mixer_local, merger, expander, reducer = fetch_weights(masters_again)
    upstream_own = cotangent.astype(jnp.float32)
    reducer_grad = jnp.einsum(
        "rf,rd->fd", activated, upstream_whole, preferred_element_type=jnp.float32
    )
    activated_grad = jnp.einsum(
        "rd,fd->rf", upstream_whole, reducer, preferred_element_type=jnp.float32
    )
    expanded_grad = (activated_grad * gelu_slope(expanded)).astype(jnp.bfloat16)
    expander_grad = jnp.einsum(
        "rd,rf->df", second_low, expanded_grad, preferred_element_type=jnp.float32
    )
    expand_shift_grad = jnp.sum(expanded_grad.astype(jnp.float32), 0)
    second_part = jnp.einsum(
        "rf,df->rd", expanded_grad, expander, preferred_element_type=jnp.float32
    )
    second_grad = column_sum(second_part)
    hidden_part = shared_back(
        second_grad, second_scaled, second_inverse, second_gain_own, feature_count
    )
    hidden_grad = upstream_own + hidden_part
    second_gain_grad = jnp.sum(second_grad * second_scaled, 0)
    second_shift_grad = jnp.sum(second_grad, 0)
    hidden_low = normed_gather(hidden_grad.astype(jnp.bfloat16))
    merger_grad = jnp.einsum("rc,rd->cd", attended, hidden_low, preferred_element_type=jnp.float32)
    attended_grad = jnp.einsum(
        "rd,cd->rc", hidden_low, merger, preferred_element_type=jnp.float32
    ).astype(jnp.bfloat16)
    query_grad, key_grad, value_grad = lax.map(
        attend_back, (queries, key_rows, values, log_total, attended_grad.reshape(head_shape))
    )
    projected_grad = jnp.stack(
        [
            query_grad.reshape(row_count, piece_width),
            key_grad.reshape(row_count, piece_width),
            value_grad.reshape(row_count, piece_width),
        ],
        1,
    ).astype(jnp.bfloat16)
    mixer_grad = jnp.einsum(
        "rd,rtc->dtc", first_low, projected_grad, preferred_element_type=jnp.float32
    )
    bias_sums = jnp.sum(projected_grad.astype(jnp.float32), 0)
    first_part = jnp.einsum(
        "rtc,dtc->rd", projected_grad, mixer_local, preferred_element_type=jnp.float32
    )
    first_grad = column_sum(first_part)
    first_scaled_own = own_columns(first_scaled, start, piece_width)
    input_part = shared_back(
        first_grad,
        first_scaled_own,
        first_inverse,
        own_columns(first_gain_row, start, piece_width),
        feature_count,
    )
    tokens_gradient = hidden_grad + input_part
    own_vector_grads = jnp.stack(
        [
            jnp.sum(first_grad * first_scaled_own, 0),
            jnp.sum(first_grad, 0),
            bias_sums[0],
            bias_sums[2],
            jnp.sum(hidden_grad, 0),
            second_gain_grad,
            second_shift_grad,
            jnp.sum(upstream_own, 0),
        ]
    )
    vector_whole = lax.dynamic_update_slice(
        jnp.zeros((8, feature_count), jnp.float32), own_vector_grads, (jnp.int32(0), start)
    )
    expand_whole = lax.dynamic_update_slice(
        jnp.zeros((hidden_width * lax.axis_size("col"),), jnp.float32),
        expand_shift_grad,
        (hidden_start,),
    )
    vector_total, expand_bias_total = (
        lax.psum_scatter(vector_whole, ("row", "col"), scatter_dimension=1, tiled=True),
        lax.psum_scatter(expand_whole, ("row", "col"), scatter_dimension=0, tiled=True),
    )
    mixer_total, merge_total, expand_total, reduce_total = (
        lax.psum_scatter(
            mixer_grad.astype(jnp.bfloat16), "row", scatter_dimension=0, tiled=True
        ).astype(jnp.float32),
        lax.psum_scatter(
            merger_grad.astype(jnp.bfloat16), "row", scatter_dimension=1, tiled=True
        ).astype(jnp.float32),
        lax.psum_scatter(
            expander_grad.astype(jnp.bfloat16), "row", scatter_dimension=0, tiled=True
        ).astype(jnp.float32),
        lax.psum_scatter(
            reducer_grad.astype(jnp.bfloat16), "row", scatter_dimension=1, tiled=True
        ).astype(jnp.float32),
    )
    return (
        layer_output,
        tokens_gradient,
        vector_total[0],
        vector_total[1],
        mixer_total,
        jnp.stack([vector_total[2], vector_total[3]]),
        merge_total,
        vector_total[4],
        vector_total[5],
        vector_total[6],
        expand_total,
        expand_bias_total,
        reduce_total,
        vector_total[7],
    )


GROUP = 128


def attention_forward_kernel(projected_ref, attended_ref):
    for head in range(GROUP // HEAD_DIM):
        at = head * HEAD_DIM
        queries = projected_ref[0, :, at : at + HEAD_DIM] * jnp.bfloat16(HEAD_DIM**-0.5)
        key_rows = projected_ref[0, :, GROUP + at : GROUP + at + HEAD_DIM]
        values = projected_ref[0, :, 2 * GROUP + at : 2 * GROUP + at + HEAD_DIM]
        scores = lax.dot_general(
            key_rows, queries, (((1,), (1,)), ((), ())), preferred_element_type=jnp.float32
        )
        exponent = jnp.exp(scores - jnp.max(scores, 0, keepdims=True))
        weights = exponent * (1.0 / jnp.sum(exponent, 0, keepdims=True))
        mixture = lax.dot_general(
            values,
            weights.astype(jnp.bfloat16),
            (((0,), (0,)), ((), ())),
            preferred_element_type=jnp.float32,
        )
        attended_ref[0, :, at : at + HEAD_DIM] = mixture.T.astype(jnp.bfloat16)


def attention_back_kernel(projected_ref, upstream_ref, grad_ref):
    for head in range(GROUP // HEAD_DIM):
        at = head * HEAD_DIM
        queries = projected_ref[0, :, at : at + HEAD_DIM] * jnp.bfloat16(HEAD_DIM**-0.5)
        key_rows = projected_ref[0, :, GROUP + at : GROUP + at + HEAD_DIM]
        values = projected_ref[0, :, 2 * GROUP + at : 2 * GROUP + at + HEAD_DIM]
        upstream = upstream_ref[0, :, at : at + HEAD_DIM]
        scores = lax.dot_general(
            key_rows, queries, (((1,), (1,)), ((), ())), preferred_element_type=jnp.float32
        )
        exponent = jnp.exp(scores - jnp.max(scores, 0, keepdims=True))
        weights = exponent * (1.0 / jnp.sum(exponent, 0, keepdims=True))
        pulled = lax.dot_general(
            values, upstream, (((1,), (1,)), ((), ())), preferred_element_type=jnp.float32
        )
        centre = jnp.sum(weights * pulled, 0, keepdims=True)
        score_grad = (weights * (pulled - centre)).astype(jnp.bfloat16)
        value_grad = jnp.dot(
            weights.astype(jnp.bfloat16), upstream, preferred_element_type=jnp.float32
        )
        key_grad = jnp.dot(score_grad, queries, preferred_element_type=jnp.float32)
        query_grad = lax.dot_general(
            key_rows, score_grad, (((0,), (0,)), ((), ())), preferred_element_type=jnp.float32
        )
        query_grad = query_grad.T * HEAD_DIM**-0.5
        grad_ref[0, :, at : at + HEAD_DIM] = query_grad.astype(jnp.bfloat16)
        grad_ref[0, :, GROUP + at : GROUP + at + HEAD_DIM] = key_grad.astype(jnp.bfloat16)
        grad_ref[0, :, 2 * GROUP + at : 2 * GROUP + at + HEAD_DIM] = value_grad.astype(
            jnp.bfloat16
        )


def attention_forward(projected):
    halves, rows, width = projected.shape
    groups = width // (3 * GROUP)
    return pl.pallas_call(
        attention_forward_kernel,
        grid=(halves, groups),
        in_specs=[pl.BlockSpec((1, rows, 3 * GROUP), lambda h, g: (h, 0, g))],
        out_specs=pl.BlockSpec((1, rows, GROUP), lambda h, g: (h, 0, g)),
        out_shape=jax.ShapeDtypeStruct((halves, rows, groups * GROUP), jnp.bfloat16),
        name="attention_forward",
    )(projected)


def attention_back(projected, upstream):
    halves, rows, width = projected.shape
    groups = width // (3 * GROUP)
    return pl.pallas_call(
        attention_back_kernel,
        grid=(halves, groups),
        in_specs=[
            pl.BlockSpec((1, rows, 3 * GROUP), lambda h, g: (h, 0, g)),
            pl.BlockSpec((1, rows, GROUP), lambda h, g: (h, 0, g)),
        ],
        out_specs=pl.BlockSpec((1, rows, 3 * GROUP), lambda h, g: (h, 0, g)),
        out_shape=jax.ShapeDtypeStruct(projected.shape, jnp.bfloat16),
        name="attention_back",
    )(projected, upstream)


MESH = pl.DeviceIdType.MESH
ANY = pl.BlockSpec(memory_space=pl.ANY)
IN_VMEM = pl.BlockSpec(memory_space=pltpu.VMEM)
SIDES = 2
BUFFERS = 6
SLOTS = 4
CHUNK = 4
AHEAD = 12
SPACING = 2


def place():
    col = lax.axis_index("col")
    row = lax.axis_index("row")
    return col, lax.div(row, 4), lax.rem(lax.div(row, 2), 2), lax.rem(row, 2)


def device_of(x, z, y, core):
    return (z * 4 + y * 2 + core, x)


def greet(x, z, y, core, depth):
    barrier = pltpu.get_barrier_semaphore()
    others = [device_of(x, lax.rem(z + k, depth), y, core) for k in range(1, depth)]
    others += [
        device_of(x, z, 1 - y, core),
        device_of(1 - x, z, y, core),
        device_of(x, z, y, 1 - core),
    ]
    for other in others:
        pl.semaphore_signal(barrier, inc=1, device_id=other, device_id_type=MESH)
    pl.semaphore_wait(barrier, len(others))


def split_width(width):
    return width // GROUP // 2 * GROUP


def chunks_of(width):
    tiles = width // GROUP
    count = max(tiles // CHUNK, 1)
    edges = [CHUNK * GROUP * at for at in range(count)] + [width]
    return [(edges[at], edges[at + 1] - edges[at]) for at in range(count)]


class Copies:
    def __init__(self, send_sems, recv_sems):
        self.send_sems, self.recv_sems, self.count, self.sent = send_sems, recv_sems, 0, []

    def slot(self):
        self.count += 1
        return self.count - 1

    def send(self, slot, source, target, device, keep=True):
        copy = pltpu.make_async_remote_copy(
            src_ref=source,
            dst_ref=target,
            send_sem=self.send_sems.at[slot],
            recv_sem=self.recv_sems.at[slot],
            device_id=device,
            device_id_type=MESH,
        )
        copy.start()
        if keep:
            self.sent.append(copy)
        return copy

    def arrived(self, slot, target, device):
        pltpu.make_async_remote_copy(
            src_ref=target,
            dst_ref=target,
            send_sem=self.send_sems.at[slot],
            recv_sem=self.recv_sems.at[slot],
            device_id=device,
            device_id_type=MESH,
        ).wait_recv()

    def finish(self):
        for copy in self.sent:
            copy.wait_send()


def run_waves(chains, ahead):
    stages = len(chains[0])
    count = len(chains)
    for at in range(min(ahead, count)):
        chains[at][0]()
    for wave in range(1, count + SPACING * (stages - 1)):
        if wave + ahead - 1 < count:
            chains[wave + ahead - 1][0]()
        for stage in range(stages - 1, 0, -1):
            at = wave - 1 - SPACING * (stage - 1)
            if 0 <= at < count:
                chains[at][stage]()


def gather_chain(copies, where, depth, block, whole, local, start, width):
    x, z, y, core = where
    first = split_width(width)
    every = pl.ds(start, width)
    a, b = pl.ds(start, first), pl.ds(start + first, width - first)
    x_peer = device_of(1 - x, z, y, core)
    y_peer = device_of(x, z, 1 - y, core)
    partner = device_of(x, z, y, 1 - core)
    steps = range(1, depth)
    z_peers = [device_of(x, lax.rem(z + k, depth), y, core) for k in steps]
    z_from = [lax.rem(z + depth - k, depth) for k in steps]
    along = [copies.slot() for _ in steps]
    ay, ax, bx, by = [copies.slot() for _ in range(4)]
    shared = [copies.slot() for _ in range(5)]

    def share(slot, target):
        copies.send(slot, target, target, partner)

    def begin():
        mine = whole.at[x, z, y, core]
        for k in range(depth - 1):
            copies.send(along[k], block.at[:, every], mine.at[:, every], z_peers[k])

    def second():
        if local is not None:
            local.wait()
        for k in range(depth - 1):
            copies.arrived(along[k], whole.at[x, z_from[k], y, core, :, every], z_peers[k])
        for slot, part, peer in ((ay, a, y_peer), (bx, b, x_peer)):
            column = whole.at[x, :, y, core, :, part]
            copies.send(slot, column, column, peer)
        share(shared[0], whole.at[x, :, y, core, :, every])

    def third():
        copies.arrived(ay, whole.at[x, :, 1 - y, core, :, a], y_peer)
        plane = whole.at[x, :, :, core, :, a]
        copies.send(ax, plane, plane, x_peer)
        copies.arrived(bx, whole.at[1 - x, :, y, core, :, b], x_peer)
        sheet = whole.at[:, :, y, core, :, b]
        copies.send(by, sheet, sheet, y_peer)
        share(shared[1], whole.at[x, :, 1 - y, core, :, a])
        share(shared[2], whole.at[1 - x, :, y, core, :, b])

    def fourth():
        copies.arrived(ax, whole.at[1 - x, :, :, core, :, a], x_peer)
        share(shared[3], whole.at[1 - x, :, :, core, :, a])
        copies.arrived(by, whole.at[:, :, 1 - y, core, :, b], y_peer)
        share(shared[4], whole.at[:, :, 1 - y, core, :, b])

    def last():
        other = 1 - core
        copies.arrived(shared[0], whole.at[x, :, y, other, :, every], partner)
        copies.arrived(shared[1], whole.at[x, :, 1 - y, other, :, a], partner)
        copies.arrived(shared[2], whole.at[1 - x, :, y, other, :, b], partner)
        copies.arrived(shared[3], whole.at[1 - x, :, :, other, :, a], partner)
        copies.arrived(shared[4], whole.at[:, :, 1 - y, other, :, b], partner)

    return begin, second, third, fourth, last


def gather_kernel(depth, pieces_count, *refs):
    count = (len(refs) - 3 - 2 * pieces_count) // 2
    pieces, blocks = refs[:pieces_count], refs[pieces_count : pieces_count + count]
    outs = refs[pieces_count + count : -3]
    images, wholes = outs[:pieces_count], outs[pieces_count:]
    send_sems, recv_sems, own_sems = refs[-3:]
    where = place()
    x, z, y, core = where
    copies = Copies(send_sems, recv_sems)
    local = [
        pltpu.make_async_copy(block, whole.at[x, z, y, core], own_sems.at[at])
        for at, (block, whole) in enumerate(zip(blocks, wholes))
    ]
    kept = [
        pltpu.make_async_copy(piece.at[x], image.at[x], own_sems.at[count + at])
        for at, (piece, image) in enumerate(zip(pieces, images))
    ]
    for copy in local + kept:
        copy.start()
    greet(*where, depth)
    chains = []
    for block, whole, copy in zip(blocks, wholes, local):
        for start, width in chunks_of(block.shape[1]):
            once = copy if start == 0 else None
            chains.append(gather_chain(copies, where, depth, block, whole, once, start, width))
    slots = []
    x_peer = device_of(1 - x, z, y, core)
    for at in range(pieces_count):
        slots.append(copies.slot())
        copies.send(slots[at], pieces[at].at[1 - x], images[at].at[x], x_peer)
    run_waves(chains, AHEAD)
    for at in range(pieces_count):
        copies.arrived(slots[at], images[at].at[1 - x], x_peer)
        kept[at].wait()
    copies.finish()


def gather_weights(pieces, blocks, depth):
    chunks = sum(len(chunks_of(block.shape[1])) for block in blocks)
    copies = (depth + 8) * chunks + len(pieces)
    return pl.pallas_call(
        functools.partial(gather_kernel, depth, len(pieces)),
        in_specs=[IN_VMEM] * (len(pieces) + len(blocks)),
        out_specs=[ANY] * (len(pieces) + len(blocks)),
        out_shape=[jax.ShapeDtypeStruct(piece.shape, piece.dtype) for piece in pieces]
        + [
            jax.ShapeDtypeStruct((SIDES, depth, 2, 2) + block.shape, block.dtype)
            for block in blocks
        ],
        scratch_shapes=[
            pltpu.SemaphoreType.DMA((copies,)),
            pltpu.SemaphoreType.DMA((copies,)),
            pltpu.SemaphoreType.DMA((len(pieces) + len(blocks),)),
        ],
        compiler_params=pltpu.CompilerParams(collective_id=1, has_side_effects=True),
        name="gather_weights",
    )(*pieces, *blocks)


def add_blocks(count, target, term):
    @pl.loop(0, count)
    def _(at):
        total = target(at)[...].astype(jnp.float32) + term(at)[...].astype(jnp.float32)
        target(at)[...] = total.astype(jnp.bfloat16)


class Loaded:
    def __init__(self, copies, core, grad, own, sems, start, width):
        self.copies, self.core, self.grad, self.own_ref = copies, core, grad, own
        self.every = pl.ds(start, width)
        self.loads = [
            pltpu.make_async_copy(
                grad[side].at[:, :, core, :, self.every],
                own.at[side, :, :, :, self.every],
                sems[side],
            )
            for side in range(SIDES)
        ]

    def prepare(self):
        for load in self.loads:
            load.start()

    def give(self, slot, side, target, partner):
        source = self.grad[side].at[:, :, 1 - self.core, :, self.every]
        self.copies.send(slot, source, target, partner)

    def ready(self):
        for load in self.loads:
            load.wait()

    def own(self, side, z, y):
        return self.own_ref.at[side, z, y, :, self.every]


class Computed:
    def __init__(self, copies, core, left, right, ring, flying, order, start, width):
        self.copies, self.core, self.left, self.right = copies, core, left, right
        self.ring, self.flying, self.slot = ring, flying, order % SLOTS
        self.every = pl.ds(start, width)

    def prepare(self):
        for copy in self.flying.pop(self.slot, ()):
            copy.wait_send()
        depth, rows, width = self.ring.shape[3], self.ring.shape[5], self.ring.shape[6]
        span = depth // 2
        block = span * 2 * rows

        @pl.loop(0, SIDES * 2 * 2)
        def _(at):
            who, side, half = lax.div(at, 4), lax.rem(lax.div(at, 2), 2), lax.rem(at, 2)
            left = self.left[
                lax.rem(self.core + who, 2), pl.ds(pl.multiple_of(half * block, block), block), :
            ]
            right = self.right[side, :, self.every]
            result = jnp.dot(left, right, preferred_element_type=jnp.float32)
            self.ring[self.slot, who, side, pl.ds(half * span, span)] = result.astype(
                jnp.bfloat16
            ).reshape(span, 2, rows, width)

    def give(self, slot, side, target, partner):
        copy = self.copies.send(slot, self.ring.at[self.slot, 1, side], target, partner, False)
        self.flying.setdefault(self.slot, []).append(copy)

    def ready(self):
        pass

    def own(self, side, z, y):
        return self.ring.at[self.slot, 0, side, z, y]


def scatter_chain(copies, where, depth, source, total, buffers, start, width):
    x, z, y, core = where
    halves, ax_in, by_in, along, along_in = buffers
    first = split_width(width)
    every = pl.ds(start, width)
    a, b = pl.ds(start, first), pl.ds(start + first, width - first)
    x_peer = device_of(1 - x, z, y, core)
    y_peer = device_of(x, z, 1 - y, core)
    partner = device_of(x, z, y, 1 - core)
    steps = range(1, depth)
    z_to = [lax.rem(z + k, depth) for k in steps]
    z_peers = [device_of(x, at, y, core) for at in z_to]
    pair = [copies.slot() for _ in range(SIDES)]
    ax, ay, bx, by = [copies.slot() for _ in range(4)]
    ca, cb = pl.ds(start // 2, first), pl.ds(start // 2, width - first)
    hops = [copies.slot() for _ in steps]
    def begin():
        source.prepare()
        for side in range(SIDES):
            source.give(pair[side], side, halves.at[side, :, :, :, every], partner)

    def second():
        source.ready()
        for side in range(SIDES):
            copies.arrived(pair[side], halves.at[side, :, :, :, every], partner)

        def block_at(at):
            return lax.div(at, depth * 2), lax.rem(lax.div(at, 2), depth), lax.rem(at, 2)

        add_blocks(
            SIDES * depth * 2,
            lambda at: halves.at[block_at(at) + (slice(None), every)],
            lambda at: source.own(*block_at(at)),
        )
        copies.send(ax, halves.at[1 - x, :, :, :, a], ax_in.at[:, :, :, ca], x_peer)
        copies.send(by, halves.at[:, :, 1 - y, :, b], by_in.at[:, :, :, cb], y_peer)

    def third():
        copies.arrived(ax, ax_in.at[:, :, :, ca], x_peer)
        add_blocks(
            depth * 2,
            lambda at: ax_in.at[lax.div(at, 2), lax.rem(at, 2), :, ca],
            lambda at: halves.at[x, lax.div(at, 2), lax.rem(at, 2), :, a],
        )
        copies.send(ay, ax_in.at[:, 1 - y, :, ca], along.at[:, :, a], y_peer)
        copies.arrived(by, by_in.at[:, :, :, cb], y_peer)
        add_blocks(
            SIDES * depth,
            lambda at: by_in.at[lax.div(at, depth), lax.rem(at, depth), :, cb],
            lambda at: halves.at[lax.div(at, depth), lax.rem(at, depth), y, :, b],
        )
        copies.send(bx, by_in.at[1 - x, :, :, cb], along.at[:, :, b], x_peer)

    def fourth():
        copies.arrived(ay, along.at[:, :, a], y_peer)
        add_blocks(depth, lambda at: along.at[at, :, a], lambda at: ax_in.at[at, y, :, ca])
        copies.arrived(bx, along.at[:, :, b], x_peer)
        add_blocks(depth, lambda at: along.at[at, :, b], lambda at: by_in.at[x, at, :, cb])
        for k in range(depth - 1):
            copies.send(
                hops[k], along.at[z_to[k], :, every], along_in.at[k, :, every], z_peers[k]
            )

    def last():
        for k in range(depth - 1):
            copies.arrived(hops[k], along_in.at[k, :, every], z_peers[k])
        sums = along[z, :, every].astype(jnp.float32)
        for k in range(depth - 1):
            sums += along_in[k, :, every].astype(jnp.float32)
        total[:, every] = sums

    return begin, second, third, fourth, last


def scatter_kernel(depth, count, pairs_count, wholes_count, *refs):
    def take(number):
        nonlocal refs
        taken, refs = refs[:number], refs[number:]
        return taken

    grads = [take(SIDES) for _ in range(count)]
    pairs = [take(2) for _ in range(pairs_count)]
    wholes = take(wholes_count)
    totals = take(count + pairs_count)
    pieces = take(wholes_count)
    owns = take(count)
    buffers = [take(BUFFERS - 1) for _ in totals]
    ring, send_sems, recv_sems, own_sems = refs
    where = place()
    x, z, y, core = where
    copies = Copies(send_sems, recv_sems)
    greet(*where, depth)
    x_peer = device_of(1 - x, z, y, core)
    kept = []
    slots = [copies.slot() for _ in wholes]
    for at in range(wholes_count):
        width = pieces[at].shape[2]
        mine = pl.ds(pl.multiple_of(x * width, width), width)
        theirs = pl.ds(pl.multiple_of((1 - x) * width, width), width)
        copy = pltpu.make_async_copy(wholes[at].at[:, mine], pieces[at].at[x], own_sems.at[at])
        copy.start()
        kept.append(copy)
        copies.send(slots[at], wholes[at].at[:, theirs], pieces[at].at[x], x_peer)
    chains, flying, order = [], {}, 0
    loads = iter(range(own_sems.shape[0] - wholes_count))
    for at, total in enumerate(totals):
        for start, width in chunks_of(total.shape[1]):
            if at < count:
                sems = [own_sems.at[wholes_count + next(loads)] for _ in range(SIDES)]
                source = Loaded(copies, core, grads[at], owns[at], sems, start, width)
            else:
                source = Computed(
                    copies, core, *pairs[at - count], ring, flying, order, start, width
                )
                order += 1
            chains.append(
                scatter_chain(copies, where, depth, source, total, buffers[at], start, width)
            )
    run_waves(chains, SLOTS - 1)
    for at in range(wholes_count):
        copies.arrived(slots[at], pieces[at].at[1 - x], x_peer)
        kept[at].wait()
    for flight in flying.values():
        for copy in flight:
            copy.wait_send()
    copies.finish()


def scatter_buffers(depth, rows, width):
    part = -(-width // (2 * GROUP)) * GROUP
    shapes = [
        (SIDES, depth, 2, rows, width),
        (depth, 2, rows, part),
        (SIDES, depth, rows, part),
        (depth, rows, width),
        (depth - 1, rows, width),
    ]
    return [pltpu.VMEM(shape, jnp.bfloat16) for shape in shapes]


def scatter_grads(grads, pairs, wholes, depth):
    rows = grads[0][0].shape[3]
    widths = [grad[0].shape[4] for grad in grads] + [pair[1].shape[2] for pair in pairs]
    loaded = sum(len(chunks_of(width)) for width in widths[: len(grads)])
    chunks = sum(len(chunks_of(width)) for width in widths)
    copies = (depth + 5) * chunks + len(wholes)
    scratch = [
        pltpu.VMEM((SIDES, depth, 2, rows, width), jnp.bfloat16) for width in widths[: len(grads)]
    ]
    for width in widths:
        scratch += scatter_buffers(depth, rows, width)
    scratch.append(pltpu.VMEM((SLOTS, 2, SIDES, depth, 2, rows, CHUNK * GROUP), jnp.bfloat16))
    return pl.pallas_call(
        functools.partial(scatter_kernel, depth, len(grads), len(pairs), len(wholes)),
        in_specs=[ANY] * SIDES * len(grads) + [IN_VMEM] * (2 * len(pairs) + len(wholes)),
        out_specs=[IN_VMEM] * len(widths) + [ANY] * len(wholes),
        out_shape=[jax.ShapeDtypeStruct((rows, width), jnp.float32) for width in widths]
        + [
            jax.ShapeDtypeStruct((SIDES, whole.shape[0], whole.shape[1] // SIDES), whole.dtype)
            for whole in wholes
        ],
        scratch_shapes=scratch
        + [
            pltpu.SemaphoreType.DMA((copies,)),
            pltpu.SemaphoreType.DMA((copies,)),
            pltpu.SemaphoreType.DMA((SIDES * loaded + len(wholes),)),
        ],
        compiler_params=pltpu.CompilerParams(
            collective_id=2, has_side_effects=True, vmem_limit_bytes=62 * 2**20
        ),
        name="scatter_grads",
    )(
        *[half for grad in grads for half in grad],
        *[part for pair in pairs for part in pair],
        *wholes,
    )


def to_image(piece):
    col = lax.axis_index("col")
    rows = piece.shape[0] // 2
    kept = lax.dynamic_slice_in_dim(piece, col * rows, rows, 0)
    sent = lax.dynamic_slice_in_dim(piece, (1 - col) * rows, rows, 0)
    other = lax.ppermute(sent, "col", [(0, 1), (1, 0)])
    return jnp.where(
        col == 0, jnp.concatenate([kept, other], 1), jnp.concatenate([other, kept], 1)
    )


def from_image(whole):
    col = lax.axis_index("col")
    width = whole.shape[1] // 2
    kept = lax.dynamic_slice_in_dim(whole, col * width, width, 1)
    sent = lax.dynamic_slice_in_dim(whole, (1 - col) * width, width, 1)
    other = lax.ppermute(sent, "col", [(0, 1), (1, 0)])
    return jnp.where(
        col == 0, jnp.concatenate([kept, other], 0), jnp.concatenate([other, kept], 0)
    )


def product(left, right, left_at, right_at):
    return lax.dot_general(
        left, right, (((left_at,), (right_at,)), ((), ())), preferred_element_type=jnp.float32
    )


def norm_back(upstream, scaled, inverse, gain_row):
    scaled_grad = upstream * gain_row
    first_mean = jnp.mean(scaled_grad, -1, keepdims=True)
    second_mean = jnp.mean(scaled_grad * scaled, -1, keepdims=True)
    return inverse * (scaled_grad - first_mean - scaled * second_mean)


def core_order(left, rows, block_rows):
    turned = left.T.reshape(rows // 2, 2, block_rows, -1).transpose(1, 0, 2, 3)
    return turned.reshape(2, rows // 2 * block_rows, -1)


def group_order(block):
    rows = block.shape[0]
    return block.reshape(rows, 3, -1, GROUP).transpose(0, 2, 1, 3).reshape(rows, -1)


def part_order(block):
    rows = block.shape[0]
    return block.reshape(rows, -1, 3, GROUP).transpose(0, 2, 1, 3).reshape(rows, 3, -1)


def image_shards(
    tokens,
    first_gain,
    first_shift,
    mixer_weight,
    mixer_bias,
    merge_weight,
    merge_bias,
    second_gain,
    second_shift,
    expand_weight,
    expand_bias,
    reduce_weight,
    reduce_bias,
    cotangent,
):
    low = jnp.bfloat16
    cols = lax.axis_size("col")
    rows = lax.axis_size("row")
    piece = first_gain.shape[0]
    hidden_piece = expand_bias.shape[0]
    block_rows = mixer_weight.shape[0]
    vectors = jnp.concatenate(
        [
            jnp.stack(
                [
                    first_gain,
                    first_shift,
                    mixer_bias[0],
                    mixer_bias[1],
                    merge_bias,
                    second_gain,
                    second_shift,
                    reduce_bias,
                ]
            ).reshape(-1),
            expand_bias,
        ]
    ).astype(low)
    vector_rows = vectors.shape[0] // GROUP
    vector_block = jnp.pad(
        vectors.reshape(vector_rows, GROUP), ((0, block_rows - vector_rows), (0, 0))
    )
    mixer_width = 3 * mixer_weight.shape[2]
    first_block = jnp.concatenate([group_order(mixer_weight).astype(low), vector_block], 1)
    depth = rows // 4
    sides = (cols, tokens.shape[0] // cols, tokens.shape[1])
    image, mixed, merger, expander, reducer = gather_weights(
        [tokens.reshape(sides)],
        [
            first_block,
            merge_weight.astype(low).T,
            expand_weight.astype(low),
            reduce_weight.astype(low).T,
        ],
        depth,
    )
    image = jnp.concatenate([image[h] for h in range(cols)], 1)
    upstream_low = to_image(cotangent)
    mixed, merger, expander, reducer = [
        whole.reshape(cols, rows * block_rows, whole.shape[-1])
        for whole in (mixed, merger, expander, reducer)
    ]
    mixer = mixed[:, :, :mixer_width]
    spread = mixed[:, :, mixer_width:].reshape(cols, rows, block_rows, GROUP)[:, :, :vector_rows]
    spread = spread.reshape(cols, rows, -1).astype(jnp.float32).transpose(1, 0, 2)
    rows_of = spread[:, :, : 8 * piece].reshape(rows, cols, 8, piece).transpose(2, 0, 1, 3)
    rows_of = rows_of.reshape(8, -1)
    expand_shift = spread[:, :, 8 * piece :].reshape(cols, -1)
    first_gain_row, first_shift_row = rows_of[0], rows_of[1]
    query_bias, value_bias, merge_shift = rows_of[2], rows_of[3], rows_of[4]
    second_gain_row, second_shift_row, reduce_shift = rows_of[5], rows_of[6], rows_of[7]
    mixer_shift = jnp.stack(
        [
            query_bias.reshape(cols, -1, GROUP),
            jnp.zeros_like(query_bias).reshape(cols, -1, GROUP),
            value_bias.reshape(cols, -1, GROUP),
        ],
        2,
    ).reshape(cols, -1)

    inputs = image.astype(jnp.float32)
    first_scaled, first_inverse, first_normed = normalize(inputs, first_gain_row, first_shift_row)
    first_low = first_normed.astype(low)
    projected = jnp.stack(
        [(product(first_low, mixer[h], 1, 0) + mixer_shift[h]).astype(low) for h in range(cols)]
    )
    attended = attention_forward(projected)
    merged = sum(product(attended[h], merger[h], 1, 1) for h in range(cols))
    hidden = inputs + merged + merge_shift
    second_scaled, second_inverse, second_normed = normalize(
        hidden, second_gain_row, second_shift_row
    )
    second_low = second_normed.astype(low)
    expanded = [product(second_low, expander[h], 1, 0) + expand_shift[h] for h in range(cols)]
    activated = [quick_gelu(part).astype(low) for part in expanded]
    reduced = sum(product(activated[h], reducer[h], 1, 1) for h in range(cols))
    layer_output = from_image((hidden + reduced + reduce_shift).astype(low))

    upstream = upstream_low.astype(jnp.float32)
    expanded_grad = [
        (product(upstream_low, reducer[h], 1, 0) * gelu_slope(expanded[h])).astype(low)
        for h in range(cols)
    ]
    expand_shift_grad = [jnp.sum(part.astype(jnp.float32), 0) for part in expanded_grad]
    second_grad = sum(product(expanded_grad[h], expander[h], 1, 1) for h in range(cols))
    hidden_grad = upstream + norm_back(
        second_grad, second_scaled, second_inverse, second_gain_row
    )
    hidden_low = hidden_grad.astype(low)
    merger_grad = [product(hidden_low, attended[h], 0, 0).astype(low) for h in range(cols)]
    attended_grad = jnp.stack(
        [product(hidden_low, merger[h], 1, 0).astype(low) for h in range(cols)]
    )
    projected_grad = attention_back(projected, attended_grad)
    mixer_grad = [product(first_low, projected_grad[h], 0, 0).astype(low) for h in range(cols)]
    bias_sums = jnp.sum(projected_grad.astype(jnp.float32), 1)
    bias_sums = bias_sums.reshape(cols, -1, 3, GROUP).transpose(2, 0, 1, 3).reshape(3, -1)
    first_grad = sum(product(projected_grad[h], mixer[h], 1, 1) for h in range(cols))
    input_grad = hidden_grad + norm_back(first_grad, first_scaled, first_inverse, first_gain_row)
    vector_grads = jnp.stack(
        [
            jnp.sum(first_grad * first_scaled, 0),
            jnp.sum(first_grad, 0),
            bias_sums[0],
            bias_sums[2],
            jnp.sum(hidden_grad, 0),
            jnp.sum(second_grad * second_scaled, 0),
            jnp.sum(second_grad, 0),
            jnp.sum(upstream, 0),
        ]
    )
    vector_grads = vector_grads.reshape(8, rows, cols, piece).transpose(2, 1, 0, 3)
    hidden_grads = jnp.concatenate(expand_shift_grad).reshape(rows, cols, hidden_piece)
    vector_grads = jnp.concatenate(
        [vector_grads.reshape(cols, rows, -1), hidden_grads.transpose(1, 0, 2)], 2
    )
    vector_grads = vector_grads.reshape(cols, rows, vector_rows, GROUP).astype(low)
    vector_grads = jnp.pad(
        vector_grads, ((0, 0), (0, 0), (0, block_rows - vector_rows), (0, 0))
    ).reshape(cols, rows * block_rows, GROUP)
    mixed_grad = [jnp.concatenate([mixer_grad[h], vector_grads[h]], 1) for h in range(cols)]
    grads = [
        [part.reshape(depth, 2, 2, block_rows, -1) for part in halves]
        for halves in (merger_grad, mixed_grad)
    ]
    pairs = [
        (core_order(left, rows, block_rows), jnp.stack(right))
        for left, right in ((upstream_low, activated), (second_low, expanded_grad))
    ]
    merge_total, mixed_total, reduce_total, expand_total, tokens_gradient = scatter_grads(
        grads, pairs, [input_grad.astype(low)], depth
    )
    tokens_gradient = tokens_gradient.reshape(tokens.shape).astype(jnp.float32)
    mixer_total = part_order(mixed_total[:, :mixer_width])
    vector_total = mixed_total[:vector_rows, mixer_width:].reshape(-1)
    small = vector_total[: 8 * piece].reshape(8, piece)
    return (
        layer_output,
        tokens_gradient,
        small[0],
        small[1],
        mixer_total,
        small[2:4],
        merge_total.T,
        small[4],
        small[5],
        small[6],
        expand_total,
        vector_total[8 * piece :],
        reduce_total.T,
        small[7],
    )


def solution(mesh):
    def body(*arguments):
        images = arguments[0].shape[0] // SEQ
        whole = images == 2 and lax.axis_size("col") == 2
        return (image_shards if whole else split_shards)(*arguments)

    return jax.shard_map(
        body,
        mesh=mesh,
        in_specs=(
            P("row", "col"),
            P(("row", "col")),
            P(("row", "col")),
            P("row", None, "col"),
            P(None, ("row", "col")),
            P("col", "row"),
            P(("row", "col")),
            P(("row", "col")),
            P(("row", "col")),
            P("row", "col"),
            P(("row", "col")),
            P("col", "row"),
            P(("row", "col")),
            P("row", "col"),
        ),
        out_specs=(
            P("row", "col"),
            P("row", "col"),
            P(("row", "col")),
            P(("row", "col")),
            P("row", None, "col"),
            P(None, ("row", "col")),
            P("col", "row"),
            P(("row", "col")),
            P(("row", "col")),
            P(("row", "col")),
            P("row", "col"),
            P(("row", "col")),
            P("col", "row"),
            P(("row", "col")),
        ),
        check_vma=False,
    )
```
